32 devices in a mesh: grp: 8 (over z, x), win: 4 (over y, core).
Axes of the slice: x: 2, y: 2, z: 4, core: 2. Of those that a mesh axis runs over, the one named last changes fastest.
Arguments:
- tokens: bfloat16 [32768, 128], P(('grp', 'win')), may hold values from -6 to 6
- positions: bfloat16 [2, 32768, 128], P(None, ('grp', 'win')), may hold values from -6 to 6
- cotangent: bfloat16 [32768, 128], P(('grp', 'win')), may hold values from -6 to 6
- route_send: int32 [2, 32768], P(None, ('grp', 'win')), may hold values from 0 to 2047, as said below
- recv_slot: int32 [2, 32, 2048], P(None, ('grp', 'win')), may hold values from 0 to 1728, as said below
- slot_bucket: int32 [2, 55296], P(None, ('grp', 'win')), may hold values from -1 to 3, as said below
- master: float32 [263936], P(('grp', 'win'))
- first_moment: float32 [263936], P(('grp', 'win'))
- second_moment: float32 [263936], P(('grp', 'win'))
Outputs:
- mixed: bfloat16 [32768, 128], P(('grp', 'win'))
- tokens_grad: float32 [32768, 128], P(('grp', 'win'))
- grad_norm: float32 [1], replicated
- clipped: float32 [263936], P(('grp', 'win'))
- new_master: float32 [263936], P(('grp', 'win'))
- new_first: float32 [263936], P(('grp', 'win'))
- new_second: float32 [263936], P(('grp', 'win'))
- new_copy: bfloat16 [263936], P(('grp', 'win'))
The draws below stay inside these ranges and needn't reach their ends.
Inputs may be any that keep to these rules, and one draw needn't show every extreme that they name: `route_send`: the values of one device's pillars in one layer are distinct; a device sends at most 64 pillars to any one device, and in every draw some device sends exactly 64 to some device. `recv_slot`: for one layer and device the values below 1728 are distinct and name slots whose bucket id is not -1; every pillar that is sent gets a slot, and a device has at most 1408 occupied slots. `slot_bucket`: slots of one bucket lie in one aligned run of 144 slots; a run holds one bucket of 144, two of 60 or four of 30 slots, and unused slots; ids tell buckets of a run apart.
All inputs are finite; a program needn't handle non-finite values.
Results may differ from the reference program's by a relative error of at most 0.02.
The reference program's roundings to bfloat16 on the way count: a program that leaves them out, or rounds other values in their place, can miss the bound.
Values may be sent and summed in bfloat16 or wider, within the bound.
No kernel may reach another device: no remote copies, remote signals or barrier semaphores. Data moves between devices by JAX's collectives and lax.ppermute only.
A program may use at most 128 MiB of HBM per device.

```python
import math
import jax
import jax.numpy as jnp
from jax import lax

PILLAR_WIDTH = 128
FF = 256
HEAD_COUNT = 8
WINDOW_SLOTS = 144
LAYERS = 2
TOK_DEV = 1024
HDIM = 16
ROUTE_CAPACITY = 64
NSUB = 12
DEVICE_SLOTS = 1728
TOKENS = 32768
NPARAM = 263936
DEVICES = 32


def pair_counts(base_offset):
    quarter = ROUTE_CAPACITY // 4
    pattern = jnp.array([3, 1, 1, 2], jnp.int32) * quarter
    spread = jax.random.permutation(jax.random.fold_in(base_offset, 1), jnp.tile(pattern, DEVICES // 4))
    extra_rows = jnp.where(jnp.arange(DEVICES) < DEVICES // 4, quarter, 0).astype(jnp.int32)
    extra_rows = jax.random.permutation(jax.random.fold_in(base_offset, 2), extra_rows)
    source = jnp.arange(DEVICES)[:, None]
    target_slot = jnp.arange(DEVICES)[None, :]
    return spread[(target_slot - source) % DEVICES] + extra_rows[None, :]


def sender_route_table(base_offset, bucket_counts):
    flattened_index = jnp.arange(DEVICES * ROUTE_CAPACITY)

    def one_device(device_key, row_counts):
        usable = flattened_index % ROUTE_CAPACITY < row_counts[flattened_index // ROUTE_CAPACITY]
        shuffle = jax.random.permutation(device_key, DEVICES * ROUTE_CAPACITY)
        sorted_order = jnp.argsort(jnp.where(usable, shuffle, DEVICES * ROUTE_CAPACITY + flattened_index), stable=True)
        return sorted_order[:TOK_DEV].astype(jnp.int32)
    device_keys = jax.random.split(jax.random.fold_in(base_offset, 3), DEVICES)
    return jax.vmap(one_device)(device_keys, bucket_counts).reshape(TOKENS)


def device_buckets(device_key, live_count):
    bucket_slot_index = jnp.arange(DEVICE_SLOTS)
    block_index = bucket_slot_index // WINDOW_SLOTS
    within_block = bucket_slot_index % WINDOW_SLOTS
    block_kind = jax.random.permutation(jax.random.fold_in(device_key, 1), jnp.arange(NSUB) % 3)[block_index]
    bucket_size = jnp.where(block_kind == 0, WINDOW_SLOTS, jnp.where(block_kind == 1, 5 * WINDOW_SLOTS // 12, 5 * WINDOW_SLOTS // 24))
    per_block = jnp.where(block_kind == 0, 1, jnp.where(block_kind == 1, 2, 4))
    local_id = within_block // bucket_size
    within_bucket = within_block % bucket_size
    usable = local_id < per_block
    bucket_tag = jax.random.permutation(jax.random.fold_in(device_key, 2), NSUB * 4)[block_index * 4 + jnp.minimum(local_id, 3)]
    sort_key = jnp.where(usable, within_bucket * (NSUB * 4) + bucket_tag, WINDOW_SLOTS * NSUB * 4 + bucket_slot_index)
    sorted_order = jnp.argsort(sort_key, stable=True)
    slot_position = jnp.zeros((DEVICE_SLOTS,), jnp.int32).at[sorted_order].set(jnp.arange(DEVICE_SLOTS, dtype=jnp.int32))
    is_live = slot_position < live_count
    return (jnp.where(is_live, local_id, -1).astype(jnp.int32), sorted_order.astype(jnp.int32))


def receiver_slots(device_key, column_index, sorted_order):
    flattened_index = jnp.arange(DEVICES * ROUTE_CAPACITY)
    usable = flattened_index % ROUTE_CAPACITY < column_index[flattened_index // ROUTE_CAPACITY]
    shuffle = jax.random.permutation(device_key, DEVICES * ROUTE_CAPACITY)
    incoming = jnp.argsort(jnp.where(usable, shuffle, DEVICES * ROUTE_CAPACITY + flattened_index), stable=True)
    padded_rows = jnp.concatenate([sorted_order, jnp.full((DEVICES * ROUTE_CAPACITY,), DEVICE_SLOTS, jnp.int32)])
    target_slot = jnp.where(flattened_index < jnp.sum(column_index), padded_rows[flattened_index], DEVICE_SLOTS)
    return jnp.zeros((DEVICES * ROUTE_CAPACITY,), jnp.int32).at[incoming].set(target_slot.astype(jnp.int32))


def routing_layout(key, layer_index):
    base_offset = jax.random.fold_in(key, 4100 + layer_index)
    bucket_counts = pair_counts(base_offset)
    received = jnp.sum(bucket_counts, axis=0)
    bucket_keys = jax.random.split(jax.random.fold_in(base_offset, 4), DEVICES)
    bucket_list, orderings = jax.vmap(device_buckets)(bucket_keys, received)
    slot_keys = jax.random.split(jax.random.fold_in(base_offset, 5), DEVICES)
    landing_slots = jax.vmap(receiver_slots)(slot_keys, bucket_counts.T, orderings)
    return (sender_route_table(base_offset, bucket_counts), landing_slots, bucket_list.reshape(DEVICES * DEVICE_SLOTS))


def draw_route_send(key, part):
    return jnp.stack([routing_layout(key, layer_index)[0] for layer_index in range(LAYERS)])


def draw_recv_slot(key, part):
    return jnp.stack([routing_layout(key, layer_index)[1] for layer_index in range(LAYERS)])


def draw_slot_bucket(key, part):
    return jnp.stack([routing_layout(key, layer_index)[2] for layer_index in range(LAYERS)])


def parameter_kinds():
    layer_size = 4 * PILLAR_WIDTH * PILLAR_WIDTH + 2 * PILLAR_WIDTH * FF + FF + 5 * PILLAR_WIDTH
    offset = jnp.arange(NPARAM) % layer_size
    end_in = 3 * PILLAR_WIDTH * PILLAR_WIDTH
    end_out = 4 * PILLAR_WIDTH * PILLAR_WIDTH
    end_expand = end_out + PILLAR_WIDTH * FF
    end_contract = end_expand + FF * PILLAR_WIDTH
    end_bias = end_contract + FF
    matrix_scale = jnp.where(offset < end_in, PILLAR_WIDTH ** (-0.5), jnp.where(offset < end_out, 2.0 * PILLAR_WIDTH ** (-0.5), jnp.where(offset < end_expand, PILLAR_WIDTH ** (-0.5), jnp.where(offset < end_contract, FF ** (-0.5), jnp.where(offset < end_bias, 0.5, 0.3)))))
    small_offset = offset - end_bias - PILLAR_WIDTH
    is_gain = (small_offset >= 0) & (small_offset < PILLAR_WIDTH) | (small_offset >= 2 * PILLAR_WIDTH) & (small_offset < 3 * PILLAR_WIDTH)
    query_key = (offset < end_in) & (offset % (3 * PILLAR_WIDTH) < 2 * PILLAR_WIDTH)
    grad_factor = jnp.where(query_key, 0.35, jnp.where(offset < end_contract, 1.0, 1.5))
    return (matrix_scale, is_gain, grad_factor)


def draw_master(key, part):
    matrix_scale, is_gain, grad_factor = parameter_kinds()
    noise = jax.random.normal(key, (NPARAM,), jnp.float32)
    jitter = jax.random.uniform(jax.random.fold_in(key, 1), (NPARAM,), jnp.float32, -1.0, 1.0)
    return jnp.where(is_gain, 1.0 + 0.25 * jitter, matrix_scale * noise).astype(jnp.float32)


def draw_first_moment(key, part):
    matrix_scale, is_gain, grad_factor = parameter_kinds()
    noise = jax.random.normal(key, (NPARAM,), jnp.float32)
    return (0.25 * grad_factor * noise).astype(jnp.float32)


def draw_second_moment(key, part):
    matrix_scale, is_gain, grad_factor = parameter_kinds()
    factor = jnp.exp(jax.random.uniform(key, (NPARAM,), jnp.float32, 0.0, math.log(4.0)))
    return ((0.25 * grad_factor) ** 2 * factor).astype(jnp.float32)


def steps_of(own_key, shape, shards, least, high):
    loudness = 1.0
    for position, shards_of in shards:
        heights = jax.random.uniform(jax.random.fold_in(jax.random.fold_in(own_key, 6), position), (shards_of,), jnp.float32, least / len(shards), high / len(shards))
        loudness = loudness * jnp.repeat(jnp.exp(heights), shape[position] // shards_of).reshape((-1,) + (1,) * (len(shape) - 1 - position))
    return loudness


def centred(rng, shape, width, bound, shards=(), kind=jnp.bfloat16):
    values = width * jax.random.normal(rng, shape, jnp.float32)
    if shards:
        values = values * steps_of(rng, shape, shards, -0.22, 0.18)
    return jnp.clip(values, -bound, bound).astype(kind)


def setup_inputs(seed: int = 0) -> dict:
    key_list = jax.random.split(jax.random.key(seed), 10)
    return {
        "tokens": centred(key_list[0], (TOKENS, PILLAR_WIDTH), 1.0, 6.0, ((0, 32),)),
        "positions": centred(key_list[1], (LAYERS, TOKENS, PILLAR_WIDTH), 1.0, 6.0, ((1, 32),)),
        "cotangent": centred(key_list[2], (TOKENS, PILLAR_WIDTH), 1.0, 6.0, ((0, 32),)),
        "route_send": draw_route_send(jax.random.fold_in(key_list[9], 71), 0),
        "recv_slot": draw_recv_slot(jax.random.fold_in(key_list[9], 71), 0),
        "slot_bucket": draw_slot_bucket(jax.random.fold_in(key_list[9], 71), 0),
        "master": draw_master(jax.random.fold_in(key_list[9], 71), 0),
        "first_moment": draw_first_moment(jax.random.fold_in(key_list[9], 71), 0),
        "second_moment": draw_second_moment(jax.random.fold_in(key_list[9], 71), 0),
    }


@jax.custom_vjp
def low(v):
    return lax.optimization_barrier(v.astype(jnp.bfloat16)).astype(jnp.float32)

@jax.custom_vjp
def low_back(v):
    return v

def low_keep(v):
    return (low(v), None)

def low_pass(kept, grad):
    return (grad,)

def back_keep(v):
    return (v, None)

def back_low(kept, grad):
    return (low(grad),)
low.defvjp(low_keep, low_pass)
low_back.defvjp(back_keep, back_low)
beta_one = 0.5
beta_two = 0.5
adam_step = 4
rate = 0.1
decay = 0.01
adam_eps = 1e-08

def matmul(left, right):
    return jnp.dot(left, right, precision=lax.Precision.HIGHEST)

def norm_rows(value_rows, gain, shift):
    centre = value_rows - lax.optimization_barrier(jnp.mean(value_rows, axis=-1, keepdims=True))
    spread = lax.optimization_barrier(jnp.mean(centre * centre, axis=-1, keepdims=True))
    return centre * lax.rsqrt(spread + 1e-05) * gain + shift

def unpack(flat_params, layer_index):
    layer_size = 4 * PILLAR_WIDTH * PILLAR_WIDTH + 2 * PILLAR_WIDTH * FF + FF + 5 * PILLAR_WIDTH
    start = layer_index * layer_size
    shapes = [('project_in', (PILLAR_WIDTH, 3 * PILLAR_WIDTH)), ('project_out', (PILLAR_WIDTH, PILLAR_WIDTH)), ('expand', (PILLAR_WIDTH, FF)), ('contract', (FF, PILLAR_WIDTH)), ('expand_bias', (FF,)), ('contract_bias', (PILLAR_WIDTH,)), ('gain_first', (PILLAR_WIDTH,)), ('shift_first', (PILLAR_WIDTH,)), ('gain_second', (PILLAR_WIDTH,)), ('shift_second', (PILLAR_WIDTH,))]
    params = {}
    for name, target_shape in shapes:
        count = math.prod(target_shape)
        params[name] = flat_params[start:start + count].reshape(target_shape)
        start = start + count
    return params

def slot_of_pillar(route_row, receive):
    home = jnp.arange(TOKENS, dtype=jnp.int32) // TOK_DEV
    target_slot = (route_row // ROUTE_CAPACITY).astype(jnp.int32)
    place = (route_row % ROUTE_CAPACITY).astype(jnp.int32)
    landing_slots = receive[target_slot, home * ROUTE_CAPACITY + place]
    return jnp.where(landing_slots < DEVICE_SLOTS, target_slot * DEVICE_SLOTS + landing_slots, DEVICES * DEVICE_SLOTS).astype(jnp.int32)

def attention(queries, keys_rows, values, bucket_index):
    groups_count = queries.shape[0] // (4 * WINDOW_SLOTS)
    scaling = float(HDIM) ** (-0.5)

    def split_heads(value_rows):
        return value_rows.reshape(groups_count, 4, WINDOW_SLOTS, HEAD_COUNT, HDIM)

    def one_group(stacked):
        query_block, key_block, value_block, bucket_block = stacked
        raw = jnp.einsum('bqhd,bkhd->bhqk', query_block, key_block, precision=lax.Precision.HIGHEST) * scaling
        same = (bucket_block[:, :, None] == bucket_block[:, None, :]) & (bucket_block[:, None, :] >= 0)
        scores = low_back(jnp.where(same[:, None], raw, -1e+30))
        probs = low(jax.nn.softmax(scores, axis=-1))
        return jnp.einsum('bhqk,bkhd->bqhd', probs, value_block, precision=lax.Precision.HIGHEST)
    stacked = (split_heads(queries), split_heads(keys_rows), split_heads(values), bucket_index.reshape(groups_count, 4, WINDOW_SLOTS))
    final_result = lax.map(jax.checkpoint(one_group), stacked)
    return final_result.reshape(-1, PILLAR_WIDTH)

def forward(inputs, weights, positions, route_send, recv_slot, slot_bucket):
    copies = low(weights)
    state = inputs
    for layer_index in range(LAYERS):
        params = unpack(copies, layer_index)
        landing_slots = slot_of_pillar(route_send[layer_index], recv_slot[layer_index])
        bucket_index = slot_bucket[layer_index]
        live_mask = (bucket_index >= 0).astype(jnp.float32)[:, None]
        blank_rows = jnp.zeros((DEVICES * DEVICE_SLOTS + 1, PILLAR_WIDTH), jnp.float32)
        slot_rows = low_back(blank_rows.at[landing_slots].set(state)[:-1])
        slot_pos = blank_rows.at[landing_slots].set(positions[layer_index].astype(jnp.float32))[:-1]
        joined = low(slot_rows + slot_pos)
        query_key = low_back(low(matmul(joined, params['project_in'][:, :2 * PILLAR_WIDTH])))
        values = low_back(low(matmul(slot_rows, params['project_in'][:, 2 * PILLAR_WIDTH:])))
        attended_output = attention(query_key[:, :PILLAR_WIDTH], query_key[:, PILLAR_WIDTH:], values, bucket_index)
        attended_output = low_back(low(attended_output * live_mask))
        branch = low_back(low(matmul(attended_output, params['project_out'])))
        back_home = jnp.concatenate([branch, jnp.zeros((1, PILLAR_WIDTH), jnp.float32)])[landing_slots]
        first = norm_rows(state + back_home, params['gain_first'], params['shift_first'])
        inner = low_back(matmul(low(first), params['expand']) + params['expand_bias'])
        active = low(jax.nn.gelu(inner, approximate=False))
        outer = low_back(matmul(active, params['contract']) + params['contract_bias'])
        state = low(norm_rows(first + outer, params['gain_second'], params['shift_second']))
    return state

def reference(tokens, positions, cotangent, route_send, recv_slot, slot_bucket, master, first_moment, second_moment):

    def run(inputs, weights):
        return forward(inputs, weights, positions, route_send, recv_slot, slot_bucket)
    output, pullback = jax.vjp(run, tokens.astype(jnp.float32), master)
    input_grad, weight_grad = pullback(cotangent.astype(jnp.float32))
    total = jnp.sqrt(jnp.sum(weight_grad * weight_grad))
    clip_limit = 0.25 * math.sqrt(NPARAM)
    factor = jnp.minimum(1.0, clip_limit / (total + 1e-06))
    clipped = weight_grad * factor
    new_first = beta_one * first_moment + (1.0 - beta_one) * clipped
    new_second = beta_two * second_moment + (1.0 - beta_two) * clipped * clipped
    first_hat = new_first / (1.0 - beta_one ** adam_step)
    second_hat = new_second / (1.0 - beta_two ** adam_step)
    new_master = master - rate * (first_hat / (jnp.sqrt(second_hat) + adam_eps) + decay * master)
    return (output.astype(jnp.bfloat16), input_grad, total.reshape(1), clipped, new_master, new_first, new_second, new_master.astype(jnp.bfloat16))
```

```python
import functools
import math

import jax
import jax.numpy as jnp
from jax import lax
from jax.experimental import pallas as pl
from jax.experimental.pallas import tpu as pltpu
from jax.sharding import PartitionSpec as P

PILLAR_WIDTH = 128
FF = 256
HEAD_COUNT = 8
HDIM = 16
WINDOW_SLOTS = 144
LAYERS = 2
DEVICE_SLOTS = 1728
NSUB = 12
NPARAM = 263936
LAYER_ROWS = 1031
EXPANDED = HEAD_COUNT * WINDOW_SLOTS
MASKED = -1e30
LOWEST = -3e38

beta_one = 0.5
beta_two = 0.5
adam_step = 4
rate = 0.1
decay = 0.01
adam_eps = 1e-08

BF16 = jnp.bfloat16
F32 = jnp.float32
AXES = ("grp", "win")
PARAMS = pltpu.CompilerParams(vmem_limit_bytes=48 << 20)

NN = (((1,), (0,)), ((), ()))
NT = (((1,), (1,)), ((), ()))
TN = (((0,), (0,)), ((), ()))


def mm(left, right, dims=NN):
    return lax.dot_general(left, right, dims, preferred_element_type=F32)


def iota(shape, dim):
    return lax.broadcasted_iota(jnp.int32, shape, dim)


def shape_of(shape, dtype):
    return jax.ShapeDtypeStruct(shape, dtype)


def one_hot_rows(row_ids, first, count):
    return jnp.where(iota((count, row_ids.shape[1]), 0) + first == row_ids, 1.0, 0.0).astype(BF16)


def one_hot_columns(column_ids, width):
    lane = iota(column_ids.shape, 1)
    pieces = [
        jnp.where(column_ids == lane + 128 * k, 1.0, 0.0).astype(BF16)
        for k in range(-(-width // 128))
    ]
    return jnp.concatenate(pieces, axis=1)[:, :width]


def expand_heads(block, heads):
    main = block[:128]
    tail = block[128:]
    return jnp.concatenate([main] * HEAD_COUNT + [tail] * HEAD_COUNT, axis=0) * heads


def scatter_rows(route_row, low_rows, send, chunk=256):
    for c in range(send.shape[0] // chunk):
        hot = one_hot_rows(route_row, c * chunk, chunk)
        send[c * chunk : (c + 1) * chunk, :] = mm(hot, low_rows).astype(BF16)


def land_rows(recv_col, slot_values, send, chunk=128):
    for c in range(send.shape[0] // chunk):
        part = slice(c * chunk, (c + 1) * chunk)
        hot = one_hot_columns(recv_col[part, :], DEVICE_SLOTS)
        send[part, :] = mm(hot, slot_values).astype(BF16)


def start_kernel(route_ref, tokens_ref, pos_ref, out_ref, out_next_ref):
    both = jnp.concatenate([tokens_ref[...], pos_ref[0]], axis=1)
    scatter_rows(route_ref[0:1, :], both, out_ref)
    scatter_rows(route_ref[1:2, :], pos_ref[1], out_next_ref)


def owner_forward_kernel(
    recv_ref,
    recv_col_ref,
    bucket_ref,
    heads_ref,
    win_ref,
    wout_ref,
    rows_ref,
    pos_ref,
    send_ref,
    kept_ref,
    qkv_ref,
    expo_ref,
    out_ref,
    total_ref,
    branch_ref,
):
    def one_run(run, carry):
        base = pl.multiple_of(run * WINDOW_SLOTS, 16)
        here = pl.ds(base, WINDOW_SLOTS)
        hot = one_hot_rows(recv_ref[...], base, WINDOW_SLOTS)
        if pos_ref is None:
            landed = mm(hot, rows_ref[...])
        else:
            landed = mm(hot, jnp.concatenate([rows_ref[...], pos_ref[...]], axis=1))
        slot_rows = landed[:, :128].astype(BF16)
        joined = (landed[:, :128] + landed[:, 128:]).astype(BF16)
        query_key = mm(joined, win_ref[:, :256]).astype(BF16)
        values = mm(slot_rows, win_ref[:, 256:]).astype(BF16)
        kept_ref[here, :] = jnp.concatenate([joined, slot_rows], axis=1)
        qkv_ref[here, :] = jnp.concatenate([query_key, values], axis=1)
        heads = heads_ref[...]
        bucket = bucket_ref[here, :]
        lane = iota((WINDOW_SLOTS, 128), 1)
        own = jnp.where(bucket == lane, 1.0, 0.0).astype(BF16)
        other = jnp.where((lane < 4) & (bucket != lane), MASKED, 0.0).astype(BF16)
        queries = (query_key[:, :128].astype(F32) * 0.25).astype(BF16)
        query_wide = jnp.concatenate([queries, own], axis=1)
        others = jnp.concatenate([other[:128]] * 8 + [other[128:]] * 8, axis=0)
        key_wide = jnp.concatenate([expand_heads(query_key[:, 128:], heads), others], axis=1)
        scores = mm(query_wide, key_wide, NT)
        tail = scores[:, 1024:]
        segment = lane >> 4
        tail_top = jnp.zeros((WINDOW_SLOTS, 128), F32)
        pieces = []
        for h in range(HEAD_COUNT):
            main = scores[:, 128 * h : 128 * h + 128]
            mine = segment == h
            top = jnp.max(
                jnp.maximum(main, jnp.where(mine, tail, LOWEST)), axis=1, keepdims=True
            )
            tail_top = jnp.where(mine, top, tail_top)
            pieces.append(jnp.exp(main - top).astype(BF16))
        pieces.append(jnp.exp(tail - tail_top).astype(BF16))
        expo = jnp.concatenate(pieces, axis=1)
        expo_ref[here, :] = expo
        value_wide = jnp.concatenate([expand_heads(values, heads), heads], axis=1)
        summed = mm(expo, value_wide)
        total = summed[:, 128:]
        attended = summed[:, :128] / total
        out_ref[here, :] = attended
        total_ref[here, :] = total
        attended = jnp.where(bucket >= 0, attended, 0.0).astype(BF16)
        branch_ref[here, :] = mm(attended, wout_ref[...]).astype(BF16)
        return carry

    lax.fori_loop(0, NSUB, one_run, 0)
    land_rows(recv_col_ref, branch_ref[...], send_ref)


def owner_backward_kernel(
    recv_ref,
    recv_col_ref,
    bucket_ref,
    heads_ref,
    unfold_ref,
    win_ref,
    wout_ref,
    grads_ref,
    kept_ref,
    qkv_ref,
    expo_ref,
    out_ref,
    total_ref,
    send_ref,
    dwin_ref,
    dwout_ref,
    attended_ref,
    dbranch_ref,
    dqkv_ref,
):
    def one_run(run, carry):
        base = pl.multiple_of(run * WINDOW_SLOTS, 16)
        here = pl.ds(base, WINDOW_SLOTS)
        heads = heads_ref[...]
        block = heads[1024:]
        hot = one_hot_rows(recv_ref[...], base, WINDOW_SLOTS)
        dbranch = mm(hot, grads_ref[...]).astype(BF16)
        live = bucket_ref[here, :] >= 0
        out = out_ref[here, :]
        attended_ref[here, :] = jnp.where(live, out, 0.0).astype(BF16)
        dbranch_ref[here, :] = dbranch
        dattended = mm(dbranch, wout_ref[...], NT).astype(BF16).astype(F32)
        dout = (jnp.where(live, dattended, 0.0) / total_ref[here, :]).astype(BF16)
        weighed = dout.astype(F32) * out
        weighed_high = weighed.astype(BF16)
        weighed_low = (weighed - weighed_high.astype(F32)).astype(BF16)
        centre = mm(weighed_high, block) + mm(weighed_low, block)
        centre_high = centre.astype(BF16).astype(F32)
        place = iota((WINDOW_SLOTS, 128), 1) & 15
        aside = jnp.where(
            place == 0, -centre_high, jnp.where(place == 1, centre_high - centre, 0.0)
        ).astype(BF16)
        dout_wide = jnp.concatenate([dout, aside], axis=1)
        queries = qkv_ref[here, 0:128]
        keys_wide = expand_heads(qkv_ref[here, 128:256], heads)
        value_wide = jnp.concatenate([expand_heads(qkv_ref[here, 256:384], heads), heads], axis=1)
        expo = expo_ref[here, :]
        dscore = (mm(dout_wide, value_wide, NT) * expo.astype(F32)).astype(BF16)
        dqueries = (mm(dscore, keys_wide) * 0.25).astype(BF16)

        def gathered(left, right, scale):
            wide = mm(left, right, TN)
            main = jnp.concatenate(
                [wide[16 * h : 16 * h + 16, 128 * h : 128 * h + 128] for h in range(HEAD_COUNT)],
                axis=0,
            )
            tail = wide[:, 1024:] * block.astype(F32)
            folded = (jnp.concatenate([main, tail], axis=1) * scale).astype(BF16)
            return mm(unfold_ref[...], folded, NT).astype(BF16)

        dkeys = gathered(queries, dscore, 0.25)
        dvalues = gathered(dout, expo, 1.0)
        dqkv_ref[here, :] = jnp.concatenate([dqueries, dkeys, dvalues], axis=1)
        return carry

    lax.fori_loop(0, NSUB, one_run, 0)
    dwout_ref[...] = mm(attended_ref[...], dbranch_ref[...], TN)
    dqkv = dqkv_ref[...]
    kept = kept_ref[...]
    dwin_ref[:, :256] = mm(kept[:, :128], dqkv[:, :256], TN)
    dwin_ref[:, 256:] = mm(kept[:, 128:], dqkv[:, 256:], TN)
    drows = mm(dqkv, win_ref[...], NT).astype(BF16)
    land_rows(recv_col_ref, drows, send_ref)


def centred_rows(rows):
    centre = rows - jnp.mean(rows, axis=-1, keepdims=True)
    spread = jnp.mean(centre * centre, axis=-1, keepdims=True)
    inverse = lax.rsqrt(spread + 1e-05)
    return centre * inverse, inverse


def norm_back(grad, gain, unit, inverse):
    dunit = grad * gain
    return (
        dunit
        - jnp.mean(dunit, axis=-1, keepdims=True)
        - unit * jnp.mean(dunit * unit, axis=-1, keepdims=True)
    ) * inverse


def feed_forward(resid, expand, contract, vecs):
    unit, inverse = centred_rows(resid)
    first = unit * vecs[3:4, :] + vecs[4:5, :]
    first_low = first.astype(BF16)
    bias = jnp.concatenate([vecs[0:1, :], vecs[1:2, :]], axis=1)
    inner = mm(first_low, expand) + bias
    below = 0.5 + 0.5 * lax.erf(inner * math.sqrt(0.5))
    active = (inner * below).astype(BF16)
    second = first + (mm(active, contract) + vecs[2:3, :])
    return unit, inverse, first_low, inner, below, active, second


ROWS = 128


def home_forward_kernel(
    route_col_ref,
    route_ref,
    branch_ref,
    state_ref,
    expand_ref,
    contract_ref,
    vecs_ref,
    result_ref,
    send_ref,
    resid_ref,
):
    def some_rows(c, carry):
        here = pl.ds(pl.multiple_of(c * ROWS, ROWS), ROWS)
        vecs = vecs_ref[...]
        hot = one_hot_columns(route_col_ref[here, :], branch_ref.shape[0])
        resid = state_ref[here, :].astype(F32) + mm(hot, branch_ref[...])
        resid_ref[here, :] = resid
        second = feed_forward(resid, expand_ref[...], contract_ref[...], vecs)[-1]
        unit, _ = centred_rows(second)
        result_ref[here, :] = (unit * vecs[5:6, :] + vecs[6:7, :]).astype(BF16)
        return carry

    lax.fori_loop(0, result_ref.shape[0] // ROWS, some_rows, 0)
    scatter_rows(route_ref[...], result_ref[...], send_ref)


def home_backward_kernel(
    top,
    route_col_ref,
    route_ref,
    arrived_ref,
    base_ref,
    cotangent_ref,
    expand_ref,
    contract_ref,
    vecs_ref,
    *rest,
):
    if top:
        result_ref, *rest = rest
    (
        dresid_ref,
        send_ref,
        dexpand_ref,
        dcontract_ref,
        dvecs_ref,
        active_ref,
        douter_ref,
        first_ref,
        dinner_ref,
        low_ref,
    ) = rest
    dvecs_ref[...] = jnp.zeros_like(dvecs_ref)

    def some_rows(c, carry):
        here = pl.ds(pl.multiple_of(c * ROWS, ROWS), ROWS)
        vecs = vecs_ref[...]
        expand = expand_ref[...]
        contract = contract_ref[...]
        hot = one_hot_columns(route_col_ref[here, :], arrived_ref.shape[0])
        taken = mm(hot, arrived_ref[...])
        if top:
            resid = base_ref[here, :].astype(F32) + taken
            grad = cotangent_ref[here, :].astype(F32)
        else:
            resid = base_ref[here, :]
            grad = cotangent_ref[here, :] + taken
        unit_first, inverse_first, first_low, inner, below, active, second = feed_forward(
            resid, expand, contract, vecs
        )
        unit, inverse = centred_rows(second)
        if top:
            result_ref[here, :] = (unit * vecs[5:6, :] + vecs[6:7, :]).astype(BF16)
        dsecond = norm_back(grad, vecs[5:6, :], unit, inverse)
        douter = dsecond.astype(BF16)
        slope = below + inner * (jnp.exp(-0.5 * inner * inner) * (1.0 / math.sqrt(2.0 * math.pi)))
        dinner = (mm(douter, contract, NT) * slope).astype(BF16)
        dfirst = mm(dinner, expand, NT) + dsecond
        dresid = norm_back(dfirst, vecs[3:4, :], unit_first, inverse_first)
        dresid_ref[here, :] = dresid
        low_ref[here, :] = dresid.astype(BF16)
        active_ref[here, :] = active
        douter_ref[here, :] = douter
        first_ref[here, :] = first_low
        dinner_ref[here, :] = dinner

        def down(rows):
            return jnp.sum(rows, axis=0, keepdims=True)

        dbias = down(dinner.astype(F32))
        dvecs_ref[...] += jnp.concatenate(
            [
                dbias[:, :128],
                dbias[:, 128:],
                down(douter.astype(F32)),
                down(dfirst * unit_first),
                down(dfirst),
                down(grad * unit),
                down(grad),
                jnp.zeros((1, 128), F32),
            ],
            axis=0,
        )
        return carry

    lax.fori_loop(0, dresid_ref.shape[0] // ROWS, some_rows, 0)
    scatter_rows(route_ref[...], low_ref[...], send_ref)
    dcontract_ref[...] = mm(active_ref[...], douter_ref[...], TN)
    dexpand_ref[...] = mm(first_ref[...], dinner_ref[...], TN)


def finish_kernel(route_col_ref, arrived_ref, dresid_ref, out_ref):
    for c in range(out_ref.shape[0] // ROWS):
        part = slice(c * ROWS, (c + 1) * ROWS)
        hot = one_hot_columns(route_col_ref[part, :], arrived_ref.shape[0])
        out_ref[part, :] = dresid_ref[part, :] + mm(hot, arrived_ref[...])


def unpack_kernel(order, share, block_rows, shards_ref, *rest):
    flat_ref = rest[-1]
    outs = rest[:-1]
    lane = iota((block_rows, 128), 1)
    for device, place in enumerate(order):
        row, shift = divmod(device * share, 128)
        block = shards_ref[place].astype(F32)
        if shift:
            block = pltpu.roll(block, shift, 1)
            before = jnp.concatenate([flat_ref[pl.ds(row, 1), :], block[:-1]], axis=0)
            block = jnp.where(lane >= shift, block, before)
        flat_ref[pl.ds(row, block_rows), :] = block
    for layer in range(LAYERS):
        win_ref, wout_ref, expand_ref, contract_ref, vecs_ref = outs[5 * layer : 5 * layer + 5]
        base = layer * LAYER_ROWS
        for j in range(3):
            win_ref[:, 128 * j : 128 * j + 128] = flat_ref[pl.ds(base + j, 128, stride=3), :].astype(
                BF16
            )
        wout_ref[...] = flat_ref[pl.ds(base + 384, 128), :].astype(BF16)
        for j in range(2):
            expand_ref[:, 128 * j : 128 * j + 128] = flat_ref[
                pl.ds(base + 512 + j, 128, stride=2), :
            ].astype(BF16)
        contract_ref[...] = flat_ref[pl.ds(base + 768, 256), :].astype(BF16)
        vecs_ref[0:7, :] = flat_ref[pl.ds(base + 1024, 7), :]
        vecs_ref[7:8, :] = jnp.zeros((1, 128), F32)


def pack_kernel(devices, share, block_rows, *refs):
    flat_ref = refs[-1]
    out_ref = refs[-2]
    for layer in range(LAYERS):
        dwin_ref, dwout_ref, dexpand_ref, dcontract_ref, dvecs_ref = refs[5 * layer : 5 * layer + 5]
        base = layer * LAYER_ROWS
        for j in range(3):
            flat_ref[pl.ds(base + j, 128, stride=3), :] = dwin_ref[:, 128 * j : 128 * j + 128]
        flat_ref[pl.ds(base + 384, 128), :] = dwout_ref[...]
        for j in range(2):
            flat_ref[pl.ds(base + 512 + j, 128, stride=2), :] = dexpand_ref[
                :, 128 * j : 128 * j + 128
            ]
        flat_ref[pl.ds(base + 768, 256), :] = dcontract_ref[...]
        flat_ref[pl.ds(base + 1024, 7), :] = dvecs_ref[0:7, :]
    end = LAYERS * LAYER_ROWS
    flat_ref[pl.ds(end, flat_ref.shape[0] - end), :] = jnp.zeros(
        (flat_ref.shape[0] - end, 128), F32
    )
    lane = iota((block_rows, 128), 1)
    for device in range(devices):
        row, shift = divmod(device * share, 128)
        block = flat_ref[pl.ds(row, block_rows), :]
        if shift:
            after = flat_ref[pl.ds(row + 1, block_rows), :]
            block = pltpu.roll(jnp.where(lane >= shift, block, after), 128 - shift, 1)
        out_ref[device] = block.astype(BF16)


def call(body, outs, *args, scratch=()):
    return pl.pallas_call(
        body,
        out_shape=tuple(shape_of(s, d) for s, d in outs),
        scratch_shapes=[pltpu.VMEM(s, d) for s, d in scratch],
        compiler_params=PARAMS,
    )(*args)


def exchange(buffer, axes=AXES):
    return lax.all_to_all(buffer, axes, split_axis=0, concat_axis=0, tiled=True)


def on_lanes(ids):
    return jnp.broadcast_to(ids[:, None], (ids.shape[0], 128))


def shards(
    tokens,
    positions,
    cotangent,
    route_send,
    recv_slot,
    slot_bucket,
    master,
    first_moment,
    second_moment,
):
    groups = lax.axis_size("grp")
    windows = lax.axis_size("win")
    devices = groups * windows
    home = tokens.shape[0]
    arrivals = recv_slot.shape[2]
    share = master.shape[0]
    block_rows = -(-share // 128)
    block_rows = -(-block_rows // 16) * 16
    width = PILLAR_WIDTH

    heads_id = jnp.concatenate(
        [jnp.arange(1024, dtype=jnp.int32) // 128, jnp.arange(128, dtype=jnp.int32) // 16]
    )
    lane = jnp.arange(128, dtype=jnp.int32)
    heads = (heads_id[:, None] == lane[None, :] // 16).astype(BF16)
    slot = jnp.arange(WINDOW_SLOTS, dtype=jnp.int32)
    wide = jnp.arange(256, dtype=jnp.int32)
    wide = jnp.where(wide < 128, wide, 128 + wide % 16)
    unfold = (slot[:, None] == wide[None, :]).astype(BF16)

    mine = jnp.pad(master.astype(BF16), (0, block_rows * 128 - share)).reshape(1, block_rows, 128)
    copies = exchange(jnp.broadcast_to(mine, (groups, block_rows, 128)), "grp")
    copies = exchange(
        jnp.broadcast_to(copies[None], (windows, groups, block_rows, 128)).reshape(
            devices, block_rows, 128
        ),
        "win",
    )
    order = [(d % windows) * groups + d // windows for d in range(devices)]
    flat_rows = -(-(((devices - 1) * share) // 128 + block_rows + 8) // 8) * 8
    layer_shapes = (
        ((width, 3 * width), BF16),
        ((width, width), BF16),
        ((width, FF), BF16),
        ((FF, width), BF16),
        ((8, width), F32),
    )
    params = call(
        functools.partial(unpack_kernel, order, share, block_rows),
        layer_shapes * LAYERS,
        copies,
        scratch=(((flat_rows, 128), F32),),
    )
    params = [params[5 * l : 5 * l + 5] for l in range(LAYERS)]

    send, send_next = call(
        start_kernel,
        (((arrivals, 2 * width), BF16), ((arrivals, width), BF16)),
        route_send,
        tokens,
        positions,
    )
    arrived = exchange(send)
    pos_next = exchange(send_next)

    recv = [recv_slot[l] for l in range(LAYERS)]
    recv_col = [on_lanes(recv_slot[l, 0]) for l in range(LAYERS)]
    route = [route_send[l : l + 1] for l in range(LAYERS)]
    route_col = [on_lanes(route_send[l]) for l in range(LAYERS)]
    bucket = [on_lanes(slot_bucket[l]) for l in range(LAYERS)]

    def owner_forward(layer, rows, pos):
        win, wout = params[layer][:2]
        args = [recv[layer], recv_col[layer], bucket[layer], heads, win, wout, rows]
        if pos is None:
            body = lambda *refs: owner_forward_kernel(*refs[:7], None, *refs[7:])
        else:
            body = owner_forward_kernel
            args.append(pos)
        return call(
            body,
            (
                ((arrivals, width), BF16),
                ((DEVICE_SLOTS, 2 * width), BF16),
                ((DEVICE_SLOTS, 3 * width), BF16),
                ((DEVICE_SLOTS, EXPANDED), BF16),
                ((DEVICE_SLOTS, width), F32),
                ((DEVICE_SLOTS, width), F32),
            ),
            *args,
            scratch=(((DEVICE_SLOTS, width), BF16),),
        )

    def owner_backward(layer, grads, kept):
        win, wout = params[layer][:2]
        return call(
            owner_backward_kernel,
            (
                ((arrivals, width), BF16),
                ((width, 3 * width), F32),
                ((width, width), F32),
            ),
            recv[layer],
            recv_col[layer],
            bucket[layer],
            heads,
            unfold,
            win,
            wout,
            grads,
            *kept,
            scratch=(
                ((DEVICE_SLOTS, width), BF16),
                ((DEVICE_SLOTS, width), BF16),
                ((DEVICE_SLOTS, 3 * width), BF16),
            ),
        )

    def home_backward(layer, top, arrived_rows, base, grad):
        outs = (
            ((home, width), F32),
            ((arrivals, width), BF16),
            ((width, FF), F32),
            ((FF, width), F32),
            ((8, width), F32),
        )
        if top:
            outs = (((home, width), BF16),) + outs
        return call(
            functools.partial(home_backward_kernel, top),
            outs,
            route_col[1],
            route[layer],
            arrived_rows,
            base,
            grad,
            *params[layer][2:],
            scratch=(
                ((home, FF), BF16),
                ((home, width), BF16),
                ((home, width), BF16),
                ((home, FF), BF16),
                ((home, width), BF16),
            ),
        )

    send, *kept_zero = owner_forward(0, arrived, None)
    state, send, resid_zero = call(
        home_forward_kernel,
        (((home, width), BF16), ((arrivals, width), BF16), ((home, width), F32)),
        route_col[0],
        route[1],
        exchange(send),
        tokens,
        *params[0][2:],
    )
    send, *kept_one = owner_forward(1, exchange(send), pos_next)
    mixed, dresid, send, *ffn_one = home_backward(1, True, exchange(send), state, cotangent)
    send, *att_one = owner_backward(1, exchange(send), kept_one)
    dresid, send, *ffn_zero = home_backward(0, False, exchange(send), resid_zero, dresid)
    send, *att_zero = owner_backward(0, exchange(send), kept_zero)
    (tokens_grad,) = call(
        finish_kernel, (((home, width), F32),), route_col[0], exchange(send), dresid
    )

    (packed,) = call(
        functools.partial(pack_kernel, devices, share, block_rows),
        (((devices, block_rows, 128), BF16),),
        *att_zero,
        *ffn_zero,
        *att_one,
        *ffn_one,
        scratch=(((flat_rows, 128), F32),),
    )
    shard = jnp.sum(exchange(packed).astype(F32), axis=0).reshape(-1)[:share]
    partial_square = jnp.broadcast_to(jnp.sum(shard * shard), (devices, 8, 128))
    total = jnp.sqrt(jnp.sum(exchange(partial_square)[:, 0, 0]))
    clip_limit = 0.25 * math.sqrt(NPARAM)
    factor = jnp.minimum(1.0, clip_limit / (total + 1e-06))
    clipped = shard * factor
    new_first = beta_one * first_moment + (1.0 - beta_one) * clipped
    new_second = beta_two * second_moment + (1.0 - beta_two) * clipped * clipped
    first_hat = new_first / (1.0 - beta_one**adam_step)
    second_hat = new_second / (1.0 - beta_two**adam_step)
    new_master = master - rate * (first_hat / (jnp.sqrt(second_hat) + adam_eps) + decay * master)
    return (
        mixed,
        tokens_grad,
        total.reshape(1),
        clipped,
        new_master,
        new_first,
        new_second,
        new_master.astype(BF16),
    )


def solution(mesh):
    in_specs = (
        P(("grp", "win"), None),
        P(None, ("grp", "win"), None),
        P(("grp", "win"), None),
        P(None, ("grp", "win")),
        P(None, ("grp", "win"), None),
        P(None, ("grp", "win")),
        P(("grp", "win")),
        P(("grp", "win")),
        P(("grp", "win")),
    )
    out_specs = (
        P(("grp", "win"), None),
        P(("grp", "win"), None),
        P(),
        P(("grp", "win")),
        P(("grp", "win")),
        P(("grp", "win")),
        P(("grp", "win")),
        P(("grp", "win")),
    )
    return jax.shard_map(shards, mesh=mesh, in_specs=in_specs, out_specs=out_specs, check_vma=False)
```

```python
import functools
import math

import jax
import jax.numpy as jnp
from jax import lax
from jax.experimental import pallas as pl
from jax.experimental.pallas import tpu as pltpu
from jax.sharding import PartitionSpec as P

PILLAR_WIDTH = 128
FF = 256
HEAD_COUNT = 8
HDIM = 16
WINDOW_SLOTS = 144
LAYERS = 2
DEVICE_SLOTS = 1728
NSUB = 12
NPARAM = 263936
LAYER_ROWS = 1031
EXPANDED = HEAD_COUNT * WINDOW_SLOTS
MASKED = -1e30
LOWEST = -3e38

beta_one = 0.5
beta_two = 0.5
adam_step = 4
rate = 0.1
decay = 0.01
adam_eps = 1e-08

BF16 = jnp.bfloat16
F32 = jnp.float32
AXES = ("grp", "win")

NN = (((1,), (0,)), ((), ()))
NT = (((1,), (1,)), ((), ()))
TN = (((0,), (0,)), ((), ()))


def mm(left, right, dims=NN):
    return lax.dot_general(left, right, dims, preferred_element_type=F32)


def iota(shape, dim):
    return lax.broadcasted_iota(jnp.int32, shape, dim)


def shape_of(shape, dtype):
    return jax.ShapeDtypeStruct(shape, dtype)


def one_hot_rows(row_ids, first, count):
    return jnp.where(iota((count, row_ids.shape[1]), 0) + first == row_ids, 1.0, 0.0).astype(BF16)


def one_hot_columns(column_ids, width):
    lane = iota(column_ids.shape, 1)
    pieces = [
        jnp.where(column_ids == lane + 128 * k, 1.0, 0.0).astype(BF16)
        for k in range(-(-width // 128))
    ]
    return jnp.concatenate(pieces, axis=1)[:, :width]


def expand_heads(block, heads):
    main = block[:128]
    tail = block[128:]
    return jnp.concatenate([main] * HEAD_COUNT + [tail] * HEAD_COUNT, axis=0) * heads


def scatter_rows(route_row, low_rows, send, chunk=256):
    for c in range(send.shape[0] // chunk):
        hot = one_hot_rows(route_row, c * chunk, chunk)
        send[c * chunk : (c + 1) * chunk, :] = mm(hot, low_rows).astype(BF16)


def land_rows(recv_col, slot_values, send, chunk=128):
    for c in range(send.shape[0] // chunk):
        part = slice(c * chunk, (c + 1) * chunk)
        hot = one_hot_columns(recv_col[part, :], DEVICE_SLOTS)
        send[part, :] = mm(hot, slot_values).astype(BF16)


def start_kernel(route_ref, tokens_ref, pos_ref, out_ref):
    both = jnp.concatenate([tokens_ref[...], pos_ref[...]], axis=1)
    scatter_rows(route_ref[...], both, out_ref)


def start_next_kernel(route_ref, pos_ref, cotangent_ref, pos_out_ref, cotangent_out_ref):
    both = jnp.concatenate([pos_ref[...], cotangent_ref[...]], axis=1)
    for c in range(pos_out_ref.shape[0] // 256):
        part = slice(c * 256, (c + 1) * 256)
        sent = mm(one_hot_rows(route_ref[...], c * 256, 256), both).astype(BF16)
        pos_out_ref[part, :] = sent[:, :128]
        cotangent_out_ref[part, :] = sent[:, 128:]


def slots_kernel(recv_ref, rows_ref, out_ref):
    for run in range(NSUB):
        part = slice(run * WINDOW_SLOTS, (run + 1) * WINDOW_SLOTS)
        hot = one_hot_rows(recv_ref[...], run * WINDOW_SLOTS, WINDOW_SLOTS)
        out_ref[part, :] = mm(hot, rows_ref[...]).astype(BF16)


def project_in(weights_ref):
    return jnp.concatenate([weights_ref[128 * j : 128 * j + 128, :] for j in range(3)], axis=1)


def project_out(weights_ref):
    return weights_ref[384:512, :]


def feed_weights(weights_ref):
    expand = jnp.concatenate([weights_ref[512:640, :], weights_ref[640:768, :]], axis=1)
    return expand, weights_ref[768:1024, :], weights_ref[1024:1040, :].astype(F32)


def interleave(count, make):
    waiting = [make(i) for i in range(count)]
    running = []
    while waiting or running:
        if waiting:
            running.insert(0, waiting.pop(0))
        running = [part for part in running if next(part, running) is not running]


def run_rows(run):
    return pl.ds(run * WINDOW_SLOTS, WINDOW_SLOTS)


def kept_copy(k, run, far, near, sems, out):
    far, near = far.at[run_rows(run), :], near.at[run_rows(run), :]
    ends = (near, far) if out else (far, near)
    return pltpu.make_async_copy(*ends, sems.at[k, run])


def attend_stages(run, slot_rows, joined, bucket, bucket_row, heads_ref, weights_ref, low, full):
    win = project_in(weights_ref)
    query_key = mm(joined, win[:, :256])
    queries = (query_key[:, :128] * 0.25).astype(BF16)
    keys = query_key[:, 128:].astype(BF16)
    values = mm(slot_rows, win[:, 256:]).astype(BF16)
    heads = heads_ref[...]
    block = heads[1024:]
    spread = jnp.concatenate(
        [
            queries * jnp.concatenate([heads[128 * h : 128 * h + 16]] * 9, axis=0)
            for h in range(HEAD_COUNT)
        ],
        axis=0,
    )
    yield
    scores = mm(spread, keys[:128], NT)
    tail = mm(queries, jnp.concatenate([keys[128:]] * 8, axis=0) * block, NT)
    yield

    def same(row):
        return jnp.where((bucket == row) & (row >= 0), 0.0, MASKED)

    main_bias = same(bucket_row[0:1, :])
    tail = tail + same(bucket_row[1:2, :])
    segment = iota((WINDOW_SLOTS, 128), 1) >> 4
    tail_top = jnp.zeros((WINDOW_SLOTS, 128), F32)
    pieces = []
    for h in range(HEAD_COUNT):
        main = scores[WINDOW_SLOTS * h : WINDOW_SLOTS * (h + 1)] + main_bias
        own_tail = segment == h
        top = jnp.max(jnp.maximum(main, jnp.where(own_tail, tail, LOWEST)), axis=1, keepdims=True)
        tail_top = jnp.where(own_tail, top, tail_top)
        pieces.append(jnp.exp(main - top).astype(BF16))
    pieces.append(jnp.exp(tail - tail_top).astype(BF16))
    expo = jnp.concatenate(pieces, axis=1)
    low(jnp.concatenate([joined, slot_rows, queries, keys, values, expo], axis=1))
    yield
    summed = mm(expo, jnp.concatenate([expand_heads(values, heads), heads], axis=1))
    yield
    share = jnp.where(bucket >= 0, 1.0, 0.0) / summed[:, 128:]
    attended = summed[:, :128] * share
    full(jnp.concatenate([attended, share], axis=1))
    return mm(attended.astype(BF16), project_out(weights_ref)).astype(BF16)


def attend_back_stages(run, dbranch, heads_ref, unfold_ref, weights_ref, low, full, scratch):
    attended_ref, dbranch_ref, dqkv_ref = scratch
    here = run_rows(run)
    dbranch_ref[here, :] = dbranch
    dattended = mm(dbranch, project_out(weights_ref), NT).astype(BF16).astype(F32)
    yield
    heads = heads_ref[...]
    block = heads[1024:]
    kept = full()
    out = kept[:, :128]
    attended_ref[here, :] = out.astype(BF16)
    dout = (dattended * kept[:, 128:256]).astype(BF16)
    weighed = dout.astype(F32) * out
    weighed_high = weighed.astype(BF16)
    weighed_low = (weighed - weighed_high.astype(F32)).astype(BF16)
    centre = mm(weighed_high, block) + mm(weighed_low, block)
    low_ref = low()
    queries = low_ref[here, 256:384]
    keys_wide = expand_heads(low_ref[here, 384:512], heads)
    dprob = mm(dout, expand_heads(low_ref[here, 512:640], heads), NT)
    yield
    expo = low_ref[here, 640:]
    pieces = [
        (
            (dprob[:, 128 * h : 128 * h + 128] - centre[:, 16 * h : 16 * h + 1])
            * expo[:, 128 * h : 128 * h + 128].astype(F32)
        ).astype(BF16)
        for h in range(HEAD_COUNT)
    ]
    pieces.append(((dprob[:, 1024:] - centre) * expo[:, 1024:].astype(F32)).astype(BF16))
    dscore = jnp.concatenate(pieces, axis=1)
    yield
    dqueries = (mm(dscore, keys_wide) * 0.25).astype(BF16)

    def gathered(left, right):
        wide = mm(left, right, TN)
        main = jnp.concatenate(
            [wide[16 * h : 16 * h + 16, 128 * h : 128 * h + 128] for h in range(HEAD_COUNT)],
            axis=0,
        )
        return jnp.concatenate([main, wide[:, 1024:] * block.astype(F32)], axis=1).astype(BF16)

    folded = jnp.concatenate([gathered(queries, dscore), gathered(dout, expo)], axis=0)
    yield
    dkeys_values = mm(unfold_ref[...], folded, NT).astype(BF16)
    dqkv = jnp.concatenate([dqueries, dkeys_values], axis=1)
    dqkv_ref[here, :] = dqkv
    yield
    return mm(dqkv, project_in(weights_ref), NT).astype(BF16)


def projection_grads(low_ref, scratch, dwin_ref, dwout_ref):
    attended_ref, dbranch_ref, dqkv_ref = scratch
    dwout_ref[...] = mm(attended_ref[...], dbranch_ref[...], TN)
    dqkv = dqkv_ref[...]
    dwin_ref[:, :256] = mm(low_ref[:, 0:128], dqkv[:, :256], TN)
    dwin_ref[:, 256:] = mm(low_ref[:, 128:256], dqkv[:, 256:], TN)


def owner_kernel(
    last,
    recv_ref,
    bucket_ref,
    bucket_row_ref,
    heads_ref,
    weights_ref,
    rows_ref,
    *rest,
):
    if last:
        pos_ref, *rest = rest
    (
        recv_col_far,
        send_ref,
        low_far,
        full_far,
        leave_ref,
        low_ref,
        full_ref,
        recv_col_ref,
        sems,
        recv_sem,
    ) = rest
    recv_copy = pltpu.make_async_copy(recv_col_far, recv_col_ref, recv_sem.at[0])
    recv_copy.start()

    def one_run(run):
        here = run_rows(run)

        def low(rows):
            low_ref[here, :] = rows
            kept_copy(0, run, low_far, low_ref, sems, True).start()

        def full(rows):
            full_ref[here, 0:256] = rows
            if not last:
                kept_copy(1, run, full_far, full_ref, sems, True).start()

        landed = mm(one_hot_rows(recv_ref[...], run * WINDOW_SLOTS, WINDOW_SLOTS), rows_ref[...])
        state = landed[:, :128]
        pos = pos_ref[here, :].astype(F32) if last else landed[:, 128:]
        yield
        branch = yield from attend_stages(
            run,
            state.astype(BF16),
            (state + pos).astype(BF16),
            bucket_ref[here, :].astype(F32),
            bucket_row_ref[run],
            heads_ref,
            weights_ref,
            low,
            full,
        )
        if not last:
            leave_ref[here, :] = branch
            return
        yield
        resid = state + branch.astype(F32)
        full_ref[here, 256:384] = resid
        kept_copy(1, run, full_far, full_ref, sems, True).start()
        expand, contract, vecs = feed_weights(weights_ref)
        second = (yield from feed_forward(resid, expand, contract, vecs))[-1]
        yield
        unit, _ = centred_rows(second)
        leave_ref[here, :] = (unit * vecs[5:6, :] + vecs[6:7, :]).astype(BF16)

    interleave(NSUB, one_run)
    recv_copy.wait()
    land_rows(recv_col_ref, leave_ref[...], send_ref)
    for run in range(NSUB):
        kept_copy(0, run, low_far, low_ref, sems, True).wait()
        kept_copy(1, run, full_far, full_ref, sems, True).wait()


def owner_back_kernel(
    last,
    late,
    recv_ref,
    heads_ref,
    unfold_ref,
    weights_ref,
    grads_ref,
    recv_col_far,
    low_far,
    full_far,
    send_ref,
    *rest,
):
    if last:
        dwin_ref, dwout_ref, dexpand_ref, dcontract_ref, dvecs_ref, *rest = rest
        active_ref, douter_ref, first_ref, dinner_ref, *rest = rest
        ffn_refs = (active_ref, douter_ref, first_ref, dinner_ref)
    else:
        dwin_ref, dwout_ref, flat_ref, *rest = rest
    (
        attended_ref,
        dbranch_ref,
        dqkv_ref,
        drows_ref,
        low_ref,
        full_ref,
        recv_col_ref,
        sems,
        recv_sem,
    ) = rest
    scratch = (attended_ref, dbranch_ref, dqkv_ref)
    for run in range(NSUB):
        kept_copy(1, run, full_far, full_ref, sems, False).start()
        kept_copy(0, run, low_far, low_ref, sems, False).start()
    recv_copy = pltpu.make_async_copy(recv_col_far, recv_col_ref, recv_sem.at[0])
    recv_copy.start()
    dvecs = []

    def one_run(run):
        here = run_rows(run)

        def low():
            kept_copy(0, run, low_far, low_ref, sems, False).wait()
            return low_ref

        grad = mm(one_hot_rows(recv_ref[...], run * WINDOW_SLOTS, WINDOW_SLOTS), grads_ref[...])
        yield
        if last:
            kept_copy(1, run, full_far, full_ref, sems, False).wait()
            dresid = yield from feed_back(
                here, full_ref[here, 256:384], grad, weights_ref, ffn_refs, dvecs
            )
            dbranch = dresid.astype(BF16)
        else:
            dbranch = grad.astype(BF16)

        def full():
            if not last:
                kept_copy(1, run, full_far, full_ref, sems, False).wait()
            return full_ref[here, 0:256]

        drows = yield from attend_back_stages(
            run, dbranch, heads_ref, unfold_ref, weights_ref, low, full, scratch
        )
        if last:
            drows = (dresid + drows.astype(F32)).astype(BF16)
        drows_ref[here, :] = drows

    interleave(NSUB, one_run)
    recv_copy.wait()
    drows = drows_ref[...]
    if last:
        dvecs_ref[...] = sum(dvecs)
        land_rows(recv_col_ref, drows, send_ref)
        projection_grads(low_ref, scratch, dwin_ref, dwout_ref)
        dcontract_ref[...] = mm(active_ref[...], douter_ref[...], TN)
        dexpand_ref[...] = mm(first_ref[...], dinner_ref[...], TN)
        return
    projection_grads(low_ref, scratch, dwin_ref, dwout_ref)
    devices, rows, _ = send_ref.shape
    capacity = recv_col_ref.shape[0] // devices
    for c in range(recv_col_ref.shape[0] // 128):
        hot = one_hot_columns(recv_col_ref[c * 128 : c * 128 + 128, :], DEVICE_SLOTS)
        sent = mm(hot, drows).astype(BF16)
        for part in range(128 // capacity):
            send_ref[c * 128 // capacity + part, 0:capacity, :] = sent[
                part * capacity : part * capacity + capacity
            ]
    share, quarter_rows = late
    store_projections(flat_ref, 0, dwin_ref, dwout_ref)
    flat_ref[pl.ds(512, flat_ref.shape[0] - 512), :] = jnp.zeros(
        (flat_ref.shape[0] - 512, 128), F32
    )
    owners = devices // 4
    for device in range(devices):
        quarter, owner = divmod(device, owners)
        block = share_block(
            flat_ref, owner * share, share, quarter * quarter_rows, rows - capacity, quarter_rows
        )
        send_ref[device, capacity:rows, :] = block.astype(BF16)


def share_block(flat_ref, start, share, first_row, rows, used_rows):
    row, shift = divmod(start, 128)
    row = row + first_row
    lane = iota((rows, 128), 1)
    line = iota((rows, 128), 0)
    block = flat_ref[pl.ds(row, rows), :]
    if shift:
        after = flat_ref[pl.ds(row + 1, rows), :]
        block = pltpu.roll(jnp.where(lane >= shift, block, after), 128 - shift, 1)
    inside = (line < used_rows) & ((line + first_row) * 128 + lane < share)
    return jnp.where(inside, block, 0.0)


def store_projections(flat_ref, base, dwin_ref, dwout_ref):
    for j in range(3):
        flat_ref[pl.ds(base + j, 128, stride=3), :] = dwin_ref[:, 128 * j : 128 * j + 128]
    flat_ref[pl.ds(base + 384, 128), :] = dwout_ref[...]


def centred_rows(rows):
    centre = rows - jnp.mean(rows, axis=-1, keepdims=True)
    spread = jnp.mean(centre * centre, axis=-1, keepdims=True)
    inverse = lax.rsqrt(spread + 1e-05)
    return centre * inverse, inverse


def norm_back(grad, gain, unit, inverse):
    dunit = grad * gain
    return (
        dunit
        - jnp.mean(dunit, axis=-1, keepdims=True)
        - unit * jnp.mean(dunit * unit, axis=-1, keepdims=True)
    ) * inverse


def feed_forward(resid, expand, contract, vecs):
    unit, inverse = centred_rows(resid)
    first = unit * vecs[3:4, :] + vecs[4:5, :]
    first_low = first.astype(BF16)
    bias = jnp.concatenate([vecs[0:1, :], vecs[1:2, :]], axis=1)
    inner = mm(first_low, expand) + bias
    yield
    below = 0.5 + 0.5 * lax.erf(inner * math.sqrt(0.5))
    active = (inner * below).astype(BF16)
    second = first + (mm(active, contract) + vecs[2:3, :])
    return unit, inverse, first_low, inner, below, active, second


def feed_back(here, resid, grad, weights_ref, ffn_refs, dvecs):
    active_ref, douter_ref, first_ref, dinner_ref = ffn_refs
    expand, contract, vecs = feed_weights(weights_ref)
    unit_first, inverse_first, first_low, inner, below, active, second = yield from feed_forward(
        resid, expand, contract, vecs
    )
    active_ref[here, :] = active
    first_ref[here, :] = first_low
    yield
    unit, inverse = centred_rows(second)
    dsecond = norm_back(grad, vecs[5:6, :], unit, inverse)
    douter = dsecond.astype(BF16)
    douter_ref[here, :] = douter
    dactive = mm(douter, contract, NT)
    slope = below + inner * (jnp.exp(-0.5 * inner * inner) * (1.0 / math.sqrt(2.0 * math.pi)))
    yield
    dinner = (dactive * slope).astype(BF16)
    dinner_ref[here, :] = dinner
    dfirst = mm(dinner, expand, NT) + dsecond
    yield

    def down(rows):
        return jnp.sum(rows, axis=0, keepdims=True)

    dbias = down(dinner.astype(F32))
    dvecs.append(
        jnp.concatenate(
            [
                dbias[:, :128],
                dbias[:, 128:],
                down(douter.astype(F32)),
                down(dfirst * unit_first),
                down(dfirst),
                down(grad * unit),
                down(grad),
                jnp.zeros((1, 128), F32),
            ],
            axis=0,
        )
    )
    return norm_back(dfirst, vecs[3:4, :], unit_first, inverse_first)


ROWS = 128


def part_rows(part):
    return pl.ds(part * ROWS, ROWS)


def home_forward_kernel(
    route_col_ref,
    route_ref,
    branch_ref,
    state_ref,
    weights_ref,
    send_ref,
    resid_ref,
    result_ref,
):
    def some_rows(part):
        here = part_rows(part)
        expand, contract, vecs = feed_weights(weights_ref)
        hot = one_hot_columns(route_col_ref[here, :], branch_ref.shape[0])
        resid = state_ref[here, :].astype(F32) + mm(hot, branch_ref[...])
        yield
        resid_ref[here, :] = resid
        second = (yield from feed_forward(resid, expand, contract, vecs))[-1]
        yield
        unit, _ = centred_rows(second)
        result_ref[here, :] = (unit * vecs[5:6, :] + vecs[6:7, :]).astype(BF16)

    interleave(result_ref.shape[0] // ROWS, some_rows)
    scatter_rows(route_ref[...], result_ref[...], send_ref)


def home_backward_kernel(
    route_col_ref,
    route_ref,
    arrived_ref,
    resid_ref,
    weights_ref,
    dresid_ref,
    send_ref,
    dexpand_ref,
    dcontract_ref,
    dvecs_ref,
    active_ref,
    douter_ref,
    first_ref,
    dinner_ref,
    low_ref,
):
    ffn_refs = (active_ref, douter_ref, first_ref, dinner_ref)
    dvecs = []

    def some_rows(part):
        here = part_rows(part)
        hot = one_hot_columns(route_col_ref[here, :], arrived_ref.shape[0])
        grad = mm(hot, arrived_ref[...])
        yield
        dresid = yield from feed_back(
            here, resid_ref[here, :], grad, weights_ref, ffn_refs, dvecs
        )
        dresid_ref[here, :] = dresid
        low_ref[here, :] = dresid.astype(BF16)

    interleave(dresid_ref.shape[0] // ROWS, some_rows)
    dvecs_ref[...] = sum(dvecs)
    scatter_rows(route_ref[...], low_ref[...], send_ref)
    dcontract_ref[...] = mm(active_ref[...], douter_ref[...], TN)
    dexpand_ref[...] = mm(first_ref[...], dinner_ref[...], TN)


def take_kernel(route_col_ref, arrived_ref, out_ref):
    for part in range(out_ref.shape[0] // ROWS):
        here = part_rows(part)
        hot = one_hot_columns(route_col_ref[here, :], arrived_ref.shape[0])
        out_ref[here, :] = mm(hot, arrived_ref[...]).astype(BF16)


def finish_kernel(route_col_ref, arrived_ref, dresid_ref, out_ref, rows_ref):
    devices, rows, _ = arrived_ref.shape
    capacity = rows_ref.shape[0] // devices
    for device in range(devices):
        rows_ref[device * capacity : (device + 1) * capacity, :] = arrived_ref[
            device, 0:capacity, :
        ]
    for part in range(out_ref.shape[0] // ROWS):
        here = part_rows(part)
        hot = one_hot_columns(route_col_ref[here, :], rows_ref.shape[0])
        out_ref[here, :] = dresid_ref[here, :] + mm(hot, rows_ref[...])


def late_kernel(arrived_ref, early_ref, late_ref, square_ref):
    devices, rows, _ = arrived_ref.shape
    capacity = rows - late_ref.shape[0]
    late = arrived_ref[0, capacity:rows, :].astype(F32)
    for device in range(1, devices):
        late = late + arrived_ref[device, capacity:rows, :].astype(F32)
    late_ref[...] = late
    early = early_ref[...]
    square = jnp.sum(early * early) + jnp.sum(late * late)
    square_ref[...] = jnp.full(square_ref.shape, square, F32)


def unpack_kernel(share, me_ref, shards_ref, *rest):
    flat_ref = rest[-1]
    outs = rest[:-1]
    devices, block_rows, _ = shards_ref.shape
    lane = iota((block_rows, 128), 1)
    me = me_ref[0]
    for device in range(devices):
        row, shift = divmod(device * share, 128)
        block = shards_ref[me ^ device].astype(F32)
        if shift:
            block = pltpu.roll(block, shift, 1)
            before = jnp.concatenate([flat_ref[pl.ds(row, 1), :], block[:-1]], axis=0)
            block = jnp.where(lane >= shift, block, before)
        flat_ref[pl.ds(row, block_rows), :] = block
    for layer, out_ref in enumerate(outs):
        base = layer * LAYER_ROWS
        for j in range(3):
            out_ref[128 * j : 128 * j + 128, :] = flat_ref[pl.ds(base + j, 128, stride=3), :].astype(
                BF16
            )
        out_ref[384:512, :] = flat_ref[pl.ds(base + 384, 128), :].astype(BF16)
        for j in range(2):
            out_ref[512 + 128 * j : 640 + 128 * j, :] = flat_ref[
                pl.ds(base + 512 + j, 128, stride=2), :
            ].astype(BF16)
        out_ref[768:1024, :] = flat_ref[pl.ds(base + 768, 256), :].astype(BF16)
        vecs = flat_ref[pl.ds(base + 1024, 16), :]
        out_ref[1024:1040, :] = jnp.where(iota((16, 128), 0) < 7, vecs, 0.0).astype(BF16)


def pack_kernel(
    share,
    dwin_ref,
    dwout_ref,
    dexpand_ref,
    dcontract_ref,
    dvecs_ref,
    dexpand_zero_ref,
    dcontract_zero_ref,
    dvecs_zero_ref,
    out_ref,
    flat_ref,
):
    devices, block_rows, _ = out_ref.shape
    flat_ref[0:512, :] = jnp.zeros((512, 128), F32)
    store_projections(flat_ref, LAYER_ROWS, dwin_ref, dwout_ref)
    for base, expand, contract, vecs in (
        (0, dexpand_zero_ref, dcontract_zero_ref, dvecs_zero_ref),
        (LAYER_ROWS, dexpand_ref, dcontract_ref, dvecs_ref),
    ):
        for j in range(2):
            flat_ref[pl.ds(base + 512 + j, 128, stride=2), :] = expand[:, 128 * j : 128 * j + 128]
        flat_ref[pl.ds(base + 768, 256), :] = contract[...]
        flat_ref[pl.ds(base + 1024, 7), :] = vecs[0:7, :]
    end = LAYERS * LAYER_ROWS
    flat_ref[pl.ds(end, flat_ref.shape[0] - end), :] = jnp.zeros(
        (flat_ref.shape[0] - end, 128), F32
    )
    for device in range(devices):
        block = share_block(flat_ref, device * share, share, 0, block_rows, block_rows)
        out_ref[device] = block.astype(BF16)


def call(
    name, micros, body, outs, *args, fresh=(), scratch=(), vmem=24, smem=0, far_in=0, far_out=0, sems=()
):
    near = pl.BlockSpec(memory_space=pltpu.VMEM)
    far = pl.BlockSpec(memory_space=pltpu.HBM)
    specs = [pl.BlockSpec(memory_space=pltpu.SMEM)] * smem
    specs += [near] * (len(args) - smem - far_in) + [far] * far_in
    args = [
        x if i < smem or i in fresh else pltpu.with_memory_space_constraint(x, pltpu.HBM)
        for i, x in enumerate(args)
    ]
    return pl.pallas_call(
        body,
        out_shape=tuple(
            shape_of(o[0], o[1]) if len(o) == 2 else pltpu.HBM(o[0], o[1]) for o in outs
        ),
        in_specs=specs,
        out_specs=tuple([near] * (len(outs) - far_out) + [far] * far_out),
        scratch_shapes=[pltpu.VMEM(s[0], s[1]) for s in scratch]
        + [pltpu.SemaphoreType.DMA(s) for s in sems],
        compiler_params=pltpu.CompilerParams(vmem_limit_bytes=vmem << 20),
        cost_estimate=pl.CostEstimate(
            flops=int(micros * 1e9), bytes_accessed=1 << 16, transcendentals=0
        ),
        name=name,
    )(*args)


def exchange(buffer):
    return lax.all_to_all(buffer, AXES, split_axis=0, concat_axis=0, tiled=True)


def after(value, *others):
    return lax.optimization_barrier((value, *others))[0]


def on_lanes(ids):
    return jnp.broadcast_to(ids[:, None], (ids.shape[0], 128))


def shards(
    tokens,
    positions,
    cotangent,
    route_send,
    recv_slot,
    slot_bucket,
    master,
    first_moment,
    second_moment,
):
    devices = lax.axis_size("grp") * lax.axis_size("win")
    me = lax.axis_index(AXES)
    home = tokens.shape[0]
    arrivals = recv_slot.shape[2]
    share = master.shape[0]
    share_rows = -(-share // 128)
    block_rows = -(-share_rows // 8) * 8
    quarter_rows = -(-share_rows // 4)
    late_rows = -(-quarter_rows // 8) * 8
    capacity = arrivals // devices
    width = PILLAR_WIDTH
    flat_rows = -(-(((devices - 1) * share) // 128 + block_rows + 8) // 8) * 8
    late_flat_rows = -(-max(520, ((devices // 4) * share) // 128 + late_rows + 16) // 8) * 8

    heads_id = jnp.concatenate(
        [jnp.arange(1024, dtype=jnp.int32) // 128, jnp.arange(128, dtype=jnp.int32) // 16]
    )
    lane = jnp.arange(128, dtype=jnp.int32)
    heads = (heads_id[:, None] == lane[None, :] // 16).astype(BF16)
    slot = jnp.arange(WINDOW_SLOTS, dtype=jnp.int32)
    wide = jnp.arange(256, dtype=jnp.int32)
    wide = jnp.where(wide < 128, wide, 128 + wide % 16)
    unfold = (slot[:, None] == wide[None, :]).astype(BF16)

    route = [route_send[l : l + 1] for l in range(LAYERS)]
    recv = [recv_slot[l] for l in range(LAYERS)]
    recv_col = [on_lanes(recv_slot[l, 0]) for l in range(LAYERS)]
    route_col = [on_lanes(route_send[l]) for l in range(LAYERS)]
    bucket = [on_lanes(slot_bucket[l].astype(BF16)) for l in range(LAYERS)]
    by_run = slot_bucket.astype(F32).reshape(LAYERS, NSUB, WINDOW_SLOTS)
    bucket_row = jnp.stack([by_run[:, :, :128], jnp.tile(by_run[:, :, 128:], (1, 1, 8))], axis=2)

    (send,) = call(
        "start", 3, start_kernel, (((arrivals, 2 * width), BF16),), route[0], tokens, positions[0]
    )
    arrived = exchange(send)

    pos_send, cotangent_send = call(
        "start_next",
        3,
        start_next_kernel,
        (((arrivals, width), BF16, True), ((arrivals, width), BF16, True)),
        route[1],
        positions[1],
        cotangent,
    )

    copies = jnp.pad(master.astype(BF16), (0, block_rows * 128 - share)).reshape(1, block_rows, 128)
    step = devices // 2
    while step:
        if step == devices // 4:
            copies, pos_send, cotangent_send = lax.optimization_barrier(
                (copies, pos_send, cotangent_send)
            )
        other = lax.ppermute(copies, AXES, [(i, i ^ step) for i in range(devices)])
        copies = jnp.stack([copies, other], axis=1).reshape(-1, block_rows, 128)
        step //= 2
    params = call(
        "unpack",
        1,
        functools.partial(unpack_kernel, share),
        (((1040, width), BF16, True),) * LAYERS,
        me.reshape(1),
        copies,
        scratch=(((flat_rows, 128), F32),),
        smem=1,
    )
    kept_zero = (
        ((DEVICE_SLOTS, 640 + EXPANDED), BF16, True),
        ((DEVICE_SLOTS, 2 * width), F32, True),
    )
    kept_one = (kept_zero[0], ((DEVICE_SLOTS, 3 * width), F32, True))
    recv_col_shape = ((arrivals, 128), jnp.int32)
    slots_low = ((DEVICE_SLOTS, width), BF16)
    slots_wide = ((DEVICE_SLOTS, FF), BF16)
    back_scratch = (slots_low, slots_low, ((DEVICE_SLOTS, 3 * width), BF16))
    arrival_shape = ((arrivals, width), BF16)

    pos_arrived = exchange(after(pos_send, arrived))
    def owner(layer, rows, *pos):
        kept = (kept_zero, kept_one)[layer]
        return call(
            ("first_owner", "last_owner")[layer],
            (13, 18)[layer],
            functools.partial(owner_kernel, layer == 1),
            (arrival_shape, *kept),
            recv[layer],
            bucket[layer],
            bucket_row[layer],
            heads,
            params[layer],
            rows,
            *pos,
            recv_col[layer],
            fresh=(5,),
            scratch=(slots_low, *kept, recv_col_shape),
            far_in=1,
            far_out=2,
            sems=((2, NSUB), (1,)),
            vmem=40,
        )

    send, *stored_zero = owner(0, arrived)
    branch = exchange(after(send, pos_arrived))
    (pos_slots,) = call(
        "slots", 4, slots_kernel, ((*slots_low, True),), recv[1], pos_arrived
    )
    send, resid_zero = call(
        "home",
        8,
        home_forward_kernel,
        (arrival_shape, ((home, width), F32, True)),
        route_col[0],
        route[1],
        branch,
        tokens,
        params[0],
        fresh=(2,),
        scratch=(((home, width), BF16),),
    )
    arrived = exchange(send)
    cotangent_arrived = exchange(after(cotangent_send, arrived))
    send, *stored_one = owner(1, arrived, pos_slots)
    mixed_arrived = exchange(after(send, cotangent_arrived))
    send, *grads_one = call(
        "last_owner_back",
        22,
        functools.partial(owner_back_kernel, True, None),
        (
            arrival_shape,
            ((width, 3 * width), F32, True),
            ((width, width), F32, True),
            ((width, FF), F32, True),
            ((FF, width), F32, True),
            ((8, width), F32, True),
        ),
        recv[1],
        heads,
        unfold,
        params[1],
        cotangent_arrived,
        recv_col[1],
        *stored_one,
        scratch=(
            slots_wide,
            slots_low,
            slots_low,
            slots_wide,
            *back_scratch,
            slots_low,
            *kept_one,
            recv_col_shape,
        ),
        far_in=3,
        sems=((2, NSUB), (1,)),
        vmem=40,
    )
    arrived = exchange(after(send, mixed_arrived))
    (mixed,) = call(
        "take", 2, take_kernel, (((home, width), BF16),), route_col[1], mixed_arrived
    )
    dresid, send, *ffn_zero = call(
        "home_back",
        10,
        home_backward_kernel,
        (
            ((home, width), F32, True),
            arrival_shape,
            ((width, FF), F32, True),
            ((FF, width), F32, True),
            ((8, width), F32, True),
        ),
        route_col[1],
        route[0],
        arrived,
        resid_zero,
        params[0],
        fresh=(2,),
        scratch=(
            ((home, FF), BF16),
            ((home, width), BF16),
            ((home, width), BF16),
            ((home, FF), BF16),
            ((home, width), BF16),
        ),
    )
    arrived = exchange(send)
    (packed,) = call(
        "pack",
        1,
        functools.partial(pack_kernel, share),
        (((devices, block_rows, 128), BF16, True),),
        *grads_one,
        *ffn_zero,
        scratch=(((flat_rows, 128), F32),),
    )
    early = exchange(after(packed, arrived))
    (send,) = call(
        "first_owner_back",
        16,
        functools.partial(owner_back_kernel, False, (share, quarter_rows)),
        (((devices, capacity + late_rows, width), BF16),),
        recv[0],
        heads,
        unfold,
        params[0],
        arrived,
        recv_col[0],
        *stored_zero,
        fresh=(4,),
        scratch=(
            ((width, 3 * width), F32),
            ((width, width), F32),
            ((late_flat_rows, 128), F32),
            *back_scratch,
            slots_low,
            *kept_zero,
            recv_col_shape,
        ),
        far_in=3,
        sems=((2, NSUB), (1,)),
        vmem=40,
    )
    arrived = exchange(after(send, early))
    early = jnp.sum(early.astype(F32), axis=0)
    late, square = call(
        "late",
        1,
        late_kernel,
        (((late_rows, 128), F32, True), ((devices, 8, 128), F32, True)),
        arrived,
        early,
        fresh=(0,),
    )
    squares = exchange(square)
    (tokens_grad,) = call(
        "finish",
        3,
        finish_kernel,
        (((home, width), F32),),
        route_col[0],
        arrived,
        dresid,
        scratch=(((arrivals, width), BF16),),
    )
    owners = devices // 4
    quarters = [jnp.where(me < owners, late, 0.0)]
    for k in range(1, 4):
        quarters.append(
            lax.ppermute(late, AXES, [(e + k * owners, e) for e in range(owners)])
        )
    late = jnp.concatenate([q[:quarter_rows] for q in quarters], axis=0)[:share_rows]
    shard = (early[:share_rows] + late).reshape(-1)[:share]
    total = jnp.sqrt(jnp.sum(squares[:, 0, 0]))
    clip_limit = 0.25 * math.sqrt(NPARAM)
    factor = jnp.minimum(1.0, clip_limit / (total + 1e-06))
    clipped = shard * factor
    new_first = beta_one * first_moment + (1.0 - beta_one) * clipped
    new_second = beta_two * second_moment + (1.0 - beta_two) * clipped * clipped
    first_hat = new_first / (1.0 - beta_one**adam_step)
    second_hat = new_second / (1.0 - beta_two**adam_step)
    new_master = master - rate * (first_hat / (jnp.sqrt(second_hat) + adam_eps) + decay * master)
    return (
        mixed,
        tokens_grad,
        total.reshape(1),
        clipped,
        new_master,
        new_first,
        new_second,
        new_master.astype(BF16),
    )


def solution(mesh):
    in_specs = (
        P(("grp", "win"), None),
        P(None, ("grp", "win"), None),
        P(("grp", "win"), None),
        P(None, ("grp", "win")),
        P(None, ("grp", "win"), None),
        P(None, ("grp", "win")),
        P(("grp", "win")),
        P(("grp", "win")),
        P(("grp", "win")),
    )
    out_specs = (
        P(("grp", "win"), None),
        P(("grp", "win"), None),
        P(),
        P(("grp", "win")),
        P(("grp", "win")),
        P(("grp", "win")),
        P(("grp", "win")),
        P(("grp", "win")),
    )
    return jax.shard_map(shards, mesh=mesh, in_specs=in_specs, out_specs=out_specs, check_vma=False)
```

```python
import functools
import math

import jax
import jax.numpy as jnp
from jax import lax
from jax.experimental import pallas as pl
from jax.experimental.pallas import tpu as pltpu
from jax.sharding import PartitionSpec as P

PILLAR_WIDTH = 128
FF = 256
HEAD_COUNT = 8
HDIM = 16
WINDOW_SLOTS = 144
LAYERS = 2
DEVICE_SLOTS = 1728
NSUB = 12
NPARAM = 263936
LAYER_ROWS = 1031
EXPANDED = HEAD_COUNT * WINDOW_SLOTS
MASKED = -1e30
LOWEST = -3e38

beta_one = 0.5
beta_two = 0.5
adam_step = 4
rate = 0.1
decay = 0.01
adam_eps = 1e-08

BF16 = jnp.bfloat16
F32 = jnp.float32
AXES = ("grp", "win")

NN = (((1,), (0,)), ((), ()))
NT = (((1,), (1,)), ((), ()))
TN = (((0,), (0,)), ((), ()))


def mm(left, right, dims=NN):
    return lax.dot_general(left, right, dims, preferred_element_type=F32)


def iota(shape, dim):
    return lax.broadcasted_iota(jnp.int32, shape, dim)


def shape_of(shape, dtype):
    return jax.ShapeDtypeStruct(shape, dtype)


def one_hot_rows(row_ids, first, count):
    return jnp.where(iota((count, row_ids.shape[1]), 0) + first == row_ids, 1.0, 0.0).astype(BF16)


def one_hot_columns(column_ids, width):
    lane = iota(column_ids.shape, 1)
    pieces = [
        jnp.where(column_ids == lane + 128 * k, 1.0, 0.0).astype(BF16)
        for k in range(-(-width // 128))
    ]
    return jnp.concatenate(pieces, axis=1)[:, :width]


def expand_heads(block, heads):
    main = block[:128]
    tail = block[128:]
    return jnp.concatenate([main] * HEAD_COUNT + [tail] * HEAD_COUNT, axis=0) * heads


def scatter_rows(route_row, low_rows, send, chunk=256):
    for c in range(send.shape[0] // chunk):
        hot = one_hot_rows(route_row, c * chunk, chunk)
        send[c * chunk : (c + 1) * chunk, :] = mm(hot, low_rows).astype(BF16)


def land_rows(recv_col, slot_values, send, chunk=128):
    for c in range(send.shape[0] // chunk):
        part = slice(c * chunk, (c + 1) * chunk)
        hot = one_hot_columns(recv_col[part, :], DEVICE_SLOTS)
        send[part, :] = mm(hot, slot_values).astype(BF16)


def on_lanes(row, out_type):
    here = iota((128, 128), 0) == iota((128, 128), 1)
    spread = jnp.where(here, jnp.broadcast_to(row, (128, 128)), 0)
    ones = jnp.ones((128, 128), BF16)
    if out_type == BF16:
        return mm(spread.astype(F32).astype(BF16), ones).astype(BF16)
    high = mm((spread >> 6).astype(F32).astype(BF16), ones)
    low = mm((spread & 63).astype(F32).astype(BF16), ones)
    return (high * 64.0 + low).astype(out_type)


def tables_kernel(route_ref, recv_ref, bucket_ref, heads_ref, unfold_ref, *outs):
    slot = iota((EXPANDED, 128), 0)
    head = jnp.where(slot < 1024, slot >> 7, (slot - 1024) >> 4)
    heads_ref[...] = jnp.where(head == iota((EXPANDED, 128), 1) >> 4, 1.0, 0.0).astype(BF16)
    wide = iota((WINDOW_SLOTS, 256), 1)
    wide = jnp.where(wide < 128, wide, 128 + (wide & 15))
    unfold_ref[...] = jnp.where(iota((WINDOW_SLOTS, 256), 0) == wide, 1.0, 0.0).astype(BF16)
    for layer in range(LAYERS):
        route_col_ref, recv_col_ref, bucket_col_ref, bucket_row_ref = outs[4 * layer : 4 * layer + 4]
        bucket = bucket_ref[layer : layer + 1, :]
        for ids, out_ref in (
            (route_ref[layer : layer + 1, :], route_col_ref),
            (recv_ref[layer], recv_col_ref),
            (jnp.concatenate([bucket, bucket[:, :64]], axis=1), bucket_col_ref),
        ):
            for c in range(out_ref.shape[0] // 128):
                part = slice(c * 128, (c + 1) * 128)
                out_ref[part, :] = on_lanes(ids[:, part], out_ref.dtype)
        bucket = bucket.astype(F32)
        for run in range(NSUB):
            base = run * WINDOW_SLOTS
            tail = bucket[:, base + 128 : base + 144]
            bucket_row_ref[run] = jnp.concatenate(
                [bucket[:, base : base + 128], jnp.concatenate([tail] * 8, axis=1)], axis=0
            )


def start_kernel(route_ref, tokens_ref, pos_ref, out_ref):
    both = jnp.concatenate([tokens_ref[...], pos_ref[0]], axis=1)
    scatter_rows(route_ref[0:1, :], both, out_ref)


def start_next_kernel(route_ref, pos_ref, cotangent_ref, pos_out_ref, cotangent_out_ref):
    both = jnp.concatenate([pos_ref[1], cotangent_ref[...]], axis=1)
    for c in range(pos_out_ref.shape[0] // 256):
        part = slice(c * 256, (c + 1) * 256)
        sent = mm(one_hot_rows(route_ref[1:2, :], c * 256, 256), both).astype(BF16)
        pos_out_ref[part, :] = sent[:, :128]
        cotangent_out_ref[part, :] = sent[:, 128:]


def slots_kernel(recv_ref, rows_ref, out_ref):
    for run in range(NSUB):
        part = slice(run * WINDOW_SLOTS, (run + 1) * WINDOW_SLOTS)
        hot = one_hot_rows(recv_ref[1], run * WINDOW_SLOTS, WINDOW_SLOTS)
        out_ref[part, :] = mm(hot, rows_ref[...]).astype(BF16)


def project_in(weights_ref):
    return jnp.concatenate([weights_ref[128 * j : 128 * j + 128, :] for j in range(3)], axis=1)


def project_out(weights_ref):
    return weights_ref[384:512, :]


def feed_weights(weights_ref):
    expand = jnp.concatenate([weights_ref[512:640, :], weights_ref[640:768, :]], axis=1)
    return expand, weights_ref[768:1024, :], weights_ref[1024:1040, :].astype(F32)


def interleave(count, make, ahead=()):
    waiting = [make(i) for i in range(count)]
    running = []
    turn = 0
    while waiting or running:
        for when, act in ahead:
            if when == turn:
                act()
        if waiting:
            running.insert(0, waiting.pop(0))
        running = [part for part in running if next(part, running) is not running]
        turn += 1
    for when, act in ahead:
        if when >= turn:
            act()


def run_rows(run):
    return pl.ds(run * WINDOW_SLOTS, WINDOW_SLOTS)


STORE_BOUNDS = tuple(range(NSUB + 1))
LOAD_BOUNDS = (0, 1, 4, 8, 12)


def kept_copy(k, group, far, near, sems, out):
    first, last = (STORE_BOUNDS if out else LOAD_BOUNDS)[group : group + 2]
    here = pl.ds(first * WINDOW_SLOTS, (last - first) * WINDOW_SLOTS)
    far, near = far.at[here, :], near.at[here, :]
    ends = (near, far) if out else (far, near)
    return pltpu.make_async_copy(*ends, sems.at[k, group])


def attend_stages(run, slot_rows, joined, bucket, bucket_row, heads_ref, weights_ref, low, full):
    win = project_in(weights_ref)
    query_key = mm(joined, win[:, :256])
    queries = (query_key[:, :128] * 0.25).astype(BF16)
    keys = query_key[:, 128:].astype(BF16)
    values = mm(slot_rows, win[:, 256:]).astype(BF16)
    heads = heads_ref[...]
    block = heads[1024:]
    spread = jnp.concatenate(
        [
            queries * jnp.concatenate([heads[128 * h : 128 * h + 16]] * 9, axis=0)
            for h in range(HEAD_COUNT)
        ],
        axis=0,
    )
    yield
    scores = mm(spread, keys[:128], NT)
    tail = mm(queries, jnp.concatenate([keys[128:]] * 8, axis=0) * block, NT)
    yield

    def same(row):
        return jnp.where((bucket == row) & (row >= 0), 0.0, MASKED)

    main_bias = same(bucket_row[0:1, :])
    tail = tail + same(bucket_row[1:2, :])
    segment = iota((WINDOW_SLOTS, 128), 1) >> 4
    tail_top = jnp.zeros((WINDOW_SLOTS, 128), F32)
    pieces = []
    for h in range(HEAD_COUNT):
        main = scores[WINDOW_SLOTS * h : WINDOW_SLOTS * (h + 1)] + main_bias
        own_tail = segment == h
        top = jnp.max(jnp.maximum(main, jnp.where(own_tail, tail, LOWEST)), axis=1, keepdims=True)
        tail_top = jnp.where(own_tail, top, tail_top)
        pieces.append(jnp.exp(main - top).astype(BF16))
    pieces.append(jnp.exp(tail - tail_top).astype(BF16))
    expo = jnp.concatenate(pieces, axis=1)
    low(jnp.concatenate([joined, slot_rows, queries, keys, values, expo], axis=1))
    yield
    summed = mm(expo, jnp.concatenate([expand_heads(values, heads), heads], axis=1))
    yield
    share = jnp.where(bucket >= 0, 1.0, 0.0) / summed[:, 128:]
    attended = summed[:, :128] * share
    full(jnp.concatenate([attended, share], axis=1))
    return mm(attended.astype(BF16), project_out(weights_ref)).astype(BF16)


def attend_back_stages(
    run, dbranch, heads_ref, unfold_ref, weights_ref, low_ref, full_ref, scratch
):
    attended_ref, dbranch_ref, dqkv_ref = scratch
    here = run_rows(run)
    dbranch_ref[here, :] = dbranch
    dattended = mm(dbranch, project_out(weights_ref), NT).astype(BF16).astype(F32)
    yield
    heads = heads_ref[...]
    block = heads[1024:]
    out = full_ref[here, 0:128]
    attended_ref[here, :] = out.astype(BF16)
    dout = (dattended * full_ref[here, 128:256]).astype(BF16)
    weighed = dout.astype(F32) * out
    weighed_high = weighed.astype(BF16)
    weighed_low = (weighed - weighed_high.astype(F32)).astype(BF16)
    centre = mm(weighed_high, block) + mm(weighed_low, block)
    queries = low_ref[here, 256:384]
    keys_wide = expand_heads(low_ref[here, 384:512], heads)
    dprob = mm(dout, expand_heads(low_ref[here, 512:640], heads), NT)
    yield
    expo = low_ref[here, 640:]
    pieces = [
        (
            (dprob[:, 128 * h : 128 * h + 128] - centre[:, 16 * h : 16 * h + 1])
            * expo[:, 128 * h : 128 * h + 128].astype(F32)
        ).astype(BF16)
        for h in range(HEAD_COUNT)
    ]
    pieces.append(((dprob[:, 1024:] - centre) * expo[:, 1024:].astype(F32)).astype(BF16))
    dscore = jnp.concatenate(pieces, axis=1)
    yield
    dqueries = (mm(dscore, keys_wide) * 0.25).astype(BF16)

    def gathered(left, right):
        wide = mm(left, right, TN)
        main = jnp.concatenate(
            [wide[16 * h : 16 * h + 16, 128 * h : 128 * h + 128] for h in range(HEAD_COUNT)],
            axis=0,
        )
        return jnp.concatenate([main, wide[:, 1024:] * block.astype(F32)], axis=1).astype(BF16)

    folded = jnp.concatenate([gathered(queries, dscore), gathered(dout, expo)], axis=0)
    yield
    dkeys_values = mm(unfold_ref[...], folded, NT).astype(BF16)
    dqkv = jnp.concatenate([dqueries, dkeys_values], axis=1)
    dqkv_ref[here, :] = dqkv
    yield
    return mm(dqkv, project_in(weights_ref), NT).astype(BF16)


def projection_grads(low_ref, scratch, dwin_ref, dwout_ref):
    attended_ref, dbranch_ref, dqkv_ref = scratch
    dwout_ref[...] = mm(attended_ref[...], dbranch_ref[...], TN)
    dqkv = dqkv_ref[...]
    dwin_ref[:, :256] = mm(low_ref[:, 0:128], dqkv[:, :256], TN)
    dwin_ref[:, 256:] = mm(low_ref[:, 128:256], dqkv[:, 256:], TN)


def owner_kernel(
    last,
    recv_ref,
    bucket_ref,
    bucket_row_ref,
    heads_ref,
    weights_ref,
    rows_ref,
    *rest,
):
    if last:
        pos_ref, *rest = rest
    (
        recv_col_far,
        send_ref,
        low_far,
        full_far,
        leave_ref,
        low_ref,
        full_ref,
        recv_col_ref,
        sems,
        recv_sem,
    ) = rest
    recv_copy = pltpu.make_async_copy(recv_col_far, recv_col_ref, recv_sem.at[0])
    recv_copy.start()

    def one_run(run):
        here = run_rows(run)

        def low(rows):
            low_ref[here, :] = rows

        def full(rows):
            full_ref[here, 0:256] = rows

        landed = mm(one_hot_rows(recv_ref[1 if last else 0], run * WINDOW_SLOTS, WINDOW_SLOTS), rows_ref[...])
        state = landed[:, :128]
        pos = pos_ref[here, :].astype(F32) if last else landed[:, 128:]
        yield
        branch = yield from attend_stages(
            run,
            state.astype(BF16),
            (state + pos).astype(BF16),
            bucket_ref[here, :].astype(F32),
            bucket_row_ref[run],
            heads_ref,
            weights_ref,
            low,
            full,
        )
        if not last:
            leave_ref[here, :] = branch
            return
        yield
        resid = state + branch.astype(F32)
        full_ref[here, 256:384] = resid
        expand, contract, vecs = feed_weights(weights_ref)
        second = (yield from feed_forward(resid, expand, contract, vecs))[-1]
        yield
        unit, _ = centred_rows(second)
        leave_ref[here, :] = (unit * vecs[5:6, :] + vecs[6:7, :]).astype(BF16)

    low_copies = [kept_copy(0, g, low_far, low_ref, sems, True) for g in range(len(STORE_BOUNDS) - 1)]
    full_copies = [kept_copy(1, g, full_far, full_ref, sems, True) for g in range(len(STORE_BOUNDS) - 1)]
    ahead = [(STORE_BOUNDS[g + 1] + 3, copy.start) for g, copy in enumerate(low_copies)]
    ahead += [(STORE_BOUNDS[g + 1] + 6, copy.start) for g, copy in enumerate(full_copies)]
    interleave(NSUB, one_run, ahead)
    recv_copy.wait()
    land_rows(recv_col_ref, leave_ref[...], send_ref)
    for copy in low_copies + full_copies:
        copy.wait()


def owner_back_kernel(
    last,
    late,
    recv_ref,
    heads_ref,
    unfold_ref,
    weights_ref,
    grads_ref,
    recv_col_far,
    low_far,
    full_far,
    send_ref,
    *rest,
):
    if last:
        dwin_ref, dwout_ref, dexpand_ref, dcontract_ref, dvecs_ref, *rest = rest
        active_ref, douter_ref, first_ref, dinner_ref, *rest = rest
        ffn_refs = (active_ref, douter_ref, first_ref, dinner_ref)
    else:
        dwin_ref, dwout_ref, flat_ref, *rest = rest
    (
        attended_ref,
        dbranch_ref,
        dqkv_ref,
        drows_ref,
        low_ref,
        full_ref,
        recv_col_ref,
        sems,
        recv_sem,
    ) = rest
    scratch = (attended_ref, dbranch_ref, dqkv_ref)
    ahead = []
    for g in range(len(LOAD_BOUNDS) - 1):
        for k, far, near in ((1, full_far, full_ref), (0, low_far, low_ref)):
            copy = kept_copy(k, g, far, near, sems, False)
            copy.start()
            ahead.append((LOAD_BOUNDS[g] + 1, copy.wait))
    recv_copy = pltpu.make_async_copy(recv_col_far, recv_col_ref, recv_sem.at[0])
    recv_copy.start()
    dvecs = []

    def one_run(run):
        here = run_rows(run)

        grad = mm(one_hot_rows(recv_ref[1 if last else 0], run * WINDOW_SLOTS, WINDOW_SLOTS), grads_ref[...])
        yield
        if last:
            dresid = yield from feed_back(
                here, full_ref[here, 256:384], grad, weights_ref, ffn_refs, dvecs
            )
            dbranch = dresid.astype(BF16)
        else:
            dbranch = grad.astype(BF16)

        drows = yield from attend_back_stages(
            run, dbranch, heads_ref, unfold_ref, weights_ref, low_ref, full_ref, scratch
        )
        if last:
            drows = (dresid + drows.astype(F32)).astype(BF16)
        drows_ref[here, :] = drows

    interleave(NSUB, one_run, ahead)
    recv_copy.wait()
    drows = drows_ref[...]
    if last:
        dvecs_ref[...] = sum(dvecs)
        land_rows(recv_col_ref, drows, send_ref)
        projection_grads(low_ref, scratch, dwin_ref, dwout_ref)
        dcontract_ref[...] = mm(active_ref[...], douter_ref[...], TN)
        dexpand_ref[...] = mm(first_ref[...], dinner_ref[...], TN)
        return
    projection_grads(low_ref, scratch, dwin_ref, dwout_ref)
    devices, rows, _ = send_ref.shape
    capacity = recv_col_ref.shape[0] // devices
    for c in range(recv_col_ref.shape[0] // 128):
        hot = one_hot_columns(recv_col_ref[c * 128 : c * 128 + 128, :], DEVICE_SLOTS)
        sent = mm(hot, drows).astype(BF16)
        for part in range(128 // capacity):
            send_ref[c * 128 // capacity + part, 0:capacity, :] = sent[
                part * capacity : part * capacity + capacity
            ]
    share, quarter_rows = late
    store_projections(flat_ref, 0, dwin_ref, dwout_ref)
    flat_ref[pl.ds(512, flat_ref.shape[0] - 512), :] = jnp.zeros(
        (flat_ref.shape[0] - 512, 128), F32
    )
    owners = devices // 4
    for device in range(devices):
        quarter, owner = divmod(device, owners)
        block = share_block(
            flat_ref, owner * share, share, quarter * quarter_rows, rows - capacity, quarter_rows
        )
        send_ref[device, capacity:rows, :] = block.astype(BF16)


def share_block(flat_ref, start, share, first_row, rows, used_rows):
    row, shift = divmod(start, 128)
    row = row + first_row
    lane = iota((rows, 128), 1)
    line = iota((rows, 128), 0)
    block = flat_ref[pl.ds(row, rows), :]
    if shift:
        after = flat_ref[pl.ds(row + 1, rows), :]
        block = pltpu.roll(jnp.where(lane >= shift, block, after), 128 - shift, 1)
    inside = (line < used_rows) & ((line + first_row) * 128 + lane < share)
    return jnp.where(inside, block, 0.0)


def store_projections(flat_ref, base, dwin_ref, dwout_ref):
    for j in range(3):
        flat_ref[pl.ds(base + j, 128, stride=3), :] = dwin_ref[:, 128 * j : 128 * j + 128]
    flat_ref[pl.ds(base + 384, 128), :] = dwout_ref[...]


def centred_rows(rows):
    centre = rows - jnp.mean(rows, axis=-1, keepdims=True)
    spread = jnp.mean(centre * centre, axis=-1, keepdims=True)
    inverse = lax.rsqrt(spread + 1e-05)
    return centre * inverse, inverse


def norm_back(grad, gain, unit, inverse):
    dunit = grad * gain
    return (
        dunit
        - jnp.mean(dunit, axis=-1, keepdims=True)
        - unit * jnp.mean(dunit * unit, axis=-1, keepdims=True)
    ) * inverse


def feed_forward(resid, expand, contract, vecs):
    unit, inverse = centred_rows(resid)
    first = unit * vecs[3:4, :] + vecs[4:5, :]
    first_low = first.astype(BF16)
    bias = jnp.concatenate([vecs[0:1, :], vecs[1:2, :]], axis=1)
    inner = mm(first_low, expand) + bias
    yield
    below = 0.5 + 0.5 * lax.erf(inner * math.sqrt(0.5))
    active = (inner * below).astype(BF16)
    second = first + (mm(active, contract) + vecs[2:3, :])
    return unit, inverse, first_low, inner, below, active, second


def feed_back(here, resid, grad, weights_ref, ffn_refs, dvecs):
    active_ref, douter_ref, first_ref, dinner_ref = ffn_refs
    expand, contract, vecs = feed_weights(weights_ref)
    unit_first, inverse_first, first_low, inner, below, active, second = yield from feed_forward(
        resid, expand, contract, vecs
    )
    active_ref[here, :] = active
    first_ref[here, :] = first_low
    yield
    unit, inverse = centred_rows(second)
    dsecond = norm_back(grad, vecs[5:6, :], unit, inverse)
    douter = dsecond.astype(BF16)
    douter_ref[here, :] = douter
    dactive = mm(douter, contract, NT)
    slope = below + inner * (jnp.exp(-0.5 * inner * inner) * (1.0 / math.sqrt(2.0 * math.pi)))
    yield
    dinner = (dactive * slope).astype(BF16)
    dinner_ref[here, :] = dinner
    dfirst = mm(dinner, expand, NT) + dsecond
    yield

    def down(rows):
        return jnp.sum(rows, axis=0, keepdims=True)

    dbias = down(dinner.astype(F32))
    dvecs.append(
        jnp.concatenate(
            [
                dbias[:, :128],
                dbias[:, 128:],
                down(douter.astype(F32)),
                down(dfirst * unit_first),
                down(dfirst),
                down(grad * unit),
                down(grad),
                jnp.zeros((1, 128), F32),
            ],
            axis=0,
        )
    )
    return norm_back(dfirst, vecs[3:4, :], unit_first, inverse_first)


ROWS = 128


def part_rows(part):
    return pl.ds(part * ROWS, ROWS)


def home_forward_kernel(
    route_col_ref,
    route_ref,
    branch_ref,
    state_ref,
    weights_ref,
    send_ref,
    resid_ref,
    result_ref,
):
    def some_rows(part):
        here = part_rows(part)
        expand, contract, vecs = feed_weights(weights_ref)
        hot = one_hot_columns(route_col_ref[here, :], branch_ref.shape[0])
        resid = state_ref[here, :].astype(F32) + mm(hot, branch_ref[...])
        yield
        resid_ref[here, :] = resid
        second = (yield from feed_forward(resid, expand, contract, vecs))[-1]
        yield
        unit, _ = centred_rows(second)
        result_ref[here, :] = (unit * vecs[5:6, :] + vecs[6:7, :]).astype(BF16)

    interleave(result_ref.shape[0] // ROWS, some_rows)
    scatter_rows(route_ref[1:2, :], result_ref[...], send_ref)


def home_backward_kernel(
    route_col_ref,
    route_ref,
    arrived_ref,
    resid_ref,
    weights_ref,
    dresid_ref,
    send_ref,
    dexpand_ref,
    dcontract_ref,
    dvecs_ref,
    active_ref,
    douter_ref,
    first_ref,
    dinner_ref,
    low_ref,
):
    ffn_refs = (active_ref, douter_ref, first_ref, dinner_ref)
    dvecs = []

    def some_rows(part):
        here = part_rows(part)
        hot = one_hot_columns(route_col_ref[here, :], arrived_ref.shape[0])
        grad = mm(hot, arrived_ref[...])
        yield
        dresid = yield from feed_back(
            here, resid_ref[here, :], grad, weights_ref, ffn_refs, dvecs
        )
        dresid_ref[here, :] = dresid
        low_ref[here, :] = dresid.astype(BF16)

    interleave(dresid_ref.shape[0] // ROWS, some_rows)
    dvecs_ref[...] = sum(dvecs)
    scatter_rows(route_ref[0:1, :], low_ref[...], send_ref)
    dcontract_ref[...] = mm(active_ref[...], douter_ref[...], TN)
    dexpand_ref[...] = mm(first_ref[...], dinner_ref[...], TN)


def take_kernel(route_col_ref, arrived_ref, out_ref):
    for part in range(out_ref.shape[0] // ROWS):
        here = part_rows(part)
        hot = one_hot_columns(route_col_ref[here, :], arrived_ref.shape[0])
        out_ref[here, :] = mm(hot, arrived_ref[...]).astype(BF16)


def finish_kernel(route_col_ref, arrived_ref, dresid_ref, out_ref, rows_ref):
    devices, rows, _ = arrived_ref.shape
    capacity = rows_ref.shape[0] // devices
    for device in range(devices):
        rows_ref[device * capacity : (device + 1) * capacity, :] = arrived_ref[
            device, 0:capacity, :
        ]
    for part in range(out_ref.shape[0] // ROWS):
        here = part_rows(part)
        hot = one_hot_columns(route_col_ref[here, :], rows_ref.shape[0])
        out_ref[here, :] = dresid_ref[here, :] + mm(hot, rows_ref[...])


def late_kernel(quarter_rows, arrived_ref, early_ref, late_ref):
    devices, rows, _ = arrived_ref.shape
    capacity = rows - late_ref.shape[0]
    late = arrived_ref[0, capacity:rows, :].astype(F32)
    for device in range(1, devices):
        late = late + arrived_ref[device, capacity:rows, :].astype(F32)
    early = early_ref[...]
    square = jnp.sum(early * early) + jnp.sum(late * late)
    late_ref[...] = jnp.where(iota(late.shape, 0) < quarter_rows, late, square)


def unpack_kernel(share, me_ref, shards_ref, *rest):
    flat_ref = rest[-1]
    outs = rest[:-1]
    devices, block_rows, _ = shards_ref.shape
    lane = iota((block_rows, 128), 1)
    me = me_ref[0]
    for device in range(devices):
        row, shift = divmod(device * share, 128)
        block = shards_ref[me ^ device].astype(F32)
        if shift:
            block = pltpu.roll(block, shift, 1)
            before = jnp.concatenate([flat_ref[pl.ds(row, 1), :], block[:-1]], axis=0)
            block = jnp.where(lane >= shift, block, before)
        flat_ref[pl.ds(row, block_rows), :] = block
    for layer, out_ref in enumerate(outs):
        base = layer * LAYER_ROWS
        for j in range(3):
            out_ref[128 * j : 128 * j + 128, :] = flat_ref[pl.ds(base + j, 128, stride=3), :].astype(
                BF16
            )
        out_ref[384:512, :] = flat_ref[pl.ds(base + 384, 128), :].astype(BF16)
        for j in range(2):
            out_ref[512 + 128 * j : 640 + 128 * j, :] = flat_ref[
                pl.ds(base + 512 + j, 128, stride=2), :
            ].astype(BF16)
        out_ref[768:1024, :] = flat_ref[pl.ds(base + 768, 256), :].astype(BF16)
        vecs = flat_ref[pl.ds(base + 1024, 16), :]
        out_ref[1024:1040, :] = jnp.where(iota((16, 128), 0) < 7, vecs, 0.0).astype(BF16)


def pack_kernel(
    share,
    dwin_ref,
    dwout_ref,
    dexpand_ref,
    dcontract_ref,
    dvecs_ref,
    dexpand_zero_ref,
    dcontract_zero_ref,
    dvecs_zero_ref,
    out_ref,
    flat_ref,
):
    devices, block_rows, _ = out_ref.shape
    flat_ref[0:512, :] = jnp.zeros((512, 128), F32)
    store_projections(flat_ref, LAYER_ROWS, dwin_ref, dwout_ref)
    for base, expand, contract, vecs in (
        (0, dexpand_zero_ref, dcontract_zero_ref, dvecs_zero_ref),
        (LAYER_ROWS, dexpand_ref, dcontract_ref, dvecs_ref),
    ):
        for j in range(2):
            flat_ref[pl.ds(base + 512 + j, 128, stride=2), :] = expand[:, 128 * j : 128 * j + 128]
        flat_ref[pl.ds(base + 768, 256), :] = contract[...]
        flat_ref[pl.ds(base + 1024, 7), :] = vecs[0:7, :]
    end = LAYERS * LAYER_ROWS
    flat_ref[pl.ds(end, flat_ref.shape[0] - end), :] = jnp.zeros(
        (flat_ref.shape[0] - end, 128), F32
    )
    for device in range(devices):
        block = share_block(flat_ref, device * share, share, 0, block_rows, block_rows)
        out_ref[device] = block.astype(BF16)


def call(
    name,
    micros,
    body,
    outs,
    *args,
    fresh=(),
    scratch=(),
    vmem=24,
    smem=0,
    far_in=0,
    far_out=0,
    sems=(),
):
    near = pl.BlockSpec(memory_space=pltpu.VMEM)
    far = pl.BlockSpec(memory_space=pltpu.HBM)
    specs = [pl.BlockSpec(memory_space=pltpu.SMEM)] * smem
    specs += [near] * (len(args) - smem - far_in) + [far] * far_in
    args = [
        x if i < smem or i in fresh else pltpu.with_memory_space_constraint(x, pltpu.HBM)
        for i, x in enumerate(args)
    ]
    return pl.pallas_call(
        body,
        out_shape=tuple(
            shape_of(o[0], o[1]) if len(o) == 2 else pltpu.HBM(o[0], o[1]) for o in outs
        ),
        in_specs=specs,
        out_specs=tuple([near] * (len(outs) - far_out) + [far] * far_out),
        scratch_shapes=[pltpu.VMEM(s[0], s[1]) for s in scratch]
        + [pltpu.SemaphoreType.DMA(s) for s in sems],
        compiler_params=pltpu.CompilerParams(vmem_limit_bytes=vmem << 20),
        cost_estimate=pl.CostEstimate(
            flops=int(micros * 1e9), bytes_accessed=1 << 16, transcendentals=0
        ),
        name=name,
    )(*args)


def exchange(buffer):
    return lax.all_to_all(buffer, AXES, split_axis=0, concat_axis=0, tiled=True)


def swapped(value, pair, devices):
    steps = [pair[-1], pair[0], pair[0] ^ pair[-1]][: 2 * len(pair) - 1]
    return [lax.ppermute(value, AXES, [(i, i ^ step) for i in range(devices)]) for step in steps]


def paired(parts):
    while len(parts) > 1:
        parts = [parts[i] + parts[i + 1] for i in range(0, len(parts), 2)]
    return parts[0]


def after(value, *others):
    return lax.optimization_barrier((value, *others))[0]


def shards(
    tokens,
    positions,
    cotangent,
    route_send,
    recv_slot,
    slot_bucket,
    master,
    first_moment,
    second_moment,
):
    devices = lax.axis_size("grp") * lax.axis_size("win")
    me = lax.axis_index(AXES)
    home = tokens.shape[0]
    arrivals = recv_slot.shape[2]
    share = master.shape[0]
    share_rows = -(-share // 128)
    block_rows = -(-share_rows // 8) * 8
    quarter_rows = -(-share_rows // 4)
    late_rows = -(-(quarter_rows + 1) // 8) * 8
    capacity = arrivals // devices
    width = PILLAR_WIDTH
    flat_rows = -(-(((devices - 1) * share) // 128 + block_rows + 8) // 8) * 8
    late_flat_rows = -(-max(520, ((devices // 4) * share) // 128 + late_rows + 16) // 8) * 8

    heads, unfold, *tables = call(
        "tables",
        4,
        tables_kernel,
        (((EXPANDED, 128), BF16, True), ((WINDOW_SLOTS, 256), BF16, True))
        + (
            ((home, 128), jnp.int32, True),
            ((arrivals, 128), jnp.int32, True),
            ((DEVICE_SLOTS + 64, 128), BF16, True),
            ((NSUB, 2, 128), F32, True),
        )
        * LAYERS,
        route_send,
        recv_slot,
        slot_bucket,
    )
    route_col, recv_col, bucket, bucket_row = (tables[k::4] for k in range(4))
    (send,) = call(
        "start",
        3,
        start_kernel,
        (((arrivals, 2 * width), BF16),),
        route_send,
        tokens,
        positions,
    )
    pos_send, cotangent_send = call(
        "start_next",
        3,
        start_next_kernel,
        (((arrivals, width), BF16, True), ((arrivals, width), BF16, True)),
        route_send,
        positions,
        cotangent,
    )

    copies = jnp.pad(master.astype(BF16), (0, block_rows * 128 - share)).reshape(1, block_rows, 128)
    bits = [devices >> (i + 1) for i in range(devices.bit_length() - 1)]
    for i in range(0, len(bits), 2):
        copies = jnp.stack([copies, *swapped(copies, bits[i : i + 2], devices)], axis=1)
        copies = copies.reshape(-1, block_rows, 128)
        if copies.shape[0] == 4:
            arrived = exchange(after(send, copies))
    params = call(
        "unpack",
        2,
        functools.partial(unpack_kernel, share),
        (((1040, width), BF16, True),) * LAYERS,
        me.reshape(1),
        copies,
        scratch=(((flat_rows, 128), F32),),
        smem=1,
    )
    kept_zero = (
        ((DEVICE_SLOTS, 640 + EXPANDED), BF16, True),
        ((DEVICE_SLOTS, 2 * width), F32, True),
    )
    kept_one = (kept_zero[0], ((DEVICE_SLOTS, 3 * width), F32, True))
    recv_col_shape = ((arrivals, 128), jnp.int32)
    slots_low = ((DEVICE_SLOTS, width), BF16)
    slots_wide = ((DEVICE_SLOTS, FF), BF16)
    back_scratch = (slots_low, slots_low, ((DEVICE_SLOTS, 3 * width), BF16))
    arrival_shape = ((arrivals, width), BF16)

    pos_arrived = exchange(after(pos_send, arrived))
    def owner(layer, rows, *pos):
        kept = (kept_zero, kept_one)[layer]
        return call(
            ("first_owner", "last_owner")[layer],
            (13, 18)[layer],
            functools.partial(owner_kernel, layer == 1),
            (arrival_shape, *kept),
            recv_slot,
            bucket[layer],
            bucket_row[layer],
            heads,
            params[layer],
            rows,
            *pos,
            recv_col[layer],
            fresh=(5,),
            scratch=(slots_low, *kept, recv_col_shape),
            far_in=1,
            far_out=2,
            sems=((2, len(STORE_BOUNDS) - 1), (1,)),
            vmem=40,
        )

    send, *stored_zero = owner(0, arrived)
    branch = exchange(after(send, pos_arrived))
    (pos_slots,) = call(
        "slots", 4, slots_kernel, ((*slots_low, True),), recv_slot, pos_arrived
    )
    send, resid_zero = call(
        "home",
        8,
        home_forward_kernel,
        (arrival_shape, ((home, width), F32, True)),
        route_col[0],
        route_send,
        branch,
        tokens,
        params[0],
        fresh=(2,),
        scratch=(((home, width), BF16),),
    )
    arrived = exchange(send)
    cotangent_arrived = exchange(after(cotangent_send, arrived))
    send, *stored_one = owner(1, arrived, pos_slots)
    mixed_arrived = exchange(after(send, cotangent_arrived))
    send, *grads_one = call(
        "last_owner_back",
        22,
        functools.partial(owner_back_kernel, True, None),
        (
            arrival_shape,
            ((width, 3 * width), F32, True),
            ((width, width), F32, True),
            ((width, FF), F32, True),
            ((FF, width), F32, True),
            ((8, width), F32, True),
        ),
        recv_slot,
        heads,
        unfold,
        params[1],
        cotangent_arrived,
        recv_col[1],
        *stored_one,
        scratch=(
            slots_wide,
            slots_low,
            slots_low,
            slots_wide,
            *back_scratch,
            slots_low,
            *kept_one,
            recv_col_shape,
        ),
        far_in=3,
        sems=((2, len(LOAD_BOUNDS) - 1), (1,)),
        vmem=40,
    )
    arrived = exchange(after(send, mixed_arrived))
    (mixed,) = call(
        "take", 2, take_kernel, (((home, width), BF16),), route_col[1], mixed_arrived
    )
    dresid, send, *ffn_zero = call(
        "home_back",
        10,
        home_backward_kernel,
        (
            ((home, width), F32, True),
            arrival_shape,
            ((width, FF), F32, True),
            ((FF, width), F32, True),
            ((8, width), F32, True),
        ),
        route_col[1],
        route_send,
        arrived,
        resid_zero,
        params[0],
        fresh=(2,),
        scratch=(
            ((home, FF), BF16),
            ((home, width), BF16),
            ((home, width), BF16),
            ((home, FF), BF16),
            ((home, width), BF16),
        ),
    )
    arrived = exchange(send)
    (packed,) = call(
        "pack",
        1,
        functools.partial(pack_kernel, share),
        (((devices, block_rows, 128), BF16, True),),
        *grads_one,
        *ffn_zero,
        scratch=(((flat_rows, 128), F32),),
    )
    early = exchange(after(packed, arrived))
    (send,) = call(
        "first_owner_back",
        16,
        functools.partial(owner_back_kernel, False, (share, quarter_rows)),
        (((devices, capacity + late_rows, width), BF16),),
        recv_slot,
        heads,
        unfold,
        params[0],
        arrived,
        recv_col[0],
        *stored_zero,
        fresh=(4,),
        scratch=(
            ((width, 3 * width), F32),
            ((width, width), F32),
            ((late_flat_rows, 128), F32),
            *back_scratch,
            slots_low,
            *kept_zero,
            recv_col_shape,
        ),
        far_in=3,
        sems=((2, len(LOAD_BOUNDS) - 1), (1,)),
        vmem=40,
    )
    arrived = exchange(after(send, early))
    early = jnp.sum(early.astype(F32), axis=0)
    (late,) = call(
        "late",
        1,
        functools.partial(late_kernel, quarter_rows),
        (((late_rows, 128), F32, True),),
        arrived,
        after(early, mixed),
        fresh=(0,),
    )
    (tokens_grad,) = call(
        "finish",
        3,
        finish_kernel,
        (((home, width), F32),),
        route_col[0],
        arrived,
        dresid,
        scratch=(((arrivals, width), BF16),),
    )
    quarters = [late, *swapped(late, bits[:2], devices)]
    square = after(paired([q[quarter_rows:] for q in quarters]), tokens_grad)
    for i in range(2, len(bits), 2):
        square = paired([square, *swapped(square, bits[i : i + 2], devices)])
    total = jnp.sqrt(square[0, 0])
    late = jnp.concatenate([q[:quarter_rows] for q in quarters], axis=0)[:share_rows]
    late = jnp.where(me < devices // 4, late, 0.0)
    shard = (early[:share_rows] + late).reshape(-1)[:share]
    clip_limit = 0.25 * math.sqrt(NPARAM)
    factor = jnp.minimum(1.0, clip_limit / (total + 1e-06))
    clipped = shard * factor
    new_first = beta_one * first_moment + (1.0 - beta_one) * clipped
    new_second = beta_two * second_moment + (1.0 - beta_two) * clipped * clipped
    first_hat = new_first / (1.0 - beta_one**adam_step)
    second_hat = new_second / (1.0 - beta_two**adam_step)
    new_master = master - rate * (first_hat / (jnp.sqrt(second_hat) + adam_eps) + decay * master)
    return (
        mixed,
        tokens_grad,
        total.reshape(1),
        clipped,
        new_master,
        new_first,
        new_second,
        new_master.astype(BF16),
    )


def solution(mesh):
    in_specs = (
        P(("grp", "win"), None),
        P(None, ("grp", "win"), None),
        P(("grp", "win"), None),
        P(None, ("grp", "win")),
        P(None, ("grp", "win"), None),
        P(None, ("grp", "win")),
        P(("grp", "win")),
        P(("grp", "win")),
        P(("grp", "win")),
    )
    out_specs = (
        P(("grp", "win"), None),
        P(("grp", "win"), None),
        P(),
        P(("grp", "win")),
        P(("grp", "win")),
        P(("grp", "win")),
        P(("grp", "win")),
        P(("grp", "win")),
    )
    return jax.shard_map(shards, mesh=mesh, in_specs=in_specs, out_specs=out_specs, check_vma=False)
```

```python
import functools
import math

import jax
import jax.numpy as jnp
from jax import lax
from jax.experimental import pallas as pl
from jax.experimental.pallas import tpu as pltpu
from jax.sharding import PartitionSpec as P

PILLAR_WIDTH = 128
FF = 256
HEAD_COUNT = 8
HDIM = 16
WINDOW_SLOTS = 144
LAYERS = 2
DEVICE_SLOTS = 1728
NSUB = 12
NPARAM = 263936
LAYER_ROWS = 1031
EXPANDED = HEAD_COUNT * WINDOW_SLOTS
MASKED = -1e30
LOWEST = -3e38

beta_one = 0.5
beta_two = 0.5
adam_step = 4
rate = 0.1
decay = 0.01
adam_eps = 1e-08

BF16 = jnp.bfloat16
F32 = jnp.float32
AXES = ("grp", "win")

NN = (((1,), (0,)), ((), ()))
NT = (((1,), (1,)), ((), ()))
TN = (((0,), (0,)), ((), ()))


def mm(left, right, dims=NN):
    return lax.dot_general(left, right, dims, preferred_element_type=F32)


def iota(shape, dim):
    return lax.broadcasted_iota(jnp.int32, shape, dim)


def shape_of(shape, dtype):
    return jax.ShapeDtypeStruct(shape, dtype)


def one_hot_rows(row_ids, first, count):
    return jnp.where(iota((count, row_ids.shape[1]), 0) + first == row_ids, 1.0, 0.0).astype(BF16)


def one_hot_columns(column_ids, width):
    lane = iota(column_ids.shape, 1)
    pieces = [
        jnp.where(column_ids == lane + 128 * k, 1.0, 0.0).astype(BF16)
        for k in range(-(-width // 128))
    ]
    return jnp.concatenate(pieces, axis=1)[:, :width]


def expand_heads(block, heads):
    main = block[:128]
    tail = block[128:]
    return jnp.concatenate([main] * HEAD_COUNT + [tail] * HEAD_COUNT, axis=0) * heads


def scatter_rows(route_row, low_rows, send, chunk=256):
    for c in range(send.shape[0] // chunk):
        hot = one_hot_rows(route_row, c * chunk, chunk)
        send[c * chunk : (c + 1) * chunk, :] = mm(hot, low_rows).astype(BF16)


def land_rows(recv_col, slot_values, send, chunk=128):
    for c in range(send.shape[0] // chunk):
        part = slice(c * chunk, (c + 1) * chunk)
        hot = one_hot_columns(recv_col[part, :], DEVICE_SLOTS)
        send[part, :] = mm(hot, slot_values).astype(BF16)


def on_lanes(row, out_type):
    here = iota((128, 128), 0) == iota((128, 128), 1)
    spread = jnp.where(here, jnp.broadcast_to(row, (128, 128)), 0)
    ones = jnp.ones((128, 128), BF16)
    if out_type == BF16:
        return mm(spread.astype(F32).astype(BF16), ones).astype(BF16)
    high = mm((spread >> 6).astype(F32).astype(BF16), ones)
    low = mm((spread & 63).astype(F32).astype(BF16), ones)
    return (high * 64.0 + low).astype(out_type)


def tables_kernel(route_ref, recv_ref, bucket_ref, heads_ref, unfold_ref, *outs):
    slot = iota((EXPANDED, 128), 0)
    head = jnp.where(slot < 1024, slot >> 7, (slot - 1024) >> 4)
    heads_ref[...] = jnp.where(head == iota((EXPANDED, 128), 1) >> 4, 1.0, 0.0).astype(BF16)
    wide = iota((WINDOW_SLOTS, 256), 1)
    wide = jnp.where(wide < 128, wide, 128 + (wide & 15))
    unfold_ref[...] = jnp.where(iota((WINDOW_SLOTS, 256), 0) == wide, 1.0, 0.0).astype(BF16)
    for layer in range(LAYERS):
        route_col_ref, recv_col_ref, bucket_col_ref, bucket_row_ref = outs[4 * layer : 4 * layer + 4]
        bucket = bucket_ref[layer : layer + 1, :]
        for ids, out_ref in (
            (route_ref[layer : layer + 1, :], route_col_ref),
            (recv_ref[layer], recv_col_ref),
            (jnp.concatenate([bucket, bucket[:, :64]], axis=1), bucket_col_ref),
        ):
            for c in range(out_ref.shape[0] // 128):
                part = slice(c * 128, (c + 1) * 128)
                out_ref[part, :] = on_lanes(ids[:, part], out_ref.dtype)
        bucket = bucket.astype(F32)
        for run in range(NSUB):
            base = run * WINDOW_SLOTS
            tail = bucket[:, base + 128 : base + 144]
            bucket_row_ref[run] = jnp.concatenate(
                [bucket[:, base : base + 128], jnp.concatenate([tail] * 8, axis=1)], axis=0
            )


def start_kernel(route_ref, tokens_ref, pos_ref, out_ref):
    both = jnp.concatenate([tokens_ref[...], pos_ref[0]], axis=1)
    scatter_rows(route_ref[0:1, :], both, out_ref)


def start_next_kernel(route_ref, pos_ref, cotangent_ref, pos_out_ref, cotangent_out_ref):
    both = jnp.concatenate([pos_ref[1], cotangent_ref[...]], axis=1)
    for c in range(pos_out_ref.shape[0] // 256):
        part = slice(c * 256, (c + 1) * 256)
        sent = mm(one_hot_rows(route_ref[1:2, :], c * 256, 256), both).astype(BF16)
        pos_out_ref[part, :] = sent[:, :128]
        cotangent_out_ref[part, :] = sent[:, 128:]


def slots_kernel(recv_ref, rows_ref, out_ref):
    for run in range(NSUB):
        part = slice(run * WINDOW_SLOTS, (run + 1) * WINDOW_SLOTS)
        hot = one_hot_rows(recv_ref[1], run * WINDOW_SLOTS, WINDOW_SLOTS)
        out_ref[part, :] = mm(hot, rows_ref[...]).astype(BF16)


def project_in(weights_ref):
    return jnp.concatenate([weights_ref[128 * j : 128 * j + 128, :] for j in range(3)], axis=1)


def project_out(weights_ref):
    return weights_ref[384:512, :]


def feed_weights(weights_ref):
    expand = jnp.concatenate([weights_ref[512:640, :], weights_ref[640:768, :]], axis=1)
    return expand, weights_ref[768:1024, :], weights_ref[1024:1040, :].astype(F32)


def interleave(count, make, ahead=()):
    waiting = [make(i) for i in range(count)]
    running = []
    turn = 0
    while waiting or running:
        for when, act in ahead:
            if when == turn:
                act()
        if waiting:
            running.insert(0, waiting.pop(0))
        running = [part for part in running if next(part, running) is not running]
        turn += 1
    for when, act in ahead:
        if when >= turn:
            act()


def run_rows(run):
    return pl.ds(run * WINDOW_SLOTS, WINDOW_SLOTS)


STORE_BOUNDS = tuple(range(NSUB + 1))
LOAD_BOUNDS = ((0, 4, 12), (0, 3, 7, 12))


def kept_copy(k, group, bounds, far, near, sems, out):
    first, last = bounds[group : group + 2]
    here = pl.ds(first * WINDOW_SLOTS, (last - first) * WINDOW_SLOTS)
    far, near = far.at[here, :], near.at[here, :]
    ends = (near, far) if out else (far, near)
    return pltpu.make_async_copy(*ends, sems.at[k, group])


def attend_stages(run, slot_rows, joined, bucket, bucket_row, heads_ref, weights_ref, low, full):
    win = project_in(weights_ref)
    query_key = mm(joined, win[:, :256])
    queries = (query_key[:, :128] * 0.25).astype(BF16)
    keys = query_key[:, 128:].astype(BF16)
    values = mm(slot_rows, win[:, 256:]).astype(BF16)
    heads = heads_ref[...]
    block = heads[1024:]
    spread = jnp.concatenate(
        [
            queries * jnp.concatenate([heads[128 * h : 128 * h + 16]] * 9, axis=0)
            for h in range(HEAD_COUNT)
        ],
        axis=0,
    )
    yield
    scores = mm(spread, keys[:128], NT)
    tail = mm(queries, jnp.concatenate([keys[128:]] * 8, axis=0) * block, NT)
    yield

    def same(row):
        return jnp.where((bucket == row) & (row >= 0), 0.0, MASKED)

    main_bias = same(bucket_row[0:1, :])
    tail = tail + same(bucket_row[1:2, :])
    segment = iota((WINDOW_SLOTS, 128), 1) >> 4
    tail_top = jnp.zeros((WINDOW_SLOTS, 128), F32)
    pieces = []
    for h in range(HEAD_COUNT):
        main = scores[WINDOW_SLOTS * h : WINDOW_SLOTS * (h + 1)] + main_bias
        own_tail = segment == h
        top = jnp.max(jnp.maximum(main, jnp.where(own_tail, tail, LOWEST)), axis=1, keepdims=True)
        tail_top = jnp.where(own_tail, top, tail_top)
        pieces.append(jnp.exp(main - top).astype(BF16))
    pieces.append(jnp.exp(tail - tail_top).astype(BF16))
    expo = jnp.concatenate(pieces, axis=1)
    low(jnp.concatenate([joined, slot_rows, queries, keys, values, expo], axis=1))
    yield
    summed = mm(expo, jnp.concatenate([expand_heads(values, heads), heads], axis=1))
    yield
    share = jnp.where(bucket >= 0, 1.0, 0.0) / summed[:, 128:]
    attended = summed[:, :128] * share
    full(jnp.concatenate([attended, share], axis=1))
    return mm(attended.astype(BF16), project_out(weights_ref)).astype(BF16)


def attend_back_stages(
    run, dbranch, heads_ref, unfold_ref, weights_ref, low_ref, full_ref, scratch
):
    attended_ref, dbranch_ref, dqkv_ref = scratch
    here = run_rows(run)
    dattended = mm(dbranch, project_out(weights_ref), NT).astype(BF16).astype(F32)
    yield
    heads = heads_ref[...]
    block = heads[1024:]
    out = full_ref[here, 0:128]
    attended_ref[here, :] = out.astype(BF16)
    dout = (dattended * full_ref[here, 128:256]).astype(BF16)
    weighed = dout.astype(F32) * out
    weighed_high = weighed.astype(BF16)
    weighed_low = (weighed - weighed_high.astype(F32)).astype(BF16)
    centre = mm(weighed_high, block) + mm(weighed_low, block)
    queries = low_ref[here, 256:384]
    keys_wide = expand_heads(low_ref[here, 384:512], heads)
    dprob = mm(dout, expand_heads(low_ref[here, 512:640], heads), NT)
    yield
    expo = low_ref[here, 640:]
    pieces = [
        (
            (dprob[:, 128 * h : 128 * h + 128] - centre[:, 16 * h : 16 * h + 1])
            * expo[:, 128 * h : 128 * h + 128].astype(F32)
        ).astype(BF16)
        for h in range(HEAD_COUNT)
    ]
    pieces.append(((dprob[:, 1024:] - centre) * expo[:, 1024:].astype(F32)).astype(BF16))
    dscore = jnp.concatenate(pieces, axis=1)
    yield
    dqueries = (mm(dscore, keys_wide) * 0.25).astype(BF16)

    def gathered(left, right):
        wide = mm(left, right, TN)
        main = jnp.concatenate(
            [wide[16 * h : 16 * h + 16, 128 * h : 128 * h + 128] for h in range(HEAD_COUNT)],
            axis=0,
        )
        return jnp.concatenate([main, wide[:, 1024:] * block.astype(F32)], axis=1).astype(BF16)

    folded = jnp.concatenate([gathered(queries, dscore), gathered(dout, expo)], axis=0)
    yield
    dkeys_values = mm(unfold_ref[...], folded, NT).astype(BF16)
    dqkv = jnp.concatenate([dqueries, dkeys_values], axis=1)
    dqkv_ref[here, :] = dqkv
    yield
    return mm(dqkv, project_in(weights_ref), NT).astype(BF16)


def projection_grads(low_ref, scratch, dwin_ref, dwout_ref):
    attended_ref, dbranch_ref, dqkv_ref = scratch
    dwout_ref[...] = mm(attended_ref[...], dbranch_ref[...], TN)
    dqkv = dqkv_ref[...]
    dwin_ref[:, :256] = mm(low_ref[:, 0:128], dqkv[:, :256], TN)
    dwin_ref[:, 256:] = mm(low_ref[:, 128:256], dqkv[:, 256:], TN)


def owner_kernel(
    last,
    recv_ref,
    bucket_ref,
    bucket_row_ref,
    heads_ref,
    weights_ref,
    rows_ref,
    *rest,
):
    if last:
        pos_ref, *rest = rest
    (
        recv_col_far,
        send_ref,
        low_far,
        full_far,
        leave_ref,
        low_ref,
        full_ref,
        recv_col_ref,
        sems,
        recv_sem,
    ) = rest
    recv_copy = pltpu.make_async_copy(recv_col_far, recv_col_ref, recv_sem.at[0])
    recv_copy.start()

    def one_run(run):
        here = run_rows(run)

        def low(rows):
            low_ref[here, :] = rows

        def full(rows):
            full_ref[here, 0:256] = rows

        landed = mm(one_hot_rows(recv_ref[1 if last else 0], run * WINDOW_SLOTS, WINDOW_SLOTS), rows_ref[...])
        state = landed[:, :128]
        pos = pos_ref[here, :].astype(F32) if last else landed[:, 128:]
        yield
        branch = yield from attend_stages(
            run,
            state.astype(BF16),
            (state + pos).astype(BF16),
            bucket_ref[here, :].astype(F32),
            bucket_row_ref[run],
            heads_ref,
            weights_ref,
            low,
            full,
        )
        if not last:
            leave_ref[here, :] = branch
            return
        yield
        resid = state + branch.astype(F32)
        full_ref[here, 256:384] = resid
        expand, contract, vecs = feed_weights(weights_ref)
        second = (yield from feed_forward(resid, expand, contract, vecs))[-1]
        yield
        unit, _ = centred_rows(second)
        leave_ref[here, :] = (unit * vecs[5:6, :] + vecs[6:7, :]).astype(BF16)

    low_copies = [kept_copy(0, g, STORE_BOUNDS, low_far, low_ref, sems, True) for g in range(len(STORE_BOUNDS) - 1)]
    full_copies = [kept_copy(1, g, STORE_BOUNDS, full_far, full_ref, sems, True) for g in range(len(STORE_BOUNDS) - 1)]
    ahead = [(STORE_BOUNDS[g + 1] + 3, copy.start) for g, copy in enumerate(low_copies)]
    ahead += [(STORE_BOUNDS[g + 1] + 6, copy.start) for g, copy in enumerate(full_copies)]
    interleave(NSUB, one_run, ahead)
    recv_copy.wait()
    land_rows(recv_col_ref, leave_ref[...], send_ref)
    for copy in low_copies + full_copies:
        copy.wait()


def owner_back_kernel(
    last,
    late,
    recv_ref,
    heads_ref,
    unfold_ref,
    weights_ref,
    grads_ref,
    *rest,
):
    if not last:
        dexpand_ref, *rest = rest
    recv_col_far, low_far, full_far, send_ref, *rest = rest
    if last:
        dwin_ref, dwout_ref, dexpand_ref, dcontract_ref, dvecs_ref, *rest = rest
        active_ref, douter_ref, first_ref, dinner_ref, *rest = rest
        ffn_refs = (active_ref, douter_ref, first_ref, dinner_ref)
    else:
        dwin_ref, dwout_ref, flat_ref, *rest = rest
    (
        attended_ref,
        dbranch_ref,
        dqkv_ref,
        drows_ref,
        low_ref,
        full_ref,
        recv_col_ref,
        sems,
        recv_sem,
    ) = rest
    scratch = (attended_ref, dbranch_ref, dqkv_ref)
    ahead = []
    bounds = LOAD_BOUNDS[1 if last else 0]
    for g, first in enumerate(bounds[:-1]):
        for k, far, near in ((1, full_far, full_ref), (0, low_far, low_ref)):
            copy = kept_copy(k, g, bounds, far, near, sems, False)
            copy.start()
            ahead.append((first if last else first + 1, copy.wait))
    recv_copy = pltpu.make_async_copy(recv_col_far, recv_col_ref, recv_sem.at[0])
    recv_copy.start()
    dvecs = []

    def one_run(run):
        here = run_rows(run)

        grad = dbranch_ref[here, :]
        if last:
            grad = grad.astype(F32)
            dresid = yield from feed_back(
                here, full_ref[here, 256:384], grad, weights_ref, ffn_refs, dvecs
            )
            dbranch = dresid.astype(BF16)
            dbranch_ref[here, :] = dbranch
        else:
            dbranch = grad

        drows = yield from attend_back_stages(
            run, dbranch, heads_ref, unfold_ref, weights_ref, low_ref, full_ref, scratch
        )
        if last:
            drows = (dresid + drows.astype(F32)).astype(BF16)
        drows_ref[here, :] = drows

    for run in range(NSUB):
        hot = one_hot_rows(recv_ref[1 if last else 0], run * WINDOW_SLOTS, WINDOW_SLOTS)
        dbranch_ref[run_rows(run), :] = mm(hot, grads_ref[...]).astype(BF16)
    interleave(NSUB, one_run, ahead)
    recv_copy.wait()
    drows = drows_ref[...]
    if last:
        dvecs_ref[...] = sum(dvecs)
        land_rows(recv_col_ref, drows, send_ref)
        projection_grads(low_ref, scratch, dwin_ref, dwout_ref)
        dcontract_ref[...] = mm(active_ref[...], douter_ref[...], TN)
        dexpand_ref[...] = mm(first_ref[...], dinner_ref[...], TN)
        return
    projection_grads(low_ref, scratch, dwin_ref, dwout_ref)
    devices, rows, _ = send_ref.shape
    capacity = recv_col_ref.shape[0] // devices
    for c in range(recv_col_ref.shape[0] // 128):
        hot = one_hot_columns(recv_col_ref[c * 128 : c * 128 + 128, :], DEVICE_SLOTS)
        sent = mm(hot, drows).astype(BF16)
        for part in range(128 // capacity):
            send_ref[c * 128 // capacity + part, 0:capacity, :] = sent[
                part * capacity : part * capacity + capacity
            ]
    share, quarter_rows = late
    store_projections(flat_ref, 0, dwin_ref, dwout_ref)
    for j in range(2):
        flat_ref[pl.ds(512 + j, 8, stride=2), :] = dexpand_ref[0:8, 128 * j : 128 * j + 128]
    flat_ref[pl.ds(528, flat_ref.shape[0] - 528), :] = jnp.zeros(
        (flat_ref.shape[0] - 528, 128), F32
    )
    owners = devices // 4
    for device in range(devices):
        quarter, owner = divmod(device, owners)
        block = share_block(
            flat_ref, owner * share, share, quarter * quarter_rows, rows - capacity, quarter_rows
        )
        send_ref[device, capacity:rows, :] = block.astype(BF16)


def share_block(flat_ref, start, share, first_row, rows, used_rows):
    row, shift = divmod(start, 128)
    row = row + first_row
    lane = iota((rows, 128), 1)
    line = iota((rows, 128), 0)
    block = flat_ref[pl.ds(row, rows), :]
    if shift:
        after = flat_ref[pl.ds(row + 1, rows), :]
        block = pltpu.roll(jnp.where(lane >= shift, block, after), 128 - shift, 1)
    inside = (line < used_rows) & ((line + first_row) * 128 + lane < share)
    return jnp.where(inside, block, 0.0)


def store_projections(flat_ref, base, dwin_ref, dwout_ref):
    for j in range(3):
        flat_ref[pl.ds(base + j, 128, stride=3), :] = dwin_ref[:, 128 * j : 128 * j + 128]
    flat_ref[pl.ds(base + 384, 128), :] = dwout_ref[...]


def centred_rows(rows):
    centre = rows - jnp.mean(rows, axis=-1, keepdims=True)
    spread = jnp.mean(centre * centre, axis=-1, keepdims=True)
    inverse = lax.rsqrt(spread + 1e-05)
    return centre * inverse, inverse


def norm_back(grad, gain, unit, inverse):
    dunit = grad * gain
    return (
        dunit
        - jnp.mean(dunit, axis=-1, keepdims=True)
        - unit * jnp.mean(dunit * unit, axis=-1, keepdims=True)
    ) * inverse


def feed_forward(resid, expand, contract, vecs):
    unit, inverse = centred_rows(resid)
    first = unit * vecs[3:4, :] + vecs[4:5, :]
    first_low = first.astype(BF16)
    bias = jnp.concatenate([vecs[0:1, :], vecs[1:2, :]], axis=1)
    inner = mm(first_low, expand) + bias
    yield
    below = 0.5 + 0.5 * lax.erf(inner * math.sqrt(0.5))
    active = (inner * below).astype(BF16)
    second = first + (mm(active, contract) + vecs[2:3, :])
    return unit, inverse, first_low, inner, below, active, second


def feed_back(here, resid, grad, weights_ref, ffn_refs, dvecs):
    active_ref, douter_ref, first_ref, dinner_ref = ffn_refs
    expand, contract, vecs = feed_weights(weights_ref)
    unit_first, inverse_first, first_low, inner, below, active, second = yield from feed_forward(
        resid, expand, contract, vecs
    )
    active_ref[here, :] = active
    first_ref[here, :] = first_low
    yield
    unit, inverse = centred_rows(second)
    dsecond = norm_back(grad, vecs[5:6, :], unit, inverse)
    douter = dsecond.astype(BF16)
    douter_ref[here, :] = douter
    dactive = mm(douter, contract, NT)
    slope = below + inner * (jnp.exp(-0.5 * inner * inner) * (1.0 / math.sqrt(2.0 * math.pi)))
    yield
    dinner = (dactive * slope).astype(BF16)
    dinner_ref[here, :] = dinner
    dfirst = mm(dinner, expand, NT) + dsecond
    yield

    def down(rows):
        return jnp.sum(rows, axis=0, keepdims=True)

    dbias = down(dinner.astype(F32))
    dvecs.append(
        jnp.concatenate(
            [
                dbias[:, :128],
                dbias[:, 128:],
                down(douter.astype(F32)),
                down(dfirst * unit_first),
                down(dfirst),
                down(grad * unit),
                down(grad),
                jnp.zeros((1, 128), F32),
            ],
            axis=0,
        )
    )
    return norm_back(dfirst, vecs[3:4, :], unit_first, inverse_first)


ROWS = 128


def part_rows(part):
    return pl.ds(part * ROWS, ROWS)


def home_forward_kernel(
    route_col_ref,
    route_ref,
    branch_ref,
    state_ref,
    weights_ref,
    send_ref,
    resid_ref,
    result_ref,
):
    def some_rows(part):
        here = part_rows(part)
        expand, contract, vecs = feed_weights(weights_ref)
        hot = one_hot_columns(route_col_ref[here, :], branch_ref.shape[0])
        resid = state_ref[here, :].astype(F32) + mm(hot, branch_ref[...])
        yield
        resid_ref[here, :] = resid
        second = (yield from feed_forward(resid, expand, contract, vecs))[-1]
        yield
        unit, _ = centred_rows(second)
        result_ref[here, :] = (unit * vecs[5:6, :] + vecs[6:7, :]).astype(BF16)

    interleave(result_ref.shape[0] // ROWS, some_rows)
    scatter_rows(route_ref[1:2, :], result_ref[...], send_ref)


def home_backward_kernel(
    route_col_ref,
    route_ref,
    arrived_ref,
    resid_ref,
    weights_ref,
    dresid_ref,
    send_ref,
    dexpand_ref,
    dcontract_ref,
    dvecs_ref,
    active_ref,
    douter_ref,
    first_ref,
    dinner_ref,
    low_ref,
):
    ffn_refs = (active_ref, douter_ref, first_ref, dinner_ref)
    dvecs = []

    def some_rows(part):
        here = part_rows(part)
        hot = one_hot_columns(route_col_ref[here, :], arrived_ref.shape[0])
        grad = mm(hot, arrived_ref[...])
        yield
        dresid = yield from feed_back(
            here, resid_ref[here, :], grad, weights_ref, ffn_refs, dvecs
        )
        dresid_ref[here, :] = dresid
        low_ref[here, :] = dresid.astype(BF16)

    interleave(dresid_ref.shape[0] // ROWS, some_rows)
    dvecs_ref[...] = sum(dvecs)
    scatter_rows(route_ref[0:1, :], low_ref[...], send_ref)
    dcontract_ref[...] = mm(active_ref[...], douter_ref[...], TN)
    dexpand_ref[...] = mm(first_ref[...], dinner_ref[...], TN)


def take_kernel(route_col_ref, arrived_ref, out_ref):
    for part in range(out_ref.shape[0] // ROWS):
        here = part_rows(part)
        hot = one_hot_columns(route_col_ref[here, :], arrived_ref.shape[0])
        out_ref[here, :] = mm(hot, arrived_ref[...]).astype(BF16)


def finish_kernel(route_col_ref, arrived_ref, dresid_ref, out_ref, rows_ref):
    devices, rows, _ = arrived_ref.shape
    capacity = rows_ref.shape[0] // devices
    for device in range(devices):
        rows_ref[device * capacity : (device + 1) * capacity, :] = arrived_ref[
            device, 0:capacity, :
        ]
    for part in range(out_ref.shape[0] // ROWS):
        here = part_rows(part)
        hot = one_hot_columns(route_col_ref[here, :], rows_ref.shape[0])
        out_ref[here, :] = dresid_ref[here, :] + mm(hot, rows_ref[...])


def late_kernel(quarter_rows, me_ref, early_ref, arrived_ref, *refs):
    outs, parts_ref = refs[:4], refs[4]
    devices, rows, _ = arrived_ref.shape
    late_rows = outs[0].shape[0]
    capacity = rows - late_rows
    late = arrived_ref[0, capacity:rows, :].astype(F32)
    for device in range(1, devices):
        late = late + arrived_ref[device, capacity:rows, :].astype(F32)
    early = early_ref[...]
    square = jnp.sum(early * early) + jnp.sum(late * late)
    line = iota((late_rows, 128), 0)
    parts_ref[0] = jnp.where(line < quarter_rows, late, square)
    for part in range(3):
        piece = early_ref[pl.ds(part * quarter_rows, quarter_rows), :]
        parts_ref[part + 1, 0:quarter_rows, :] = piece
        parts_ref[part + 1, quarter_rows:late_rows, :] = jnp.full(
            (late_rows - quarter_rows, 128), square, F32
        )
    quarter = me_ref[0] // (devices // 4)
    for k, out_ref in enumerate(outs):
        out_ref[...] = parts_ref[quarter ^ k]


def unpack_kernel(share, me_ref, shards_ref, *rest):
    flat_ref = rest[-1]
    outs = rest[:-1]
    devices, block_rows, _ = shards_ref.shape
    lane = iota((block_rows, 128), 1)
    me = me_ref[0]
    for device in range(devices):
        row, shift = divmod(device * share, 128)
        block = shards_ref[me ^ device].astype(F32)
        if shift:
            block = pltpu.roll(block, shift, 1)
            before = jnp.concatenate([flat_ref[pl.ds(row, 1), :], block[:-1]], axis=0)
            block = jnp.where(lane >= shift, block, before)
        flat_ref[pl.ds(row, block_rows), :] = block
    for layer, out_ref in enumerate(outs):
        base = layer * LAYER_ROWS
        for j in range(3):
            out_ref[128 * j : 128 * j + 128, :] = flat_ref[pl.ds(base + j, 128, stride=3), :].astype(
                BF16
            )
        out_ref[384:512, :] = flat_ref[pl.ds(base + 384, 128), :].astype(BF16)
        for j in range(2):
            out_ref[512 + 128 * j : 640 + 128 * j, :] = flat_ref[
                pl.ds(base + 512 + j, 128, stride=2), :
            ].astype(BF16)
        out_ref[768:1024, :] = flat_ref[pl.ds(base + 768, 256), :].astype(BF16)
        vecs = flat_ref[pl.ds(base + 1024, 16), :]
        out_ref[1024:1040, :] = jnp.where(iota((16, 128), 0) < 7, vecs, 0.0).astype(BF16)


def pack_kernel(
    share,
    quarter_rows,
    dwin_ref,
    dwout_ref,
    dexpand_ref,
    dcontract_ref,
    dvecs_ref,
    dexpand_zero_ref,
    dcontract_zero_ref,
    dvecs_zero_ref,
    out_ref,
    flat_ref,
    block_ref,
):
    devices, early_rows, _ = out_ref.shape
    flat_ref[0:512, :] = jnp.zeros((512, 128), F32)
    store_projections(flat_ref, LAYER_ROWS, dwin_ref, dwout_ref)
    for base, expand, contract, vecs in (
        (0, dexpand_zero_ref, dcontract_zero_ref, dvecs_zero_ref),
        (LAYER_ROWS, dexpand_ref, dcontract_ref, dvecs_ref),
    ):
        for j in range(2):
            flat_ref[pl.ds(base + 512 + j, 128, stride=2), :] = expand[:, 128 * j : 128 * j + 128]
        flat_ref[pl.ds(base + 768, 256), :] = contract[...]
        flat_ref[pl.ds(base + 1024, 7), :] = vecs[0:7, :]
    end = LAYERS * LAYER_ROWS
    flat_ref[pl.ds(end, flat_ref.shape[0] - end), :] = jnp.zeros(
        (flat_ref.shape[0] - end, 128), F32
    )
    owners = devices // 4
    block_ref[...] = jnp.zeros_like(block_ref)
    for device in range(devices):
        quarter, owner = divmod(device, owners)
        for part in range(3):
            start = ((part + 1) * owners + owner) * share
            first_row = quarter * quarter_rows
            block_ref[pl.ds(part * quarter_rows, quarter_rows), :] = share_block(
                flat_ref, start, share, first_row, quarter_rows, quarter_rows
            )
        out_ref[device] = block_ref[...].astype(BF16)


def call(
    name,
    micros,
    body,
    outs,
    *args,
    fresh=(),
    scratch=(),
    vmem=24,
    smem=0,
    far_in=0,
    far_out=0,
    sems=(),
):
    near = pl.BlockSpec(memory_space=pltpu.VMEM)
    far = pl.BlockSpec(memory_space=pltpu.HBM)
    specs = [pl.BlockSpec(memory_space=pltpu.SMEM)] * smem
    specs += [near] * (len(args) - smem - far_in) + [far] * far_in
    args = [
        x if i < smem or i in fresh else pltpu.with_memory_space_constraint(x, pltpu.HBM)
        for i, x in enumerate(args)
    ]
    return pl.pallas_call(
        body,
        out_shape=tuple(
            shape_of(o[0], o[1]) if len(o) == 2 else pltpu.HBM(o[0], o[1]) for o in outs
        ),
        in_specs=specs,
        out_specs=tuple([near] * (len(outs) - far_out) + [far] * far_out),
        scratch_shapes=[pltpu.VMEM(s[0], s[1]) for s in scratch]
        + [pltpu.SemaphoreType.DMA(s) for s in sems],
        compiler_params=pltpu.CompilerParams(vmem_limit_bytes=vmem << 20),
        cost_estimate=pl.CostEstimate(
            flops=int(micros * 1e9), bytes_accessed=1 << 16, transcendentals=0
        ),
        name=name,
    )(*args)


def exchange(buffer):
    return lax.all_to_all(buffer, AXES, split_axis=0, concat_axis=0, tiled=True)


def swapped(value, pair, devices, k):
    step = (pair[-1] if k & 1 else 0) ^ (pair[0] if k & 2 else 0)
    return lax.ppermute(value, AXES, [(i, i ^ step) for i in range(devices)])


def paired(parts):
    while len(parts) > 1:
        parts = [parts[i] + parts[i + 1] for i in range(0, len(parts), 2)]
    return parts[0]


def after(value, *others):
    return lax.optimization_barrier((value, *others))[0]


def shards(
    tokens,
    positions,
    cotangent,
    route_send,
    recv_slot,
    slot_bucket,
    master,
    first_moment,
    second_moment,
):
    devices = lax.axis_size("grp") * lax.axis_size("win")
    me = lax.axis_index(AXES)
    home = tokens.shape[0]
    arrivals = recv_slot.shape[2]
    share = master.shape[0]
    share_rows = -(-share // 128)
    block_rows = -(-share_rows // 8) * 8
    quarter_rows = -(-share_rows // 4)
    late_rows = -(-(quarter_rows + 1) // 8) * 8
    early_rows = -(-3 * quarter_rows // 8) * 8
    capacity = arrivals // devices
    width = PILLAR_WIDTH
    flat_rows = -(-(((devices - 1) * share) // 128 + block_rows + 8) // 8) * 8
    late_flat_rows = -(-max(536, ((devices // 4) * share) // 128 + late_rows + 16) // 8) * 8

    heads, unfold, *tables = call(
        "tables",
        4,
        tables_kernel,
        (((EXPANDED, 128), BF16, True), ((WINDOW_SLOTS, 256), BF16, True))
        + (
            ((home, 128), jnp.int32, True),
            ((arrivals, 128), jnp.int32, True),
            ((DEVICE_SLOTS + 64, 128), BF16, True),
            ((NSUB, 2, 128), F32, True),
        )
        * LAYERS,
        route_send,
        recv_slot,
        slot_bucket,
    )
    route_col, recv_col, bucket, bucket_row = (tables[k::4] for k in range(4))
    (send,) = call(
        "start",
        3,
        start_kernel,
        (((arrivals, 2 * width), BF16),),
        route_send,
        tokens,
        positions,
    )
    pos_send, cotangent_send = call(
        "start_next",
        3,
        start_next_kernel,
        (((arrivals, width), BF16, True), ((arrivals, width), BF16, True)),
        route_send,
        positions,
        cotangent,
    )

    copies = jnp.pad(master.astype(BF16), (0, block_rows * 128 - share)).reshape(1, block_rows, 128)
    bits = [devices >> (i + 1) for i in range(devices.bit_length() - 1)]
    for i in range(0, len(bits), 2):
        pair = bits[i : i + 2]
        others = [swapped(copies, pair, devices, k) for k in range(1, 2 ** len(pair))]
        copies = jnp.stack([copies, *others], axis=1).reshape(-1, block_rows, 128)
        if copies.shape[0] == 4:
            arrived = exchange(after(send, copies))
    params = call(
        "unpack",
        2,
        functools.partial(unpack_kernel, share),
        (((1040, width), BF16, True),) * LAYERS,
        me.reshape(1),
        copies,
        scratch=(((flat_rows, 128), F32),),
        smem=1,
    )
    kept_zero = (
        ((DEVICE_SLOTS, 640 + EXPANDED), BF16, True),
        ((DEVICE_SLOTS, 2 * width), F32, True),
    )
    kept_one = (kept_zero[0], ((DEVICE_SLOTS, 3 * width), F32, True))
    recv_col_shape = ((arrivals, 128), jnp.int32)
    slots_low = ((DEVICE_SLOTS, width), BF16)
    slots_wide = ((DEVICE_SLOTS, FF), BF16)
    back_scratch = (slots_low, slots_low, ((DEVICE_SLOTS, 3 * width), BF16))
    arrival_shape = ((arrivals, width), BF16)

    pos_arrived = exchange(after(pos_send, arrived))
    def owner(layer, rows, *pos):
        kept = (kept_zero, kept_one)[layer]
        return call(
            ("first_owner", "last_owner")[layer],
            (13, 18)[layer],
            functools.partial(owner_kernel, layer == 1),
            (arrival_shape, *kept),
            recv_slot,
            bucket[layer],
            bucket_row[layer],
            heads,
            params[layer],
            rows,
            *pos,
            recv_col[layer],
            fresh=(5,),
            scratch=(slots_low, *kept, recv_col_shape),
            far_in=1,
            far_out=2,
            sems=((2, len(STORE_BOUNDS) - 1), (1,)),
            vmem=40,
        )

    send, *stored_zero = owner(0, arrived)
    branch = exchange(after(send, pos_arrived))
    (pos_slots,) = call(
        "slots", 4, slots_kernel, ((*slots_low, True),), recv_slot, pos_arrived
    )
    send, resid_zero = call(
        "home",
        8,
        home_forward_kernel,
        (arrival_shape, ((home, width), F32, True)),
        route_col[0],
        route_send,
        branch,
        tokens,
        params[0],
        fresh=(2,),
        scratch=(((home, width), BF16),),
    )
    arrived = exchange(send)
    cotangent_arrived = exchange(after(cotangent_send, arrived))
    send, *stored_one = owner(1, arrived, pos_slots)
    mixed_arrived = exchange(after(send, cotangent_arrived))
    send, *grads_one = call(
        "last_owner_back",
        22,
        functools.partial(owner_back_kernel, True, None),
        (
            arrival_shape,
            ((width, 3 * width), F32, True),
            ((width, width), F32, True),
            ((width, FF), F32, True),
            ((FF, width), F32, True),
            ((8, width), F32, True),
        ),
        recv_slot,
        heads,
        unfold,
        params[1],
        cotangent_arrived,
        recv_col[1],
        *stored_one,
        scratch=(
            slots_wide,
            slots_low,
            slots_low,
            slots_wide,
            *back_scratch,
            slots_low,
            *kept_one,
            recv_col_shape,
        ),
        far_in=3,
        sems=((2, len(LOAD_BOUNDS[1]) - 1), (1,)),
        vmem=40,
    )
    arrived = exchange(after(send, mixed_arrived))
    (mixed,) = call(
        "take", 2, take_kernel, (((home, width), BF16),), route_col[1], mixed_arrived
    )
    dresid, send, *ffn_zero = call(
        "home_back",
        10,
        home_backward_kernel,
        (
            ((home, width), F32, True),
            arrival_shape,
            ((width, FF), F32, True),
            ((FF, width), F32, True),
            ((8, width), F32, True),
        ),
        route_col[1],
        route_send,
        arrived,
        resid_zero,
        params[0],
        fresh=(2,),
        scratch=(
            ((home, FF), BF16),
            ((home, width), BF16),
            ((home, width), BF16),
            ((home, FF), BF16),
            ((home, width), BF16),
        ),
    )
    arrived = exchange(send)
    (packed,) = call(
        "pack",
        1,
        functools.partial(pack_kernel, share, quarter_rows),
        (((devices, early_rows, 128), BF16, True),),
        *grads_one,
        *ffn_zero,
        scratch=(((flat_rows, 128), F32), ((early_rows, 128), F32)),
    )
    early = exchange(after(packed, arrived))
    (send,) = call(
        "first_owner_back",
        16,
        functools.partial(owner_back_kernel, False, (share, quarter_rows)),
        (((devices, capacity + late_rows, width), BF16),),
        recv_slot,
        heads,
        unfold,
        params[0],
        arrived,
        ffn_zero[0],
        recv_col[0],
        *stored_zero,
        fresh=(4,),
        scratch=(
            ((width, 3 * width), F32),
            ((width, width), F32),
            ((late_flat_rows, 128), F32),
            *back_scratch,
            slots_low,
            *kept_zero,
            recv_col_shape,
        ),
        far_in=3,
        sems=((2, len(LOAD_BOUNDS[0]) - 1), (1,)),
        vmem=40,
    )
    arrived = exchange(after(send, early))
    early = jnp.sum(early.astype(F32), axis=0)
    quarters = call(
        "late",
        1,
        functools.partial(late_kernel, quarter_rows),
        (((late_rows, 128), F32, True),) * 4,
        me.reshape(1),
        after(early, mixed),
        arrived,
        fresh=(2,),
        scratch=(((4, late_rows, 128), F32),),
        smem=1,
    )
    (tokens_grad,) = call(
        "finish",
        3,
        finish_kernel,
        (((home, width), F32),),
        route_col[0],
        arrived,
        dresid,
        fresh=(1,),
        scratch=(((arrivals, width), BF16),),
    )
    quarters = [quarters[0]] + [
        swapped(quarters[k], bits[:2], devices, k) for k in range(1, 4)
    ]
    square = after(paired([q[quarter_rows:] for q in quarters]), tokens_grad)
    for i in range(2, len(bits), 2):
        pair = bits[i : i + 2]
        square = paired(
            [square] + [swapped(square, pair, devices, k) for k in range(1, 2 ** len(pair))]
        )
    total = jnp.sqrt(square[0, 0])
    quarters = jnp.stack([q[:quarter_rows] for q in quarters])
    quarter = me // (devices // 4)
    for bit in (1, 2):
        other = quarters.reshape(4 // (2 * bit), 2, bit, quarter_rows, 128)[:, ::-1]
        quarters = jnp.where(quarter & bit, other.reshape(quarters.shape), quarters)
    shard = quarters.reshape(-1)[:share]
    clip_limit = 0.25 * math.sqrt(NPARAM)
    factor = jnp.minimum(1.0, clip_limit / (total + 1e-06))
    clipped = shard * factor
    new_first = beta_one * first_moment + (1.0 - beta_one) * clipped
    new_second = beta_two * second_moment + (1.0 - beta_two) * clipped * clipped
    first_hat = new_first / (1.0 - beta_one**adam_step)
    second_hat = new_second / (1.0 - beta_two**adam_step)
    new_master = master - rate * (first_hat / (jnp.sqrt(second_hat) + adam_eps) + decay * master)
    return (
        mixed,
        tokens_grad,
        total.reshape(1),
        clipped,
        new_master,
        new_first,
        new_second,
        new_master.astype(BF16),
    )


def solution(mesh):
    in_specs = (
        P(("grp", "win"), None),
        P(None, ("grp", "win"), None),
        P(("grp", "win"), None),
        P(None, ("grp", "win")),
        P(None, ("grp", "win"), None),
        P(None, ("grp", "win")),
        P(("grp", "win")),
        P(("grp", "win")),
        P(("grp", "win")),
    )
    out_specs = (
        P(("grp", "win"), None),
        P(("grp", "win"), None),
        P(),
        P(("grp", "win")),
        P(("grp", "win")),
        P(("grp", "win")),
        P(("grp", "win")),
        P(("grp", "win")),
    )
    return jax.shard_map(shards, mesh=mesh, in_specs=in_specs, out_specs=out_specs, check_vma=False)
```

```python
import functools
import math

import jax
import jax.numpy as jnp
from jax import lax
from jax.experimental import pallas as pl
from jax.experimental.pallas import tpu as pltpu
from jax.sharding import PartitionSpec as P

PILLAR_WIDTH = 128
FF = 256
HEAD_COUNT = 8
HDIM = 16
WINDOW_SLOTS = 144
LAYERS = 2
DEVICE_SLOTS = 1728
NSUB = 12
NPARAM = 263936
LAYER_ROWS = 1031
EXPANDED = HEAD_COUNT * WINDOW_SLOTS
MASKED = -1e30
LOWEST = -3e38

beta_one = 0.5
beta_two = 0.5
adam_step = 4
rate = 0.1
decay = 0.01
adam_eps = 1e-08

BF16 = jnp.bfloat16
F32 = jnp.float32
AXES = ("grp", "win")

NN = (((1,), (0,)), ((), ()))
NT = (((1,), (1,)), ((), ()))
TN = (((0,), (0,)), ((), ()))


def mm(left, right, dims=NN):
    return lax.dot_general(left, right, dims, preferred_element_type=F32)


def iota(shape, dim):
    return lax.broadcasted_iota(jnp.int32, shape, dim)


def shape_of(shape, dtype):
    return jax.ShapeDtypeStruct(shape, dtype)


def one_hot_rows(row_ids, first, count):
    return jnp.where(iota((count, row_ids.shape[1]), 0) + first == row_ids, 1.0, 0.0).astype(BF16)


def one_hot_columns(column_ids, width):
    lane = iota(column_ids.shape, 1)
    pieces = [
        jnp.where(column_ids == lane + 128 * k, 1.0, 0.0).astype(BF16)
        for k in range(-(-width // 128))
    ]
    return jnp.concatenate(pieces, axis=1)[:, :width]


def expand_heads(block, heads):
    main = block[:128]
    tail = block[128:]
    return jnp.concatenate([main] * HEAD_COUNT + [tail] * HEAD_COUNT, axis=0) * heads


def pick_rows(column_ids, source):
    half = source.shape[0] // 2
    upper = column_ids >= half
    local = jnp.where(upper, column_ids - half, column_ids)
    both = mm(one_hot_columns(local, half), jnp.concatenate([source[:half], source[half:]], axis=1))
    return jnp.where(upper, both[:, 128:], both[:, :128])


def inverse_kernel(route_ref, recv_ref, *outs):
    for layer in range(LAYERS):
        for ids, out_ref in (
            (recv_ref[layer], outs[2 * layer]),
            (route_ref[layer : layer + 1, :], outs[2 * layer + 1]),
        ):
            place = iota((ids.shape[1], 128), 0) + 1
            parts = jnp.concatenate(
                [(place >> 6).astype(F32).astype(BF16), (place & 63).astype(F32).astype(BF16)], axis=1
            )
            for c in range(out_ref.shape[0] // 128):
                found = mm(one_hot_rows(ids, c * 128, 128), parts)
                found = found[:, :128] * 64.0 + found[:, 128:] - 1.0
                out_ref[c * 128 : (c + 1) * 128, :] = found.astype(jnp.int32)


def place_rows(place_col_ref, low_rows, send, chunk=256):
    for c in range(send.shape[0] // chunk):
        part = slice(c * chunk, (c + 1) * chunk)
        send[part, :] = pick_rows(place_col_ref[part, :], low_rows).astype(BF16)


def scatter_rows(route_row, low_rows, send, chunk=256):
    for c in range(send.shape[0] // chunk):
        hot = one_hot_rows(route_row, c * chunk, chunk)
        send[c * chunk : (c + 1) * chunk, :] = mm(hot, low_rows).astype(BF16)


def land_rows(recv_col, slot_values, send, chunk=128):
    for c in range(send.shape[0] // chunk):
        part = slice(c * chunk, (c + 1) * chunk)
        send[part, :] = pick_rows(recv_col[part, :], slot_values).astype(BF16)


def on_lanes(row, out_type):
    here = iota((128, 128), 0) == iota((128, 128), 1)
    spread = jnp.where(here, jnp.broadcast_to(row, (128, 128)), 0)
    ones = jnp.ones((128, 128), BF16)
    if out_type == BF16:
        return mm(spread.astype(F32).astype(BF16), ones).astype(BF16)
    high = mm((spread >> 6).astype(F32).astype(BF16), ones)
    low = mm((spread & 63).astype(F32).astype(BF16), ones)
    return (high * 64.0 + low).astype(out_type)


def tables_kernel(route_ref, recv_ref, bucket_ref, heads_ref, unfold_ref, *outs):
    slot = iota((EXPANDED, 128), 0)
    head = jnp.where(slot < 1024, slot >> 7, (slot - 1024) >> 4)
    heads_ref[...] = jnp.where(head == iota((EXPANDED, 128), 1) >> 4, 1.0, 0.0).astype(BF16)
    wide = iota((WINDOW_SLOTS, 256), 1)
    wide = jnp.where(wide < 128, wide, 128 + (wide & 15))
    unfold_ref[...] = jnp.where(iota((WINDOW_SLOTS, 256), 0) == wide, 1.0, 0.0).astype(BF16)
    for layer in range(LAYERS):
        route_col_ref, recv_col_ref, bucket_col_ref, bucket_row_ref = outs[4 * layer : 4 * layer + 4]
        bucket = bucket_ref[layer : layer + 1, :]
        for ids, out_ref in (
            (route_ref[layer : layer + 1, :], route_col_ref),
            (recv_ref[layer], recv_col_ref),
            (jnp.concatenate([bucket, bucket[:, :64]], axis=1), bucket_col_ref),
        ):
            for c in range(out_ref.shape[0] // 128):
                part = slice(c * 128, (c + 1) * 128)
                out_ref[part, :] = on_lanes(ids[:, part], out_ref.dtype)
        bucket = bucket.astype(F32)
        for run in range(NSUB):
            base = run * WINDOW_SLOTS
            tail = bucket[:, base + 128 : base + 144]
            bucket_row_ref[run] = jnp.concatenate(
                [bucket[:, base : base + 128], jnp.concatenate([tail] * 8, axis=1)], axis=0
            )


def start_kernel(route_ref, tokens_ref, pos_ref, out_ref):
    both = jnp.concatenate([tokens_ref[...], pos_ref[0]], axis=1)
    scatter_rows(route_ref[0:1, :], both, out_ref)


def start_next_kernel(route_ref, pos_ref, cotangent_ref, pos_out_ref, cotangent_out_ref):
    both = jnp.concatenate([pos_ref[1], cotangent_ref[...]], axis=1)
    for c in range(pos_out_ref.shape[0] // 256):
        part = slice(c * 256, (c + 1) * 256)
        sent = mm(one_hot_rows(route_ref[1:2, :], c * 256, 256), both).astype(BF16)
        pos_out_ref[part, :] = sent[:, :128]
        cotangent_out_ref[part, :] = sent[:, 128:]


def slots_kernel(slot_col_ref, rows_ref, out_ref):
    for run in range(NSUB):
        part = slice(run * WINDOW_SLOTS, (run + 1) * WINDOW_SLOTS)
        out_ref[part, :] = pick_rows(slot_col_ref[part, :], rows_ref[...]).astype(BF16)


def project_in(weights_ref):
    return jnp.concatenate([weights_ref[128 * j : 128 * j + 128, :] for j in range(3)], axis=1)


def project_out(weights_ref):
    return weights_ref[384:512, :]


def feed_weights(weights_ref):
    expand = jnp.concatenate([weights_ref[512:640, :], weights_ref[640:768, :]], axis=1)
    return expand, weights_ref[768:1024, :], weights_ref[1024:1040, :].astype(F32)


def interleave(count, make, ahead=()):
    waiting = [make(i) for i in range(count)]
    running = []
    turn = 0
    while waiting or running:
        for when, act in ahead:
            if when == turn:
                act()
        if waiting:
            running.insert(0, waiting.pop(0))
        running = [part for part in running if next(part, running) is not running]
        turn += 1
    for when, act in ahead:
        if when >= turn:
            act()


def run_rows(run):
    return pl.ds(run * WINDOW_SLOTS, WINDOW_SLOTS)


STORE_BOUNDS = tuple(range(NSUB + 1))
LOAD_BOUNDS = ((0, 4, 12), (0, 3, 7, 12))


def kept_copy(k, group, bounds, far, near, sems, out):
    first, last = bounds[group : group + 2]
    here = pl.ds(first * WINDOW_SLOTS, (last - first) * WINDOW_SLOTS)
    far, near = far.at[here, :], near.at[here, :]
    ends = (near, far) if out else (far, near)
    return pltpu.make_async_copy(*ends, sems.at[k, group])


def attend_stages(run, slot_rows, joined, bucket, bucket_row, heads_ref, weights_ref, low, full):
    win = project_in(weights_ref)
    query_key = mm(joined, win[:, :256])
    queries = (query_key[:, :128] * 0.25).astype(BF16)
    keys = query_key[:, 128:].astype(BF16)
    values = mm(slot_rows, win[:, 256:]).astype(BF16)
    heads = heads_ref[...]
    block = heads[1024:]
    spread = jnp.concatenate(
        [
            queries * jnp.concatenate([heads[128 * h : 128 * h + 16]] * 9, axis=0)
            for h in range(HEAD_COUNT)
        ],
        axis=0,
    )
    yield
    scores = mm(spread, keys[:128], NT)
    tail = mm(queries, jnp.concatenate([keys[128:]] * 8, axis=0) * block, NT)
    yield

    def same(row):
        return jnp.where((bucket == row) & (row >= 0), 0.0, MASKED)

    main_bias = same(bucket_row[0:1, :])
    tail = tail + same(bucket_row[1:2, :])
    segment = iota((WINDOW_SLOTS, 128), 1) >> 4
    tail_top = jnp.zeros((WINDOW_SLOTS, 128), F32)
    pieces = []
    for h in range(HEAD_COUNT):
        main = scores[WINDOW_SLOTS * h : WINDOW_SLOTS * (h + 1)] + main_bias
        own_tail = segment == h
        top = jnp.max(jnp.maximum(main, jnp.where(own_tail, tail, LOWEST)), axis=1, keepdims=True)
        tail_top = jnp.where(own_tail, top, tail_top)
        pieces.append(jnp.exp(main - top).astype(BF16))
    pieces.append(jnp.exp(tail - tail_top).astype(BF16))
    expo = jnp.concatenate(pieces, axis=1)
    low(jnp.concatenate([joined, slot_rows, queries, keys, values, expo], axis=1))
    yield
    summed = mm(expo, jnp.concatenate([expand_heads(values, heads), heads], axis=1))
    yield
    share = jnp.where(bucket >= 0, 1.0, 0.0) / summed[:, 128:]
    attended = summed[:, :128] * share
    full(jnp.concatenate([attended, share], axis=1))
    return mm(attended.astype(BF16), project_out(weights_ref)).astype(BF16)


def attend_back_stages(
    run, dbranch, heads_ref, unfold_ref, weights_ref, low_ref, full_ref, scratch
):
    attended_ref, dbranch_ref, dqkv_ref = scratch
    here = run_rows(run)
    dattended = mm(dbranch, project_out(weights_ref), NT).astype(BF16).astype(F32)
    yield
    heads = heads_ref[...]
    block = heads[1024:]
    out = full_ref[here, 0:128]
    attended_ref[here, :] = out.astype(BF16)
    dout = (dattended * full_ref[here, 128:256]).astype(BF16)
    weighed = dout.astype(F32) * out
    weighed_high = weighed.astype(BF16)
    weighed_low = (weighed - weighed_high.astype(F32)).astype(BF16)
    centre = mm(weighed_high, block) + mm(weighed_low, block)
    queries = low_ref[here, 256:384]
    keys_wide = expand_heads(low_ref[here, 384:512], heads)
    dprob = mm(dout, expand_heads(low_ref[here, 512:640], heads), NT)
    yield
    expo = low_ref[here, 640:]
    pieces = [
        (
            (dprob[:, 128 * h : 128 * h + 128] - centre[:, 16 * h : 16 * h + 1])
            * expo[:, 128 * h : 128 * h + 128].astype(F32)
        ).astype(BF16)
        for h in range(HEAD_COUNT)
    ]
    pieces.append(((dprob[:, 1024:] - centre) * expo[:, 1024:].astype(F32)).astype(BF16))
    dscore = jnp.concatenate(pieces, axis=1)
    yield
    dqueries = (mm(dscore, keys_wide) * 0.25).astype(BF16)

    def gathered(left, right):
        wide = mm(left, right, TN)
        main = jnp.concatenate(
            [wide[16 * h : 16 * h + 16, 128 * h : 128 * h + 128] for h in range(HEAD_COUNT)],
            axis=0,
        )
        return jnp.concatenate([main, wide[:, 1024:] * block.astype(F32)], axis=1).astype(BF16)

    folded = jnp.concatenate([gathered(queries, dscore), gathered(dout, expo)], axis=0)
    yield
    dkeys_values = mm(unfold_ref[...], folded, NT).astype(BF16)
    dqkv = jnp.concatenate([dqueries, dkeys_values], axis=1)
    dqkv_ref[here, :] = dqkv
    yield
    return mm(dqkv, project_in(weights_ref), NT).astype(BF16)


def projection_grads(low_ref, scratch, dwin_ref, dwout_ref):
    attended_ref, dbranch_ref, dqkv_ref = scratch
    dwout_ref[...] = mm(attended_ref[...], dbranch_ref[...], TN)
    dqkv = dqkv_ref[...]
    dwin_ref[:, :256] = mm(low_ref[:, 0:128], dqkv[:, :256], TN)
    dwin_ref[:, 256:] = mm(low_ref[:, 128:256], dqkv[:, 256:], TN)


def owner_kernel(
    last,
    recv_ref,
    bucket_ref,
    bucket_row_ref,
    heads_ref,
    weights_ref,
    rows_ref,
    *rest,
):
    if last:
        pos_ref, *rest = rest
    (
        recv_col_far,
        send_ref,
        low_far,
        full_far,
        leave_ref,
        low_ref,
        full_ref,
        recv_col_ref,
        sems,
        recv_sem,
    ) = rest
    recv_copy = pltpu.make_async_copy(recv_col_far, recv_col_ref, recv_sem.at[0])
    recv_copy.start()

    def one_run(run):
        here = run_rows(run)

        def low(rows):
            low_ref[here, :] = rows

        def full(rows):
            full_ref[here, 0:256] = rows

        if last:
            landed = pick_rows(recv_ref[here, :], rows_ref[...])
        else:
            landed = mm(one_hot_rows(recv_ref[0], run * WINDOW_SLOTS, WINDOW_SLOTS), rows_ref[...])
        state = landed[:, :128]
        pos = pos_ref[here, :].astype(F32) if last else landed[:, 128:]
        yield
        branch = yield from attend_stages(
            run,
            state.astype(BF16),
            (state + pos).astype(BF16),
            bucket_ref[here, :].astype(F32),
            bucket_row_ref[run],
            heads_ref,
            weights_ref,
            low,
            full,
        )
        if not last:
            leave_ref[here, :] = branch
            return
        yield
        resid = state + branch.astype(F32)
        full_ref[here, 256:384] = resid
        expand, contract, vecs = feed_weights(weights_ref)
        second = (yield from feed_forward(resid, expand, contract, vecs))[-1]
        yield
        unit, _ = centred_rows(second)
        leave_ref[here, :] = (unit * vecs[5:6, :] + vecs[6:7, :]).astype(BF16)

    low_copies = [kept_copy(0, g, STORE_BOUNDS, low_far, low_ref, sems, True) for g in range(len(STORE_BOUNDS) - 1)]
    full_copies = [kept_copy(1, g, STORE_BOUNDS, full_far, full_ref, sems, True) for g in range(len(STORE_BOUNDS) - 1)]
    ahead = [(STORE_BOUNDS[g + 1] + 3, copy.start) for g, copy in enumerate(low_copies)]
    ahead += [(STORE_BOUNDS[g + 1] + 6, copy.start) for g, copy in enumerate(full_copies)]
    interleave(NSUB, one_run, ahead)
    recv_copy.wait()
    land_rows(recv_col_ref, leave_ref[...], send_ref)
    for copy in low_copies + full_copies:
        copy.wait()


def owner_back_kernel(
    last,
    late,
    slot_col_ref,
    heads_ref,
    unfold_ref,
    weights_ref,
    grads_ref,
    *rest,
):
    if not last:
        dexpand_ref, *rest = rest
    recv_col_far, low_far, full_far, send_ref, *rest = rest
    if last:
        dwin_ref, dwout_ref, dexpand_ref, dcontract_ref, dvecs_ref, *rest = rest
        active_ref, douter_ref, first_ref, dinner_ref, *rest = rest
        ffn_refs = (active_ref, douter_ref, first_ref, dinner_ref)
    else:
        dwin_ref, dwout_ref, flat_ref, *rest = rest
    (
        attended_ref,
        dbranch_ref,
        dqkv_ref,
        drows_ref,
        low_ref,
        full_ref,
        recv_col_ref,
        sems,
        recv_sem,
    ) = rest
    scratch = (attended_ref, dbranch_ref, dqkv_ref)
    ahead = []
    bounds = LOAD_BOUNDS[1 if last else 0]
    for g, first in enumerate(bounds[:-1]):
        for k, far, near in ((1, full_far, full_ref), (0, low_far, low_ref)):
            copy = kept_copy(k, g, bounds, far, near, sems, False)
            copy.start()
            ahead.append((first if last else first + 1, copy.wait))
    recv_copy = pltpu.make_async_copy(recv_col_far, recv_col_ref, recv_sem.at[0])
    recv_copy.start()
    dvecs = []

    def one_run(run):
        here = run_rows(run)

        grad = dbranch_ref[here, :]
        if last:
            grad = grad.astype(F32)
            dresid = yield from feed_back(
                here, full_ref[here, 256:384], grad, weights_ref, ffn_refs, dvecs
            )
            dbranch = dresid.astype(BF16)
            dbranch_ref[here, :] = dbranch
        else:
            dbranch = grad

        drows = yield from attend_back_stages(
            run, dbranch, heads_ref, unfold_ref, weights_ref, low_ref, full_ref, scratch
        )
        if last:
            drows = (dresid + drows.astype(F32)).astype(BF16)
        drows_ref[here, :] = drows

    for run in range(NSUB):
        here = run_rows(run)
        dbranch_ref[here, :] = pick_rows(slot_col_ref[here, :], grads_ref[...]).astype(BF16)
    interleave(NSUB, one_run, ahead)
    recv_copy.wait()
    drows = drows_ref[...]
    if last:
        dvecs_ref[...] = sum(dvecs)
        land_rows(recv_col_ref, drows, send_ref)
        projection_grads(low_ref, scratch, dwin_ref, dwout_ref)
        dcontract_ref[...] = mm(active_ref[...], douter_ref[...], TN)
        dexpand_ref[...] = mm(first_ref[...], dinner_ref[...], TN)
        return
    projection_grads(low_ref, scratch, dwin_ref, dwout_ref)
    devices, rows, _ = send_ref.shape
    capacity = recv_col_ref.shape[0] // devices
    for c in range(recv_col_ref.shape[0] // 128):
        sent = pick_rows(recv_col_ref[c * 128 : c * 128 + 128, :], drows).astype(BF16)
        for part in range(128 // capacity):
            send_ref[c * 128 // capacity + part, 0:capacity, :] = sent[
                part * capacity : part * capacity + capacity
            ]
    share, quarter_rows = late
    store_projections(flat_ref, 0, dwin_ref, dwout_ref)
    for j in range(2):
        flat_ref[pl.ds(512 + j, 8, stride=2), :] = dexpand_ref[0:8, 128 * j : 128 * j + 128]
    flat_ref[pl.ds(528, flat_ref.shape[0] - 528), :] = jnp.zeros(
        (flat_ref.shape[0] - 528, 128), F32
    )
    owners = devices // 4
    for device in range(devices):
        quarter, owner = divmod(device, owners)
        block = share_block(
            flat_ref, owner * share, share, quarter * quarter_rows, rows - capacity, quarter_rows
        )
        send_ref[device, capacity:rows, :] = block.astype(BF16)


def share_block(flat_ref, start, share, first_row, rows, used_rows):
    row, shift = divmod(start, 128)
    row = row + first_row
    lane = iota((rows, 128), 1)
    line = iota((rows, 128), 0)
    block = flat_ref[pl.ds(row, rows), :]
    if shift:
        after = flat_ref[pl.ds(row + 1, rows), :]
        block = pltpu.roll(jnp.where(lane >= shift, block, after), 128 - shift, 1)
    inside = (line < used_rows) & ((line + first_row) * 128 + lane < share)
    return jnp.where(inside, block, 0.0)


def store_projections(flat_ref, base, dwin_ref, dwout_ref):
    for j in range(3):
        flat_ref[pl.ds(base + j, 128, stride=3), :] = dwin_ref[:, 128 * j : 128 * j + 128]
    flat_ref[pl.ds(base + 384, 128), :] = dwout_ref[...]


def centred_rows(rows):
    centre = rows - jnp.mean(rows, axis=-1, keepdims=True)
    spread = jnp.mean(centre * centre, axis=-1, keepdims=True)
    inverse = lax.rsqrt(spread + 1e-05)
    return centre * inverse, inverse


def norm_back(grad, gain, unit, inverse):
    dunit = grad * gain
    return (
        dunit
        - jnp.mean(dunit, axis=-1, keepdims=True)
        - unit * jnp.mean(dunit * unit, axis=-1, keepdims=True)
    ) * inverse


def feed_forward(resid, expand, contract, vecs):
    unit, inverse = centred_rows(resid)
    first = unit * vecs[3:4, :] + vecs[4:5, :]
    first_low = first.astype(BF16)
    bias = jnp.concatenate([vecs[0:1, :], vecs[1:2, :]], axis=1)
    inner = mm(first_low, expand) + bias
    yield
    below = 0.5 + 0.5 * lax.erf(inner * math.sqrt(0.5))
    active = (inner * below).astype(BF16)
    second = first + (mm(active, contract) + vecs[2:3, :])
    return unit, inverse, first_low, inner, below, active, second


def feed_back(here, resid, grad, weights_ref, ffn_refs, dvecs):
    active_ref, douter_ref, first_ref, dinner_ref = ffn_refs
    expand, contract, vecs = feed_weights(weights_ref)
    unit_first, inverse_first, first_low, inner, below, active, second = yield from feed_forward(
        resid, expand, contract, vecs
    )
    active_ref[here, :] = active
    first_ref[here, :] = first_low
    yield
    unit, inverse = centred_rows(second)
    dsecond = norm_back(grad, vecs[5:6, :], unit, inverse)
    douter = dsecond.astype(BF16)
    douter_ref[here, :] = douter
    dactive = mm(douter, contract, NT)
    slope = below + inner * (jnp.exp(-0.5 * inner * inner) * (1.0 / math.sqrt(2.0 * math.pi)))
    yield
    dinner = (dactive * slope).astype(BF16)
    dinner_ref[here, :] = dinner
    dfirst = mm(dinner, expand, NT) + dsecond
    yield

    def down(rows):
        return jnp.sum(rows, axis=0, keepdims=True)

    dbias = down(dinner.astype(F32))
    dvecs.append(
        jnp.concatenate(
            [
                dbias[:, :128],
                dbias[:, 128:],
                down(douter.astype(F32)),
                down(dfirst * unit_first),
                down(dfirst),
                down(grad * unit),
                down(grad),
                jnp.zeros((1, 128), F32),
            ],
            axis=0,
        )
    )
    return norm_back(dfirst, vecs[3:4, :], unit_first, inverse_first)


ROWS = 128


def part_rows(part):
    return pl.ds(part * ROWS, ROWS)


def home_forward_kernel(
    route_col_ref,
    place_col_ref,
    branch_ref,
    state_ref,
    weights_ref,
    send_ref,
    resid_ref,
    result_ref,
):
    def some_rows(part):
        here = part_rows(part)
        expand, contract, vecs = feed_weights(weights_ref)
        resid = state_ref[here, :].astype(F32) + pick_rows(route_col_ref[here, :], branch_ref[...])
        yield
        resid_ref[here, :] = resid
        second = (yield from feed_forward(resid, expand, contract, vecs))[-1]
        yield
        unit, _ = centred_rows(second)
        result_ref[here, :] = (unit * vecs[5:6, :] + vecs[6:7, :]).astype(BF16)

    interleave(result_ref.shape[0] // ROWS, some_rows)
    place_rows(place_col_ref, result_ref[...], send_ref)


def home_backward_kernel(
    route_col_ref,
    arrived_ref,
    resid_ref,
    weights_ref,
    place_col_far,
    dresid_ref,
    send_ref,
    dexpand_ref,
    dcontract_ref,
    dvecs_ref,
    active_ref,
    douter_ref,
    first_ref,
    dinner_ref,
    low_ref,
    place_col_ref,
    sem,
):
    place_copy = pltpu.make_async_copy(place_col_far, place_col_ref, sem.at[0])
    place_copy.start()
    ffn_refs = (active_ref, douter_ref, first_ref, dinner_ref)
    dvecs = []

    def some_rows(part):
        here = part_rows(part)
        grad = pick_rows(route_col_ref[here, :], arrived_ref[...])
        yield
        dresid = yield from feed_back(
            here, resid_ref[here, :], grad, weights_ref, ffn_refs, dvecs
        )
        dresid_ref[here, :] = dresid
        low_ref[here, :] = dresid.astype(BF16)

    interleave(dresid_ref.shape[0] // ROWS, some_rows)
    dvecs_ref[...] = sum(dvecs)
    place_copy.wait()
    place_rows(place_col_ref, low_ref[...], send_ref)
    dcontract_ref[...] = mm(active_ref[...], douter_ref[...], TN)
    dexpand_ref[...] = mm(first_ref[...], dinner_ref[...], TN)


def take_kernel(route_col_ref, arrived_ref, out_ref):
    for part in range(out_ref.shape[0] // ROWS):
        here = part_rows(part)
        out_ref[here, :] = pick_rows(route_col_ref[here, :], arrived_ref[...]).astype(BF16)


def finish_kernel(route_col_ref, arrived_ref, dresid_ref, out_ref, rows_ref):
    devices, rows, _ = arrived_ref.shape
    capacity = rows_ref.shape[0] // devices
    for device in range(devices):
        rows_ref[device * capacity : (device + 1) * capacity, :] = arrived_ref[
            device, 0:capacity, :
        ]
    for part in range(out_ref.shape[0] // ROWS):
        here = part_rows(part)
        out_ref[here, :] = dresid_ref[here, :] + pick_rows(route_col_ref[here, :], rows_ref[...])


def late_kernel(quarter_rows, me_ref, early_ref, arrived_ref, *refs):
    outs, parts_ref = refs[:4], refs[4]
    devices, rows, _ = arrived_ref.shape
    late_rows = outs[0].shape[0]
    capacity = rows - late_rows
    late = arrived_ref[0, capacity:rows, :].astype(F32)
    for device in range(1, devices):
        late = late + arrived_ref[device, capacity:rows, :].astype(F32)
    early = early_ref[...]
    square = jnp.sum(early * early) + jnp.sum(late * late)
    line = iota((late_rows, 128), 0)
    parts_ref[0] = jnp.where(line < quarter_rows, late, square)
    for part in range(3):
        piece = early_ref[pl.ds(part * quarter_rows, quarter_rows), :]
        parts_ref[part + 1, 0:quarter_rows, :] = piece
        parts_ref[part + 1, quarter_rows:late_rows, :] = jnp.full(
            (late_rows - quarter_rows, 128), square, F32
        )
    quarter = me_ref[0] // (devices // 4)
    for k, out_ref in enumerate(outs):
        out_ref[...] = parts_ref[quarter ^ k]


def unpack_kernel(share, me_ref, shards_ref, *rest):
    flat_ref = rest[-1]
    outs = rest[:-1]
    devices, block_rows, _ = shards_ref.shape
    lane = iota((block_rows, 128), 1)
    me = me_ref[0]
    for device in range(devices):
        row, shift = divmod(device * share, 128)
        block = shards_ref[me ^ device].astype(F32)
        if shift:
            block = pltpu.roll(block, shift, 1)
            before = jnp.concatenate([flat_ref[pl.ds(row, 1), :], block[:-1]], axis=0)
            block = jnp.where(lane >= shift, block, before)
        flat_ref[pl.ds(row, block_rows), :] = block
    for layer, out_ref in enumerate(outs):
        base = layer * LAYER_ROWS
        for j in range(3):
            out_ref[128 * j : 128 * j + 128, :] = flat_ref[pl.ds(base + j, 128, stride=3), :].astype(
                BF16
            )
        out_ref[384:512, :] = flat_ref[pl.ds(base + 384, 128), :].astype(BF16)
        for j in range(2):
            out_ref[512 + 128 * j : 640 + 128 * j, :] = flat_ref[
                pl.ds(base + 512 + j, 128, stride=2), :
            ].astype(BF16)
        out_ref[768:1024, :] = flat_ref[pl.ds(base + 768, 256), :].astype(BF16)
        vecs = flat_ref[pl.ds(base + 1024, 16), :]
        out_ref[1024:1040, :] = jnp.where(iota((16, 128), 0) < 7, vecs, 0.0).astype(BF16)


def pack_kernel(
    share,
    quarter_rows,
    dwin_ref,
    dwout_ref,
    dexpand_ref,
    dcontract_ref,
    dvecs_ref,
    dexpand_zero_ref,
    dcontract_zero_ref,
    dvecs_zero_ref,
    out_ref,
    flat_ref,
    block_ref,
):
    devices, early_rows, _ = out_ref.shape
    flat_ref[0:512, :] = jnp.zeros((512, 128), F32)
    store_projections(flat_ref, LAYER_ROWS, dwin_ref, dwout_ref)
    for base, expand, contract, vecs in (
        (0, dexpand_zero_ref, dcontract_zero_ref, dvecs_zero_ref),
        (LAYER_ROWS, dexpand_ref, dcontract_ref, dvecs_ref),
    ):
        for j in range(2):
            flat_ref[pl.ds(base + 512 + j, 128, stride=2), :] = expand[:, 128 * j : 128 * j + 128]
        flat_ref[pl.ds(base + 768, 256), :] = contract[...]
        flat_ref[pl.ds(base + 1024, 7), :] = vecs[0:7, :]
    end = LAYERS * LAYER_ROWS
    flat_ref[pl.ds(end, flat_ref.shape[0] - end), :] = jnp.zeros(
        (flat_ref.shape[0] - end, 128), F32
    )
    owners = devices // 4
    block_ref[...] = jnp.zeros_like(block_ref)
    for device in range(devices):
        quarter, owner = divmod(device, owners)
        for part in range(3):
            start = ((part + 1) * owners + owner) * share
            first_row = quarter * quarter_rows
            block_ref[pl.ds(part * quarter_rows, quarter_rows), :] = share_block(
                flat_ref, start, share, first_row, quarter_rows, quarter_rows
            )
        out_ref[device] = block_ref[...].astype(BF16)


def call(
    name,
    micros,
    body,
    outs,
    *args,
    fresh=(),
    scratch=(),
    vmem=24,
    smem=0,
    far_in=0,
    far_out=0,
    sems=(),
):
    near = pl.BlockSpec(memory_space=pltpu.VMEM)
    far = pl.BlockSpec(memory_space=pltpu.HBM)
    specs = [pl.BlockSpec(memory_space=pltpu.SMEM)] * smem
    specs += [near] * (len(args) - smem - far_in) + [far] * far_in
    args = [
        x if i < smem or i in fresh else pltpu.with_memory_space_constraint(x, pltpu.HBM)
        for i, x in enumerate(args)
    ]
    return pl.pallas_call(
        body,
        out_shape=tuple(
            shape_of(o[0], o[1]) if len(o) == 2 else pltpu.HBM(o[0], o[1]) for o in outs
        ),
        in_specs=specs,
        out_specs=tuple([near] * (len(outs) - far_out) + [far] * far_out),
        scratch_shapes=[pltpu.VMEM(s[0], s[1]) for s in scratch]
        + [pltpu.SemaphoreType.DMA(s) for s in sems],
        compiler_params=pltpu.CompilerParams(vmem_limit_bytes=vmem << 20),
        cost_estimate=pl.CostEstimate(
            flops=int(micros * 1e9), bytes_accessed=1 << 16, transcendentals=0
        ),
        name=name,
    )(*args)


def exchange(buffer):
    return lax.all_to_all(buffer, AXES, split_axis=0, concat_axis=0, tiled=True)


def swapped(value, pair, devices, k):
    step = (pair[-1] if k & 1 else 0) ^ (pair[0] if k & 2 else 0)
    return lax.ppermute(value, AXES, [(i, i ^ step) for i in range(devices)])


def paired(parts):
    while len(parts) > 1:
        parts = [parts[i] + parts[i + 1] for i in range(0, len(parts), 2)]
    return parts[0]


def after(value, *others):
    return lax.optimization_barrier((value, *others))[0]


def shards(
    tokens,
    positions,
    cotangent,
    route_send,
    recv_slot,
    slot_bucket,
    master,
    first_moment,
    second_moment,
):
    devices = lax.axis_size("grp") * lax.axis_size("win")
    me = lax.axis_index(AXES)
    home = tokens.shape[0]
    arrivals = recv_slot.shape[2]
    share = master.shape[0]
    share_rows = -(-share // 128)
    block_rows = -(-share_rows // 8) * 8
    quarter_rows = -(-share_rows // 4)
    late_rows = -(-(quarter_rows + 1) // 8) * 8
    early_rows = -(-3 * quarter_rows // 8) * 8
    capacity = arrivals // devices
    width = PILLAR_WIDTH
    flat_rows = -(-(((devices - 1) * share) // 128 + block_rows + 8) // 8) * 8
    late_flat_rows = -(-max(536, ((devices // 4) * share) // 128 + late_rows + 16) // 8) * 8

    heads, unfold, *tables = call(
        "tables",
        4,
        tables_kernel,
        (((EXPANDED, 128), BF16, True), ((WINDOW_SLOTS, 256), BF16, True))
        + (
            ((home, 128), jnp.int32, True),
            ((arrivals, 128), jnp.int32, True),
            ((DEVICE_SLOTS + 64, 128), BF16, True),
            ((NSUB, 2, 128), F32, True),
        )
        * LAYERS,
        route_send,
        recv_slot,
        slot_bucket,
    )
    route_col, recv_col, bucket, bucket_row = (tables[k::4] for k in range(4))
    (send,) = call(
        "start",
        3,
        start_kernel,
        (((arrivals, 2 * width), BF16),),
        route_send,
        tokens,
        positions,
    )
    pos_send, cotangent_send = call(
        "start_next",
        3,
        start_next_kernel,
        (((arrivals, width), BF16, True), ((arrivals, width), BF16, True)),
        route_send,
        positions,
        cotangent,
    )

    copies = jnp.pad(master.astype(BF16), (0, block_rows * 128 - share)).reshape(1, block_rows, 128)
    bits = [devices >> (i + 1) for i in range(devices.bit_length() - 1)]
    for i in range(0, len(bits), 2):
        pair = bits[i : i + 2]
        others = [swapped(copies, pair, devices, k) for k in range(1, 2 ** len(pair))]
        copies = jnp.stack([copies, *others], axis=1).reshape(-1, block_rows, 128)
        if copies.shape[0] == 4:
            arrived = exchange(after(send, copies))
    params = call(
        "unpack",
        2,
        functools.partial(unpack_kernel, share),
        (((1040, width), BF16, True),) * LAYERS,
        me.reshape(1),
        copies,
        scratch=(((flat_rows, 128), F32),),
        smem=1,
    )
    kept_zero = (
        ((DEVICE_SLOTS, 640 + EXPANDED), BF16, True),
        ((DEVICE_SLOTS, 2 * width), F32, True),
    )
    kept_one = (kept_zero[0], ((DEVICE_SLOTS, 3 * width), F32, True))
    recv_col_shape = ((arrivals, 128), jnp.int32)
    slots_low = ((DEVICE_SLOTS, width), BF16)
    slots_wide = ((DEVICE_SLOTS, FF), BF16)
    back_scratch = (slots_low, slots_low, ((DEVICE_SLOTS, 3 * width), BF16))
    arrival_shape = ((arrivals, width), BF16)

    pos_arrived = exchange(after(pos_send, arrived))
    def owner(layer, rows, *pos):
        kept = (kept_zero, kept_one)[layer]
        return call(
            ("first_owner", "last_owner")[layer],
            (13, 18)[layer],
            functools.partial(owner_kernel, layer == 1),
            (arrival_shape, *kept),
            slot_col[1] if layer else recv_slot,
            bucket[layer],
            bucket_row[layer],
            heads,
            params[layer],
            rows,
            *pos,
            recv_col[layer],
            fresh=(5,),
            scratch=(slots_low, *kept, recv_col_shape),
            far_in=1,
            far_out=2,
            sems=((2, len(STORE_BOUNDS) - 1), (1,)),
            vmem=40,
        )

    send, *stored_zero = owner(0, arrived)
    inverse = call(
        "inverse",
        6,
        inverse_kernel,
        (
            ((DEVICE_SLOTS + 64, 128), jnp.int32, True),
            ((arrivals, 128), jnp.int32, True),
        )
        * LAYERS,
        after(route_send, stored_zero[1]),
        recv_slot,
    )
    slot_col, place_col = inverse[0::2], inverse[1::2]
    branch = exchange(after(send, pos_arrived))
    (pos_slots,) = call(
        "slots", 4, slots_kernel, ((*slots_low, True),), slot_col[1], pos_arrived
    )
    send, resid_zero = call(
        "home",
        8,
        home_forward_kernel,
        (arrival_shape, ((home, width), F32, True)),
        route_col[0],
        place_col[1],
        branch,
        tokens,
        params[0],
        fresh=(2,),
        scratch=(((home, width), BF16),),
    )
    arrived = exchange(send)
    cotangent_arrived = exchange(after(cotangent_send, arrived))
    send, *stored_one = owner(1, arrived, pos_slots)
    mixed_arrived = exchange(after(send, cotangent_arrived))
    send, *grads_one = call(
        "last_owner_back",
        22,
        functools.partial(owner_back_kernel, True, None),
        (
            arrival_shape,
            ((width, 3 * width), F32, True),
            ((width, width), F32, True),
            ((width, FF), F32, True),
            ((FF, width), F32, True),
            ((8, width), F32, True),
        ),
        slot_col[1],
        heads,
        unfold,
        params[1],
        cotangent_arrived,
        recv_col[1],
        *stored_one,
        scratch=(
            slots_wide,
            slots_low,
            slots_low,
            slots_wide,
            *back_scratch,
            slots_low,
            *kept_one,
            recv_col_shape,
        ),
        far_in=3,
        sems=((2, len(LOAD_BOUNDS[1]) - 1), (1,)),
        vmem=40,
    )
    arrived = exchange(after(send, mixed_arrived))
    (mixed,) = call(
        "take", 2, take_kernel, (((home, width), BF16),), route_col[1], mixed_arrived
    )
    dresid, send, *ffn_zero = call(
        "home_back",
        10,
        home_backward_kernel,
        (
            ((home, width), F32, True),
            arrival_shape,
            ((width, FF), F32, True),
            ((FF, width), F32, True),
            ((8, width), F32, True),
        ),
        route_col[1],
        arrived,
        resid_zero,
        params[0],
        place_col[0],
        fresh=(1,),
        far_in=1,
        sems=((1,),),
        scratch=(
            ((home, FF), BF16),
            ((home, width), BF16),
            ((home, width), BF16),
            ((home, FF), BF16),
            ((home, width), BF16),
            recv_col_shape,
        ),
    )
    arrived = exchange(send)
    (packed,) = call(
        "pack",
        1,
        functools.partial(pack_kernel, share, quarter_rows),
        (((devices, early_rows, 128), BF16, True),),
        *grads_one,
        *ffn_zero,
        scratch=(((flat_rows, 128), F32), ((early_rows, 128), F32)),
    )
    early = exchange(after(packed, arrived))
    (send,) = call(
        "first_owner_back",
        16,
        functools.partial(owner_back_kernel, False, (share, quarter_rows)),
        (((devices, capacity + late_rows, width), BF16),),
        slot_col[0],
        heads,
        unfold,
        params[0],
        arrived,
        ffn_zero[0],
        recv_col[0],
        *stored_zero,
        fresh=(4,),
        scratch=(
            ((width, 3 * width), F32),
            ((width, width), F32),
            ((late_flat_rows, 128), F32),
            *back_scratch,
            slots_low,
            *kept_zero,
            recv_col_shape,
        ),
        far_in=3,
        sems=((2, len(LOAD_BOUNDS[0]) - 1), (1,)),
        vmem=40,
    )
    arrived = exchange(after(send, early))
    early = jnp.sum(early.astype(F32), axis=0)
    quarters = call(
        "late",
        1,
        functools.partial(late_kernel, quarter_rows),
        (((late_rows, 128), F32, True),) * 4,
        me.reshape(1),
        after(early, mixed),
        arrived,
        fresh=(2,),
        scratch=(((4, late_rows, 128), F32),),
        smem=1,
    )
    (tokens_grad,) = call(
        "finish",
        3,
        finish_kernel,
        (((home, width), F32),),
        route_col[0],
        arrived,
        dresid,
        fresh=(1,),
        scratch=(((arrivals, width), BF16),),
    )
    quarters = [quarters[0]] + [
        swapped(quarters[k], bits[:2], devices, k) for k in range(1, 4)
    ]
    square = after(paired([q[quarter_rows:] for q in quarters]), tokens_grad)
    for i in range(2, len(bits), 2):
        pair = bits[i : i + 2]
        square = paired(
            [square] + [swapped(square, pair, devices, k) for k in range(1, 2 ** len(pair))]
        )
    total = jnp.sqrt(square[0, 0])
    quarters = jnp.stack([q[:quarter_rows] for q in quarters])
    quarter = me // (devices // 4)
    for bit in (1, 2):
        other = quarters.reshape(4 // (2 * bit), 2, bit, quarter_rows, 128)[:, ::-1]
        quarters = jnp.where(quarter & bit, other.reshape(quarters.shape), quarters)
    shard = quarters.reshape(-1)[:share]
    clip_limit = 0.25 * math.sqrt(NPARAM)
    factor = jnp.minimum(1.0, clip_limit / (total + 1e-06))
    clipped = shard * factor
    new_first = beta_one * first_moment + (1.0 - beta_one) * clipped
    new_second = beta_two * second_moment + (1.0 - beta_two) * clipped * clipped
    first_hat = new_first / (1.0 - beta_one**adam_step)
    second_hat = new_second / (1.0 - beta_two**adam_step)
    new_master = master - rate * (first_hat / (jnp.sqrt(second_hat) + adam_eps) + decay * master)
    return (
        mixed,
        tokens_grad,
        total.reshape(1),
        clipped,
        new_master,
        new_first,
        new_second,
        new_master.astype(BF16),
    )


def solution(mesh):
    in_specs = (
        P(("grp", "win"), None),
        P(None, ("grp", "win"), None),
        P(("grp", "win"), None),
        P(None, ("grp", "win")),
        P(None, ("grp", "win"), None),
        P(None, ("grp", "win")),
        P(("grp", "win")),
        P(("grp", "win")),
        P(("grp", "win")),
    )
    out_specs = (
        P(("grp", "win"), None),
        P(("grp", "win"), None),
        P(),
        P(("grp", "win")),
        P(("grp", "win")),
        P(("grp", "win")),
        P(("grp", "win")),
        P(("grp", "win")),
    )
    return jax.shard_map(shards, mesh=mesh, in_specs=in_specs, out_specs=out_specs, check_vma=False)
```

```python
import functools
import math

import jax
import jax.numpy as jnp
from jax import lax
from jax.experimental import pallas as pl
from jax.experimental.pallas import tpu as pltpu
from jax.sharding import PartitionSpec as P

PILLAR_WIDTH = 128
FF = 256
HEAD_COUNT = 8
HDIM = 16
WINDOW_SLOTS = 144
LAYERS = 2
DEVICE_SLOTS = 1728
NSUB = 12
NPARAM = 263936
LAYER_ROWS = 1031
EXPANDED = HEAD_COUNT * WINDOW_SLOTS
MASKED = -1e30
LOWEST = -3e38

beta_one = 0.5
beta_two = 0.5
adam_step = 4
rate = 0.1
decay = 0.01
adam_eps = 1e-08

BF16 = jnp.bfloat16
F32 = jnp.float32
AXES = ("grp", "win")

NN = (((1,), (0,)), ((), ()))
NT = (((1,), (1,)), ((), ()))
TN = (((0,), (0,)), ((), ()))


def mm(left, right, dims=NN):
    return lax.dot_general(left, right, dims, preferred_element_type=F32)


def iota(shape, dim):
    return lax.broadcasted_iota(jnp.int32, shape, dim)


def shape_of(shape, dtype):
    return jax.ShapeDtypeStruct(shape, dtype)


def one_hot_rows(row_ids, first, count):
    return jnp.where(iota((count, row_ids.shape[1]), 0) + first == row_ids, 1.0, 0.0).astype(BF16)


def one_hot_columns(column_ids, width):
    lane = iota(column_ids.shape, 1)
    pieces = [
        jnp.where(column_ids == lane + 128 * k, 1.0, 0.0).astype(BF16)
        for k in range(-(-width // 128))
    ]
    return jnp.concatenate(pieces, axis=1)[:, :width]


def expand_heads(block, heads):
    main = block[:128]
    tail = block[128:]
    return jnp.concatenate([main] * HEAD_COUNT + [tail] * HEAD_COUNT, axis=0) * heads


def pick_rows(column_ids, source):
    half = source.shape[0] // 2
    column_ids = column_ids.astype(jnp.int32)
    upper = column_ids >= half
    local = jnp.where(upper, column_ids - half, column_ids)
    both = mm(one_hot_columns(local, half), jnp.concatenate([source[:half], source[half:]], axis=1))
    return jnp.where(upper, both[:, 128:], both[:, :128])


def inverse_kernel(route_ref, recv_ref, *outs):
    for layer in range(LAYERS):
        for ids, out_ref in (
            (recv_ref[layer], outs[2 * layer]),
            (route_ref[layer : layer + 1, :], outs[2 * layer + 1]),
        ):
            place = iota((ids.shape[1], 128), 0) + 1
            parts = jnp.concatenate(
                [(place >> 6).astype(F32).astype(BF16), (place & 63).astype(F32).astype(BF16)], axis=1
            )
            for c in range(out_ref.shape[0] // 128):
                found = mm(one_hot_rows(ids, c * 128, 128), parts)
                found = found[:, :128] * 64.0 + found[:, 128:] - 1.0
                out_ref[c * 128 : (c + 1) * 128, :] = found.astype(jnp.int32).astype(jnp.int16)


def place_rows(place_col_ref, low_rows, send, chunk=256):
    for c in range(send.shape[0] // chunk):
        part = slice(c * chunk, (c + 1) * chunk)
        send[part, :] = pick_rows(place_col_ref[part, :], low_rows).astype(BF16)


def scatter_rows(route_row, low_rows, send, chunk=256):
    for c in range(send.shape[0] // chunk):
        hot = one_hot_rows(route_row, c * chunk, chunk)
        send[c * chunk : (c + 1) * chunk, :] = mm(hot, low_rows).astype(BF16)


def land_rows(recv_col, slot_values, send, chunk=128):
    for c in range(send.shape[0] // chunk):
        part = slice(c * chunk, (c + 1) * chunk)
        send[part, :] = pick_rows(recv_col[part, :], slot_values).astype(BF16)


def on_lanes(row, out_type):
    here = iota((128, 128), 0) == iota((128, 128), 1)
    spread = jnp.where(here, jnp.broadcast_to(row, (128, 128)), 0)
    ones = jnp.ones((128, 128), BF16)
    if out_type == BF16:
        return mm(spread.astype(F32).astype(BF16), ones).astype(BF16)
    high = mm((spread >> 6).astype(F32).astype(BF16), ones)
    low = mm((spread & 63).astype(F32).astype(BF16), ones)
    return (high * 64.0 + low).astype(jnp.int32).astype(out_type)


def tables_kernel(route_ref, recv_ref, bucket_ref, heads_ref, unfold_ref, *outs):
    slot = iota((EXPANDED, 128), 0)
    head = jnp.where(slot < 1024, slot >> 7, (slot - 1024) >> 4)
    heads_ref[...] = jnp.where(head == iota((EXPANDED, 128), 1) >> 4, 1.0, 0.0).astype(BF16)
    wide = iota((WINDOW_SLOTS, 256), 1)
    wide = jnp.where(wide < 128, wide, 128 + (wide & 15))
    unfold_ref[...] = jnp.where(iota((WINDOW_SLOTS, 256), 0) == wide, 1.0, 0.0).astype(BF16)
    for layer in range(LAYERS):
        route_col_ref, recv_col_ref, bucket_col_ref, bucket_row_ref = outs[4 * layer : 4 * layer + 4]
        bucket = bucket_ref[layer : layer + 1, :]
        for ids, out_ref in (
            (route_ref[layer : layer + 1, :], route_col_ref),
            (recv_ref[layer], recv_col_ref),
            (jnp.concatenate([bucket, bucket[:, :64]], axis=1), bucket_col_ref),
        ):
            for c in range(out_ref.shape[0] // 128):
                part = slice(c * 128, (c + 1) * 128)
                out_ref[part, :] = on_lanes(ids[:, part], out_ref.dtype)
        bucket = bucket.astype(F32)
        for run in range(NSUB):
            base = run * WINDOW_SLOTS
            tail = bucket[:, base + 128 : base + 144]
            bucket_row_ref[run] = jnp.concatenate(
                [bucket[:, base : base + 128], jnp.concatenate([tail] * 8, axis=1)], axis=0
            )


def start_kernel(route_ref, tokens_ref, pos_ref, out_ref):
    both = jnp.concatenate([tokens_ref[...], pos_ref[0]], axis=1)
    scatter_rows(route_ref[0:1, :], both, out_ref)


def start_next_kernel(route_ref, pos_ref, cotangent_ref, pos_out_ref, cotangent_out_ref):
    both = jnp.concatenate([pos_ref[1], cotangent_ref[...]], axis=1)
    for c in range(pos_out_ref.shape[0] // 256):
        part = slice(c * 256, (c + 1) * 256)
        sent = mm(one_hot_rows(route_ref[1:2, :], c * 256, 256), both).astype(BF16)
        pos_out_ref[part, :] = sent[:, :128]
        cotangent_out_ref[part, :] = sent[:, 128:]


def slots_kernel(slot_col_ref, rows_ref, out_ref):
    for run in range(NSUB):
        part = slice(run * WINDOW_SLOTS, (run + 1) * WINDOW_SLOTS)
        out_ref[part, :] = pick_rows(slot_col_ref[part, :], rows_ref[...]).astype(BF16)


def project_in(weights_ref):
    return jnp.concatenate([weights_ref[128 * j : 128 * j + 128, :] for j in range(3)], axis=1)


def project_out(weights_ref):
    return weights_ref[384:512, :]


def feed_weights(weights_ref):
    expand = jnp.concatenate([weights_ref[512:640, :], weights_ref[640:768, :]], axis=1)
    return expand, weights_ref[768:1024, :], weights_ref[1024:1040, :].astype(F32)


def interleave(count, make, ahead=()):
    waiting = [make(i) for i in range(count)]
    running = []
    turn = 0
    while waiting or running:
        for when, act in ahead:
            if when == turn:
                act()
        if waiting:
            running.insert(0, waiting.pop(0))
        running = [part for part in running if next(part, running) is not running]
        turn += 1
    for when, act in ahead:
        if when >= turn:
            act()


def run_rows(run):
    return pl.ds(run * WINDOW_SLOTS, WINDOW_SLOTS)


STORE_BOUNDS = tuple(range(NSUB + 1))
LOAD_BOUNDS = ((0, 4, 12), (0, 3, 7, 12))


def kept_copy(k, group, bounds, far, near, sems, out):
    first, last = bounds[group : group + 2]
    here = pl.ds(first * WINDOW_SLOTS, (last - first) * WINDOW_SLOTS)
    far, near = far.at[here, :], near.at[here, :]
    ends = (near, far) if out else (far, near)
    return pltpu.make_async_copy(*ends, sems.at[k, group])


def attend_stages(run, slot_rows, joined, bucket, bucket_row, heads_ref, weights_ref, low, full):
    win = project_in(weights_ref)
    query_key = mm(joined, win[:, :256])
    queries = (query_key[:, :128] * 0.25).astype(BF16)
    keys = query_key[:, 128:].astype(BF16)
    values = mm(slot_rows, win[:, 256:]).astype(BF16)
    heads = heads_ref[...]
    block = heads[1024:]
    spread = jnp.concatenate(
        [
            queries * jnp.concatenate([heads[128 * h : 128 * h + 16]] * 9, axis=0)
            for h in range(HEAD_COUNT)
        ],
        axis=0,
    )
    yield
    scores = mm(spread, keys[:128], NT)
    tail = mm(queries, jnp.concatenate([keys[128:]] * 8, axis=0) * block, NT)
    yield

    def same(row):
        return jnp.where((bucket == row) & (row >= 0), 0.0, MASKED)

    main_bias = same(bucket_row[0:1, :])
    tail = tail + same(bucket_row[1:2, :])
    segment = iota((WINDOW_SLOTS, 128), 1) >> 4
    tail_top = jnp.zeros((WINDOW_SLOTS, 128), F32)
    pieces = []
    for h in range(HEAD_COUNT):
        main = scores[WINDOW_SLOTS * h : WINDOW_SLOTS * (h + 1)] + main_bias
        own_tail = segment == h
        top = jnp.max(jnp.maximum(main, jnp.where(own_tail, tail, LOWEST)), axis=1, keepdims=True)
        tail_top = jnp.where(own_tail, top, tail_top)
        pieces.append(jnp.exp(main - top).astype(BF16))
    pieces.append(jnp.exp(tail - tail_top).astype(BF16))
    expo = jnp.concatenate(pieces, axis=1)
    low(jnp.concatenate([joined, slot_rows, queries, keys, values, expo], axis=1))
    yield
    summed = mm(expo, jnp.concatenate([expand_heads(values, heads), heads], axis=1))
    yield
    share = jnp.where(bucket >= 0, 1.0, 0.0) / summed[:, 128:]
    attended = summed[:, :128] * share
    full(jnp.concatenate([attended, share], axis=1))
    return mm(attended.astype(BF16), project_out(weights_ref)).astype(BF16)


def attend_back_stages(
    run, dbranch, heads_ref, unfold_ref, weights_ref, low_ref, full_ref, scratch
):
    attended_ref, dbranch_ref, dqkv_ref = scratch
    here = run_rows(run)
    dattended = mm(dbranch, project_out(weights_ref), NT).astype(BF16).astype(F32)
    yield
    heads = heads_ref[...]
    block = heads[1024:]
    out = full_ref[here, 0:128]
    attended_ref[here, :] = out.astype(BF16)
    dout = (dattended * full_ref[here, 128:256]).astype(BF16)
    weighed = dout.astype(F32) * out
    weighed_high = weighed.astype(BF16)
    weighed_low = (weighed - weighed_high.astype(F32)).astype(BF16)
    centre = mm(weighed_high, block) + mm(weighed_low, block)
    queries = low_ref[here, 256:384]
    keys_wide = expand_heads(low_ref[here, 384:512], heads)
    dprob = mm(dout, expand_heads(low_ref[here, 512:640], heads), NT)
    yield
    expo = low_ref[here, 640:]
    pieces = [
        (
            (dprob[:, 128 * h : 128 * h + 128] - centre[:, 16 * h : 16 * h + 1])
            * expo[:, 128 * h : 128 * h + 128].astype(F32)
        ).astype(BF16)
        for h in range(HEAD_COUNT)
    ]
    pieces.append(((dprob[:, 1024:] - centre) * expo[:, 1024:].astype(F32)).astype(BF16))
    dscore = jnp.concatenate(pieces, axis=1)
    yield
    dqueries = (mm(dscore, keys_wide) * 0.25).astype(BF16)

    def gathered(left, right):
        wide = mm(left, right, TN)
        main = jnp.concatenate(
            [wide[16 * h : 16 * h + 16, 128 * h : 128 * h + 128] for h in range(HEAD_COUNT)],
            axis=0,
        )
        return jnp.concatenate([main, wide[:, 1024:] * block.astype(F32)], axis=1).astype(BF16)

    folded = jnp.concatenate([gathered(queries, dscore), gathered(dout, expo)], axis=0)
    yield
    dkeys_values = mm(unfold_ref[...], folded, NT).astype(BF16)
    dqkv = jnp.concatenate([dqueries, dkeys_values], axis=1)
    dqkv_ref[here, :] = dqkv
    yield
    return mm(dqkv, project_in(weights_ref), NT).astype(BF16)


def projection_grads(low_ref, scratch, dwin_ref, dwout_ref):
    attended_ref, dbranch_ref, dqkv_ref = scratch
    dwout_ref[...] = mm(attended_ref[...], dbranch_ref[...], TN)
    dqkv = dqkv_ref[...]
    dwin_ref[:, :256] = mm(low_ref[:, 0:128], dqkv[:, :256], TN)
    dwin_ref[:, 256:] = mm(low_ref[:, 128:256], dqkv[:, 256:], TN)


def owner_kernel(
    last,
    recv_ref,
    bucket_ref,
    bucket_row_ref,
    heads_ref,
    weights_ref,
    rows_ref,
    *rest,
):
    if last:
        pos_ref, *rest = rest
    (
        recv_col_far,
        send_ref,
        low_far,
        full_far,
        leave_ref,
        low_ref,
        full_ref,
        recv_col_ref,
        sems,
        recv_sem,
    ) = rest
    recv_copy = pltpu.make_async_copy(recv_col_far, recv_col_ref, recv_sem.at[0])
    recv_copy.start()

    def one_run(run):
        here = run_rows(run)

        def low(rows):
            low_ref[here, :] = rows

        def full(rows):
            full_ref[here, 0:256] = rows

        if last:
            landed = pick_rows(recv_ref[here, :], rows_ref[...])
        else:
            landed = mm(one_hot_rows(recv_ref[0], run * WINDOW_SLOTS, WINDOW_SLOTS), rows_ref[...])
        state = landed[:, :128]
        pos = pos_ref[here, :].astype(F32) if last else landed[:, 128:]
        yield
        branch = yield from attend_stages(
            run,
            state.astype(BF16),
            (state + pos).astype(BF16),
            bucket_ref[here, :].astype(F32),
            bucket_row_ref[run],
            heads_ref,
            weights_ref,
            low,
            full,
        )
        if not last:
            leave_ref[here, :] = branch
            return
        yield
        resid = state + branch.astype(F32)
        full_ref[here, 256:384] = resid
        expand, contract, vecs = feed_weights(weights_ref)
        second = (yield from feed_forward(resid, expand, contract, vecs))[-1]
        yield
        unit, _ = centred_rows(second)
        leave_ref[here, :] = (unit * vecs[5:6, :] + vecs[6:7, :]).astype(BF16)

    low_copies = [kept_copy(0, g, STORE_BOUNDS, low_far, low_ref, sems, True) for g in range(len(STORE_BOUNDS) - 1)]
    full_copies = [kept_copy(1, g, STORE_BOUNDS, full_far, full_ref, sems, True) for g in range(len(STORE_BOUNDS) - 1)]
    ahead = [(STORE_BOUNDS[g + 1] + 3, copy.start) for g, copy in enumerate(low_copies)]
    ahead += [(STORE_BOUNDS[g + 1] + 6, copy.start) for g, copy in enumerate(full_copies)]
    interleave(NSUB, one_run, ahead)
    recv_copy.wait()
    land_rows(recv_col_ref, leave_ref[...], send_ref)
    for copy in low_copies + full_copies:
        copy.wait()


def owner_back_kernel(
    last,
    late,
    slot_col_ref,
    heads_ref,
    unfold_ref,
    weights_ref,
    grads_ref,
    *rest,
):
    if not last:
        dexpand_ref, *rest = rest
    recv_col_far, low_far, full_far, send_ref, *rest = rest
    if last:
        dwin_ref, dwout_ref, dexpand_ref, dcontract_ref, dvecs_ref, *rest = rest
        active_ref, douter_ref, first_ref, dinner_ref, *rest = rest
        ffn_refs = (active_ref, douter_ref, first_ref, dinner_ref)
    else:
        dwin_ref, dwout_ref, flat_ref, *rest = rest
    (
        attended_ref,
        dbranch_ref,
        dqkv_ref,
        drows_ref,
        low_ref,
        full_ref,
        recv_col_ref,
        sems,
        recv_sem,
    ) = rest
    scratch = (attended_ref, dbranch_ref, dqkv_ref)
    ahead = []
    bounds = LOAD_BOUNDS[1 if last else 0]
    for g, first in enumerate(bounds[:-1]):
        for k, far, near in ((1, full_far, full_ref), (0, low_far, low_ref)):
            copy = kept_copy(k, g, bounds, far, near, sems, False)
            copy.start()
            ahead.append((first if last else first + 1, copy.wait))
    recv_copy = pltpu.make_async_copy(recv_col_far, recv_col_ref, recv_sem.at[0])
    recv_copy.start()
    dvecs = []

    def one_run(run):
        here = run_rows(run)

        grad = dbranch_ref[here, :]
        if last:
            grad = grad.astype(F32)
            dresid = yield from feed_back(
                here, full_ref[here, 256:384], grad, weights_ref, ffn_refs, dvecs
            )
            dbranch = dresid.astype(BF16)
            dbranch_ref[here, :] = dbranch
        else:
            dbranch = grad

        drows = yield from attend_back_stages(
            run, dbranch, heads_ref, unfold_ref, weights_ref, low_ref, full_ref, scratch
        )
        if last:
            drows = (dresid + drows.astype(F32)).astype(BF16)
        drows_ref[here, :] = drows

    for run in range(NSUB):
        here = run_rows(run)
        dbranch_ref[here, :] = pick_rows(slot_col_ref[here, :], grads_ref[...]).astype(BF16)
    interleave(NSUB, one_run, ahead)
    recv_copy.wait()
    drows = drows_ref[...]
    if last:
        dvecs_ref[...] = sum(dvecs)
        land_rows(recv_col_ref, drows, send_ref)
        projection_grads(low_ref, scratch, dwin_ref, dwout_ref)
        dcontract_ref[...] = mm(active_ref[...], douter_ref[...], TN)
        dexpand_ref[...] = mm(first_ref[...], dinner_ref[...], TN)
        return
    projection_grads(low_ref, scratch, dwin_ref, dwout_ref)
    devices, rows, _ = send_ref.shape
    capacity = recv_col_ref.shape[0] // devices
    for c in range(recv_col_ref.shape[0] // 128):
        sent = pick_rows(recv_col_ref[c * 128 : c * 128 + 128, :], drows).astype(BF16)
        for part in range(128 // capacity):
            send_ref[c * 128 // capacity + part, 0:capacity, :] = sent[
                part * capacity : part * capacity + capacity
            ]
    share, quarter_rows = late
    store_projections(flat_ref, 0, dwin_ref, dwout_ref)
    for j in range(2):
        flat_ref[pl.ds(512 + j, 8, stride=2), :] = dexpand_ref[0:8, 128 * j : 128 * j + 128]
    flat_ref[pl.ds(528, flat_ref.shape[0] - 528), :] = jnp.zeros(
        (flat_ref.shape[0] - 528, 128), F32
    )
    owners = devices // 4
    for device in range(devices):
        quarter, owner = divmod(device, owners)
        block = share_block(
            flat_ref, owner * share, share, quarter * quarter_rows, rows - capacity, quarter_rows
        )
        send_ref[device, capacity:rows, :] = block.astype(BF16)


def share_block(flat_ref, start, share, first_row, rows, used_rows):
    row, shift = divmod(start, 128)
    row = row + first_row
    lane = iota((rows, 128), 1)
    line = iota((rows, 128), 0)
    block = flat_ref[pl.ds(row, rows), :]
    if shift:
        after = flat_ref[pl.ds(row + 1, rows), :]
        block = pltpu.roll(jnp.where(lane >= shift, block, after), 128 - shift, 1)
    inside = (line < used_rows) & ((line + first_row) * 128 + lane < share)
    return jnp.where(inside, block, 0.0)


def store_projections(flat_ref, base, dwin_ref, dwout_ref):
    for j in range(3):
        flat_ref[pl.ds(base + j, 128, stride=3), :] = dwin_ref[:, 128 * j : 128 * j + 128]
    flat_ref[pl.ds(base + 384, 128), :] = dwout_ref[...]


def centred_rows(rows):
    centre = rows - jnp.mean(rows, axis=-1, keepdims=True)
    spread = jnp.mean(centre * centre, axis=-1, keepdims=True)
    inverse = lax.rsqrt(spread + 1e-05)
    return centre * inverse, inverse


def norm_back(grad, gain, unit, inverse):
    dunit = grad * gain
    return (
        dunit
        - jnp.mean(dunit, axis=-1, keepdims=True)
        - unit * jnp.mean(dunit * unit, axis=-1, keepdims=True)
    ) * inverse


def feed_forward(resid, expand, contract, vecs):
    unit, inverse = centred_rows(resid)
    first = unit * vecs[3:4, :] + vecs[4:5, :]
    first_low = first.astype(BF16)
    bias = jnp.concatenate([vecs[0:1, :], vecs[1:2, :]], axis=1)
    inner = mm(first_low, expand) + bias
    yield
    below = 0.5 + 0.5 * lax.erf(inner * math.sqrt(0.5))
    active = (inner * below).astype(BF16)
    second = first + (mm(active, contract) + vecs[2:3, :])
    return unit, inverse, first_low, inner, below, active, second


def feed_back(here, resid, grad, weights_ref, ffn_refs, dvecs):
    active_ref, douter_ref, first_ref, dinner_ref = ffn_refs
    expand, contract, vecs = feed_weights(weights_ref)
    unit_first, inverse_first, first_low, inner, below, active, second = yield from feed_forward(
        resid, expand, contract, vecs
    )
    active_ref[here, :] = active
    first_ref[here, :] = first_low
    yield
    unit, inverse = centred_rows(second)
    dsecond = norm_back(grad, vecs[5:6, :], unit, inverse)
    douter = dsecond.astype(BF16)
    douter_ref[here, :] = douter
    dactive = mm(douter, contract, NT)
    slope = below + inner * (jnp.exp(-0.5 * inner * inner) * (1.0 / math.sqrt(2.0 * math.pi)))
    yield
    dinner = (dactive * slope).astype(BF16)
    dinner_ref[here, :] = dinner
    dfirst = mm(dinner, expand, NT) + dsecond
    yield

    def down(rows):
        return jnp.sum(rows, axis=0, keepdims=True)

    dbias = down(dinner.astype(F32))
    dvecs.append(
        jnp.concatenate(
            [
                dbias[:, :128],
                dbias[:, 128:],
                down(douter.astype(F32)),
                down(dfirst * unit_first),
                down(dfirst),
                down(grad * unit),
                down(grad),
                jnp.zeros((1, 128), F32),
            ],
            axis=0,
        )
    )
    return norm_back(dfirst, vecs[3:4, :], unit_first, inverse_first)


ROWS = 128


def part_rows(part):
    return pl.ds(part * ROWS, ROWS)


def home_forward_kernel(
    route_col_ref,
    place_col_ref,
    branch_ref,
    state_ref,
    weights_ref,
    send_ref,
    resid_ref,
    result_ref,
):
    def some_rows(part):
        here = part_rows(part)
        expand, contract, vecs = feed_weights(weights_ref)
        resid = state_ref[here, :].astype(F32) + pick_rows(route_col_ref[here, :], branch_ref[...])
        yield
        resid_ref[here, :] = resid
        second = (yield from feed_forward(resid, expand, contract, vecs))[-1]
        yield
        unit, _ = centred_rows(second)
        result_ref[here, :] = (unit * vecs[5:6, :] + vecs[6:7, :]).astype(BF16)

    interleave(result_ref.shape[0] // ROWS, some_rows)
    place_rows(place_col_ref, result_ref[...], send_ref)


def home_backward_kernel(
    route_col_ref,
    arrived_ref,
    resid_ref,
    weights_ref,
    place_col_far,
    dresid_ref,
    send_ref,
    dexpand_ref,
    dcontract_ref,
    dvecs_ref,
    active_ref,
    douter_ref,
    first_ref,
    dinner_ref,
    low_ref,
    place_col_ref,
    sem,
):
    place_copy = pltpu.make_async_copy(place_col_far, place_col_ref, sem.at[0])
    place_copy.start()
    ffn_refs = (active_ref, douter_ref, first_ref, dinner_ref)
    dvecs = []

    def some_rows(part):
        here = part_rows(part)
        grad = pick_rows(route_col_ref[here, :], arrived_ref[...])
        yield
        dresid = yield from feed_back(
            here, resid_ref[here, :], grad, weights_ref, ffn_refs, dvecs
        )
        dresid_ref[here, :] = dresid
        low_ref[here, :] = dresid.astype(BF16)

    interleave(dresid_ref.shape[0] // ROWS, some_rows)
    dvecs_ref[...] = sum(dvecs)
    place_copy.wait()
    place_rows(place_col_ref, low_ref[...], send_ref)
    dcontract_ref[...] = mm(active_ref[...], douter_ref[...], TN)
    dexpand_ref[...] = mm(first_ref[...], dinner_ref[...], TN)


def take_kernel(route_col_ref, arrived_ref, out_ref):
    for part in range(out_ref.shape[0] // ROWS):
        here = part_rows(part)
        out_ref[here, :] = pick_rows(route_col_ref[here, :], arrived_ref[...]).astype(BF16)


def finish_kernel(route_col_ref, arrived_ref, dresid_ref, out_ref, rows_ref):
    devices, rows, _ = arrived_ref.shape
    capacity = rows_ref.shape[0] // devices
    for device in range(devices):
        rows_ref[device * capacity : (device + 1) * capacity, :] = arrived_ref[
            device, 0:capacity, :
        ]
    for part in range(out_ref.shape[0] // ROWS):
        here = part_rows(part)
        out_ref[here, :] = dresid_ref[here, :] + pick_rows(route_col_ref[here, :], rows_ref[...])


def late_kernel(quarter_rows, me_ref, early_ref, arrived_ref, *refs):
    outs, parts_ref = refs[:4], refs[4]
    devices, rows, _ = arrived_ref.shape
    late_rows = outs[0].shape[0]
    capacity = rows - late_rows
    late = arrived_ref[0, capacity:rows, :].astype(F32)
    for device in range(1, devices):
        late = late + arrived_ref[device, capacity:rows, :].astype(F32)
    early = early_ref[...]
    square = jnp.sum(early * early) + jnp.sum(late * late)
    line = iota((late_rows, 128), 0)
    parts_ref[0] = jnp.where(line < quarter_rows, late, square)
    for part in range(3):
        piece = early_ref[pl.ds(part * quarter_rows, quarter_rows), :]
        parts_ref[part + 1, 0:quarter_rows, :] = piece
        parts_ref[part + 1, quarter_rows:late_rows, :] = jnp.full(
            (late_rows - quarter_rows, 128), square, F32
        )
    quarter = me_ref[0] // (devices // 4)
    for k, out_ref in enumerate(outs):
        out_ref[...] = parts_ref[quarter ^ k]


def unpack_kernel(share, me_ref, shards_ref, *rest):
    flat_ref = rest[-1]
    outs = rest[:-1]
    devices, block_rows, _ = shards_ref.shape
    lane = iota((block_rows, 128), 1)
    me = me_ref[0]
    for device in range(devices):
        row, shift = divmod(device * share, 128)
        block = shards_ref[me ^ device].astype(F32)
        if shift:
            block = pltpu.roll(block, shift, 1)
            before = jnp.concatenate([flat_ref[pl.ds(row, 1), :], block[:-1]], axis=0)
            block = jnp.where(lane >= shift, block, before)
        flat_ref[pl.ds(row, block_rows), :] = block
    for layer, out_ref in enumerate(outs):
        base = layer * LAYER_ROWS
        for j in range(3):
            out_ref[128 * j : 128 * j + 128, :] = flat_ref[pl.ds(base + j, 128, stride=3), :].astype(
                BF16
            )
        out_ref[384:512, :] = flat_ref[pl.ds(base + 384, 128), :].astype(BF16)
        for j in range(2):
            out_ref[512 + 128 * j : 640 + 128 * j, :] = flat_ref[
                pl.ds(base + 512 + j, 128, stride=2), :
            ].astype(BF16)
        out_ref[768:1024, :] = flat_ref[pl.ds(base + 768, 256), :].astype(BF16)
        vecs = flat_ref[pl.ds(base + 1024, 16), :]
        out_ref[1024:1040, :] = jnp.where(iota((16, 128), 0) < 7, vecs, 0.0).astype(BF16)


def pack_kernel(
    share,
    quarter_rows,
    dwin_ref,
    dwout_ref,
    dexpand_ref,
    dcontract_ref,
    dvecs_ref,
    dexpand_zero_ref,
    dcontract_zero_ref,
    dvecs_zero_ref,
    out_ref,
    flat_ref,
    block_ref,
):
    devices, early_rows, _ = out_ref.shape
    flat_ref[0:512, :] = jnp.zeros((512, 128), F32)
    store_projections(flat_ref, LAYER_ROWS, dwin_ref, dwout_ref)
    for base, expand, contract, vecs in (
        (0, dexpand_zero_ref, dcontract_zero_ref, dvecs_zero_ref),
        (LAYER_ROWS, dexpand_ref, dcontract_ref, dvecs_ref),
    ):
        for j in range(2):
            flat_ref[pl.ds(base + 512 + j, 128, stride=2), :] = expand[:, 128 * j : 128 * j + 128]
        flat_ref[pl.ds(base + 768, 256), :] = contract[...]
        flat_ref[pl.ds(base + 1024, 7), :] = vecs[0:7, :]
    end = LAYERS * LAYER_ROWS
    flat_ref[pl.ds(end, flat_ref.shape[0] - end), :] = jnp.zeros(
        (flat_ref.shape[0] - end, 128), F32
    )
    owners = devices // 4
    block_ref[...] = jnp.zeros_like(block_ref)
    for device in range(devices):
        quarter, owner = divmod(device, owners)
        for part in range(3):
            start = ((part + 1) * owners + owner) * share
            first_row = quarter * quarter_rows
            block_ref[pl.ds(part * quarter_rows, quarter_rows), :] = share_block(
                flat_ref, start, share, first_row, quarter_rows, quarter_rows
            )
        out_ref[device] = block_ref[...].astype(BF16)


def call(
    name,
    micros,
    body,
    outs,
    *args,
    fresh=(),
    scratch=(),
    vmem=24,
    smem=0,
    far_in=0,
    far_out=0,
    sems=(),
):
    near = pl.BlockSpec(memory_space=pltpu.VMEM)
    far = pl.BlockSpec(memory_space=pltpu.HBM)
    specs = [pl.BlockSpec(memory_space=pltpu.SMEM)] * smem
    specs += [near] * (len(args) - smem - far_in) + [far] * far_in
    args = [
        x if i < smem or i in fresh else pltpu.with_memory_space_constraint(x, pltpu.HBM)
        for i, x in enumerate(args)
    ]
    return pl.pallas_call(
        body,
        out_shape=tuple(
            shape_of(o[0], o[1]) if len(o) == 2 else pltpu.HBM(o[0], o[1]) for o in outs
        ),
        in_specs=specs,
        out_specs=tuple([near] * (len(outs) - far_out) + [far] * far_out),
        scratch_shapes=[pltpu.VMEM(s[0], s[1]) for s in scratch]
        + [pltpu.SemaphoreType.DMA(s) for s in sems],
        compiler_params=pltpu.CompilerParams(vmem_limit_bytes=vmem << 20),
        cost_estimate=pl.CostEstimate(
            flops=int(micros * 1e9), bytes_accessed=1 << 16, transcendentals=0
        ),
        name=name,
    )(*args)


def exchange(buffer):
    return lax.all_to_all(buffer, AXES, split_axis=0, concat_axis=0, tiled=True)


def swapped(value, pair, devices, k):
    step = (pair[-1] if k & 1 else 0) ^ (pair[0] if k & 2 else 0)
    return lax.ppermute(value, AXES, [(i, i ^ step) for i in range(devices)])


def paired(parts):
    while len(parts) > 1:
        parts = [parts[i] + parts[i + 1] for i in range(0, len(parts), 2)]
    return parts[0]


def after(value, *others):
    return lax.optimization_barrier((value, *others))[0]


def shards(
    tokens,
    positions,
    cotangent,
    route_send,
    recv_slot,
    slot_bucket,
    master,
    first_moment,
    second_moment,
):
    devices = lax.axis_size("grp") * lax.axis_size("win")
    me = lax.axis_index(AXES)
    home = tokens.shape[0]
    arrivals = recv_slot.shape[2]
    share = master.shape[0]
    share_rows = -(-share // 128)
    block_rows = -(-share_rows // 8) * 8
    quarter_rows = -(-share_rows // 4)
    late_rows = -(-(quarter_rows + 1) // 8) * 8
    early_rows = -(-3 * quarter_rows // 8) * 8
    capacity = arrivals // devices
    width = PILLAR_WIDTH
    flat_rows = -(-(((devices - 1) * share) // 128 + block_rows + 8) // 8) * 8
    late_flat_rows = -(-max(536, ((devices // 4) * share) // 128 + late_rows + 16) // 8) * 8

    heads, unfold, *tables = call(
        "tables",
        4,
        tables_kernel,
        (((EXPANDED, 128), BF16, True), ((WINDOW_SLOTS, 256), BF16, True))
        + (
            ((home, 128), jnp.int16, True),
            ((arrivals, 128), jnp.int16, True),
            ((DEVICE_SLOTS + 64, 128), BF16, True),
            ((NSUB, 2, 128), F32, True),
        )
        * LAYERS,
        route_send,
        recv_slot,
        slot_bucket,
    )
    route_col, recv_col, bucket, bucket_row = (tables[k::4] for k in range(4))
    (send,) = call(
        "start",
        3,
        start_kernel,
        (((arrivals, 2 * width), BF16),),
        route_send,
        tokens,
        positions,
    )
    pos_send, cotangent_send = call(
        "start_next",
        3,
        start_next_kernel,
        (((arrivals, width), BF16, True), ((arrivals, width), BF16, True)),
        route_send,
        positions,
        cotangent,
    )

    copies = jnp.pad(master.astype(BF16), (0, block_rows * 128 - share)).reshape(1, block_rows, 128)
    bits = [devices >> (i + 1) for i in range(devices.bit_length() - 1)]
    for i in range(0, len(bits), 2):
        pair = bits[i : i + 2]
        others = [swapped(copies, pair, devices, k) for k in range(1, 2 ** len(pair))]
        copies = jnp.stack([copies, *others], axis=1).reshape(-1, block_rows, 128)
        if copies.shape[0] == 4:
            arrived = exchange(after(send, copies))
    params = call(
        "unpack",
        2,
        functools.partial(unpack_kernel, share),
        (((1040, width), BF16, True),) * LAYERS,
        me.reshape(1),
        copies,
        scratch=(((flat_rows, 128), F32),),
        smem=1,
    )
    kept_zero = (
        ((DEVICE_SLOTS, 640 + EXPANDED), BF16, True),
        ((DEVICE_SLOTS, 2 * width), F32, True),
    )
    kept_one = (kept_zero[0], ((DEVICE_SLOTS, 3 * width), F32, True))
    recv_col_shape = ((arrivals, 128), jnp.int16)
    slots_low = ((DEVICE_SLOTS, width), BF16)
    slots_wide = ((DEVICE_SLOTS, FF), BF16)
    back_scratch = (slots_low, slots_low, ((DEVICE_SLOTS, 3 * width), BF16))
    arrival_shape = ((arrivals, width), BF16)

    pos_arrived = exchange(after(pos_send, arrived))
    def owner(layer, rows, *pos):
        kept = (kept_zero, kept_one)[layer]
        return call(
            ("first_owner", "last_owner")[layer],
            (13, 18)[layer],
            functools.partial(owner_kernel, layer == 1),
            (arrival_shape, *kept),
            slot_col[1] if layer else recv_slot,
            bucket[layer],
            bucket_row[layer],
            heads,
            params[layer],
            rows,
            *pos,
            recv_col[layer],
            fresh=(5,),
            scratch=(slots_low, *kept, recv_col_shape),
            far_in=1,
            far_out=2,
            sems=((2, len(STORE_BOUNDS) - 1), (1,)),
            vmem=40,
        )

    send, *stored_zero = owner(0, arrived)
    inverse = call(
        "inverse",
        6,
        inverse_kernel,
        (
            ((DEVICE_SLOTS + 64, 128), jnp.int16, True),
            ((arrivals, 128), jnp.int16, True),
        )
        * LAYERS,
        after(route_send, stored_zero[1]),
        recv_slot,
    )
    slot_col, place_col = inverse[0::2], inverse[1::2]
    branch = exchange(after(send, pos_arrived))
    (pos_slots,) = call(
        "slots", 4, slots_kernel, ((*slots_low, True),), slot_col[1], pos_arrived
    )
    send, resid_zero = call(
        "home",
        8,
        home_forward_kernel,
        (arrival_shape, ((home, width), F32, True)),
        route_col[0],
        place_col[1],
        branch,
        tokens,
        params[0],
        fresh=(2,),
        scratch=(((home, width), BF16),),
    )
    arrived = exchange(send)
    cotangent_arrived = exchange(after(cotangent_send, arrived))
    send, *stored_one = owner(1, arrived, pos_slots)
    mixed_arrived = exchange(after(send, cotangent_arrived))
    send, *grads_one = call(
        "last_owner_back",
        22,
        functools.partial(owner_back_kernel, True, None),
        (
            arrival_shape,
            ((width, 3 * width), F32, True),
            ((width, width), F32, True),
            ((width, FF), F32, True),
            ((FF, width), F32, True),
            ((8, width), F32, True),
        ),
        slot_col[1],
        heads,
        unfold,
        params[1],
        cotangent_arrived,
        recv_col[1],
        *stored_one,
        scratch=(
            slots_wide,
            slots_low,
            slots_low,
            slots_wide,
            *back_scratch,
            slots_low,
            *kept_one,
            recv_col_shape,
        ),
        far_in=3,
        sems=((2, len(LOAD_BOUNDS[1]) - 1), (1,)),
        vmem=40,
    )
    arrived = exchange(after(send, mixed_arrived))
    (mixed,) = call(
        "take", 2, take_kernel, (((home, width), BF16),), route_col[1], mixed_arrived
    )
    dresid, send, *ffn_zero = call(
        "home_back",
        10,
        home_backward_kernel,
        (
            ((home, width), F32, True),
            arrival_shape,
            ((width, FF), F32, True),
            ((FF, width), F32, True),
            ((8, width), F32, True),
        ),
        route_col[1],
        arrived,
        resid_zero,
        params[0],
        place_col[0],
        fresh=(1,),
        far_in=1,
        sems=((1,),),
        scratch=(
            ((home, FF), BF16),
            ((home, width), BF16),
            ((home, width), BF16),
            ((home, FF), BF16),
            ((home, width), BF16),
            recv_col_shape,
        ),
    )
    arrived = exchange(send)
    (packed,) = call(
        "pack",
        1,
        functools.partial(pack_kernel, share, quarter_rows),
        (((devices, early_rows, 128), BF16, True),),
        *grads_one,
        *ffn_zero,
        scratch=(((flat_rows, 128), F32), ((early_rows, 128), F32)),
    )
    early = exchange(after(packed, arrived))
    (send,) = call(
        "first_owner_back",
        16,
        functools.partial(owner_back_kernel, False, (share, quarter_rows)),
        (((devices, capacity + late_rows, width), BF16),),
        slot_col[0],
        heads,
        unfold,
        params[0],
        arrived,
        ffn_zero[0],
        recv_col[0],
        *stored_zero,
        fresh=(4,),
        scratch=(
            ((width, 3 * width), F32),
            ((width, width), F32),
            ((late_flat_rows, 128), F32),
            *back_scratch,
            slots_low,
            *kept_zero,
            recv_col_shape,
        ),
        far_in=3,
        sems=((2, len(LOAD_BOUNDS[0]) - 1), (1,)),
        vmem=40,
    )
    arrived = exchange(after(send, early))
    early = jnp.sum(early.astype(F32), axis=0)
    quarters = call(
        "late",
        1,
        functools.partial(late_kernel, quarter_rows),
        (((late_rows, 128), F32, True),) * 4,
        me.reshape(1),
        after(early, mixed),
        arrived,
        fresh=(2,),
        scratch=(((4, late_rows, 128), F32),),
        smem=1,
    )
    (tokens_grad,) = call(
        "finish",
        3,
        finish_kernel,
        (((home, width), F32),),
        route_col[0],
        arrived,
        dresid,
        fresh=(1,),
        scratch=(((arrivals, width), BF16),),
    )
    quarters = [quarters[0]] + [
        swapped(quarters[k], bits[:2], devices, k) for k in range(1, 4)
    ]
    square = after(paired([q[quarter_rows:] for q in quarters]), tokens_grad)
    for i in range(2, len(bits), 2):
        pair = bits[i : i + 2]
        square = paired(
            [square] + [swapped(square, pair, devices, k) for k in range(1, 2 ** len(pair))]
        )
    total = jnp.sqrt(square[0, 0])
    quarters = jnp.stack([q[:quarter_rows] for q in quarters])
    quarter = me // (devices // 4)
    for bit in (1, 2):
        other = quarters.reshape(4 // (2 * bit), 2, bit, quarter_rows, 128)[:, ::-1]
        quarters = jnp.where(quarter & bit, other.reshape(quarters.shape), quarters)
    shard = quarters.reshape(-1)[:share]
    clip_limit = 0.25 * math.sqrt(NPARAM)
    factor = jnp.minimum(1.0, clip_limit / (total + 1e-06))
    clipped = shard * factor
    new_first = beta_one * first_moment + (1.0 - beta_one) * clipped
    new_second = beta_two * second_moment + (1.0 - beta_two) * clipped * clipped
    first_hat = new_first / (1.0 - beta_one**adam_step)
    second_hat = new_second / (1.0 - beta_two**adam_step)
    new_master = master - rate * (first_hat / (jnp.sqrt(second_hat) + adam_eps) + decay * master)
    return (
        mixed,
        tokens_grad,
        total.reshape(1),
        clipped,
        new_master,
        new_first,
        new_second,
        new_master.astype(BF16),
    )


def solution(mesh):
    in_specs = (
        P(("grp", "win"), None),
        P(None, ("grp", "win"), None),
        P(("grp", "win"), None),
        P(None, ("grp", "win")),
        P(None, ("grp", "win"), None),
        P(None, ("grp", "win")),
        P(("grp", "win")),
        P(("grp", "win")),
        P(("grp", "win")),
    )
    out_specs = (
        P(("grp", "win"), None),
        P(("grp", "win"), None),
        P(),
        P(("grp", "win")),
        P(("grp", "win")),
        P(("grp", "win")),
        P(("grp", "win")),
        P(("grp", "win")),
    )
    return jax.shard_map(shards, mesh=mesh, in_specs=in_specs, out_specs=out_specs, check_vma=False)
```

```python
import functools
import math

import jax
import jax.numpy as jnp
from jax import lax
from jax.experimental import pallas as pl
from jax.experimental.pallas import tpu as pltpu
from jax.sharding import PartitionSpec as P

PILLAR_WIDTH = 128
FF = 256
HEAD_COUNT = 8
HDIM = 16
WINDOW_SLOTS = 144
LAYERS = 2
DEVICE_SLOTS = 1728
NSUB = 12
NPARAM = 263936
LAYER_ROWS = 1031
EXPANDED = HEAD_COUNT * WINDOW_SLOTS
MASKED = -1e30
LOWEST = -3e38

beta_one = 0.5
beta_two = 0.5
adam_step = 4
rate = 0.1
decay = 0.01
adam_eps = 1e-08

BF16 = jnp.bfloat16
F32 = jnp.float32
AXES = ("grp", "win")

NN = (((1,), (0,)), ((), ()))
NT = (((1,), (1,)), ((), ()))
TN = (((0,), (0,)), ((), ()))


def mm(left, right, dims=NN):
    return lax.dot_general(left, right, dims, preferred_element_type=F32)


def iota(shape, dim):
    return lax.broadcasted_iota(jnp.int32, shape, dim)


def shape_of(shape, dtype):
    return jax.ShapeDtypeStruct(shape, dtype)


def one_hot_rows(row_ids, first, count):
    return jnp.where(iota((count, row_ids.shape[1]), 0) + first == row_ids, 1.0, 0.0).astype(BF16)


def one_hot_columns(column_ids, width):
    lane = iota(column_ids.shape, 1)
    pieces = [
        jnp.where(column_ids == lane + 128 * k, 1.0, 0.0).astype(BF16)
        for k in range(-(-width // 128))
    ]
    return jnp.concatenate(pieces, axis=1)[:, :width]


def expand_heads(block, heads):
    main = block[:128]
    tail = block[128:]
    return jnp.concatenate([main] * HEAD_COUNT + [tail] * HEAD_COUNT, axis=0) * heads


def pick_rows(column_ids, source):
    half = source.shape[0] // 2
    column_ids = column_ids.astype(jnp.int32)
    upper = column_ids >= half
    local = jnp.where(upper, column_ids - half, column_ids)
    both = mm(one_hot_columns(local, half), jnp.concatenate([source[:half], source[half:]], axis=1))
    return jnp.where(upper, both[:, 128:], both[:, :128])


def inverse_kernel(route_ref, recv_ref, *outs):
    for layer in range(LAYERS):
        for ids, out_ref in (
            (recv_ref[layer], outs[2 * layer]),
            (route_ref[layer : layer + 1, :], outs[2 * layer + 1]),
        ):
            place = iota((ids.shape[1], 128), 0) + 1
            parts = jnp.concatenate(
                [(place >> 6).astype(F32).astype(BF16), (place & 63).astype(F32).astype(BF16)], axis=1
            )
            for c in range(out_ref.shape[0] // 128):
                found = mm(one_hot_rows(ids, c * 128, 128), parts)
                found = found[:, :128] * 64.0 + found[:, 128:] - 1.0
                out_ref[c * 128 : (c + 1) * 128, :] = found.astype(jnp.int32).astype(jnp.int16)


def place_rows(place_col_ref, low_rows, send, chunk=256):
    for c in range(send.shape[0] // chunk):
        part = slice(c * chunk, (c + 1) * chunk)
        send[part, :] = pick_rows(place_col_ref[part, :], low_rows).astype(BF16)


def scatter_rows(route_row, low_rows, send, chunk=256):
    for c in range(send.shape[0] // chunk):
        hot = one_hot_rows(route_row, c * chunk, chunk)
        send[c * chunk : (c + 1) * chunk, :] = mm(hot, low_rows).astype(BF16)


def land_rows(recv_col, slot_values, send, chunk=128):
    for c in range(send.shape[0] // chunk):
        part = slice(c * chunk, (c + 1) * chunk)
        send[part, :] = pick_rows(recv_col[part, :], slot_values).astype(BF16)


def on_lanes(row, out_type):
    here = iota((128, 128), 0) == iota((128, 128), 1)
    spread = jnp.where(here, jnp.broadcast_to(row, (128, 128)), 0)
    ones = jnp.ones((128, 128), BF16)
    if out_type == BF16:
        return mm(spread.astype(F32).astype(BF16), ones).astype(BF16)
    high = mm((spread >> 6).astype(F32).astype(BF16), ones)
    low = mm((spread & 63).astype(F32).astype(BF16), ones)
    return (high * 64.0 + low).astype(jnp.int32).astype(out_type)


def tables_kernel(route_ref, recv_ref, bucket_ref, heads_ref, unfold_ref, *outs):
    slot = iota((EXPANDED, 128), 0)
    head = jnp.where(slot < 1024, slot >> 7, (slot - 1024) >> 4)
    heads_ref[...] = jnp.where(head == iota((EXPANDED, 128), 1) >> 4, 1.0, 0.0).astype(BF16)
    wide = iota((WINDOW_SLOTS, 256), 1)
    wide = jnp.where(wide < 128, wide, 128 + (wide & 15))
    unfold_ref[...] = jnp.where(iota((WINDOW_SLOTS, 256), 0) == wide, 1.0, 0.0).astype(BF16)
    for layer in range(LAYERS):
        route_col_ref, recv_col_ref, bucket_col_ref, bucket_row_ref = outs[4 * layer : 4 * layer + 4]
        bucket = bucket_ref[layer : layer + 1, :]
        for ids, out_ref in (
            (route_ref[layer : layer + 1, :], route_col_ref),
            (recv_ref[layer], recv_col_ref),
            (jnp.concatenate([bucket, bucket[:, :64]], axis=1), bucket_col_ref),
        ):
            for c in range(out_ref.shape[0] // 128):
                part = slice(c * 128, (c + 1) * 128)
                out_ref[part, :] = on_lanes(ids[:, part], out_ref.dtype)
        bucket = bucket.astype(F32)
        for run in range(NSUB):
            base = run * WINDOW_SLOTS
            tail = bucket[:, base + 128 : base + 144]
            bucket_row_ref[run] = jnp.concatenate(
                [bucket[:, base : base + 128], jnp.concatenate([tail] * 8, axis=1)], axis=0
            )


def start_kernel(route_ref, tokens_ref, pos_ref, out_ref):
    both = jnp.concatenate([tokens_ref[...], pos_ref[0]], axis=1)
    scatter_rows(route_ref[0:1, :], both, out_ref)


def start_next_kernel(route_ref, pos_ref, cotangent_ref, pos_out_ref, cotangent_out_ref):
    both = jnp.concatenate([pos_ref[1], cotangent_ref[...]], axis=1)
    for c in range(pos_out_ref.shape[0] // 256):
        part = slice(c * 256, (c + 1) * 256)
        sent = mm(one_hot_rows(route_ref[1:2, :], c * 256, 256), both).astype(BF16)
        pos_out_ref[part, :] = sent[:, :128]
        cotangent_out_ref[part, :] = sent[:, 128:]


def slots_kernel(slot_col_ref, rows_ref, out_ref):
    for run in range(NSUB):
        part = slice(run * WINDOW_SLOTS, (run + 1) * WINDOW_SLOTS)
        out_ref[part, :] = pick_rows(slot_col_ref[part, :], rows_ref[...]).astype(BF16)


def project_in(weights_ref):
    return jnp.concatenate([weights_ref[128 * j : 128 * j + 128, :] for j in range(3)], axis=1)


def project_out(weights_ref):
    return weights_ref[384:512, :]


def feed_weights(weights_ref):
    expand = jnp.concatenate([weights_ref[512:640, :], weights_ref[640:768, :]], axis=1)
    return expand, weights_ref[768:1024, :], weights_ref[1024:1040, :].astype(F32)


def interleave(count, make, ahead=()):
    waiting = [make(i) for i in range(count)]
    running = []
    turn = 0
    while waiting or running:
        for when, act in ahead:
            if when == turn:
                act()
        if waiting:
            running.insert(0, waiting.pop(0))
        running = [part for part in running if next(part, running) is not running]
        turn += 1
    for when, act in ahead:
        if when >= turn:
            act()


def run_rows(run):
    return pl.ds(run * WINDOW_SLOTS, WINDOW_SLOTS)


STORE_BOUNDS = tuple(range(NSUB + 1))
LOAD_BOUNDS = ((0, 4, 12), (0, 3, 7, 12))


def kept_copy(k, group, bounds, far, near, sems, out):
    first, last = bounds[group : group + 2]
    here = pl.ds(first * WINDOW_SLOTS, (last - first) * WINDOW_SLOTS)
    far, near = far.at[here, :], near.at[here, :]
    ends = (near, far) if out else (far, near)
    return pltpu.make_async_copy(*ends, sems.at[k, group])


def attend_stages(run, slot_rows, joined, bucket, bucket_row, heads_ref, weights_ref, low, full):
    win = project_in(weights_ref)
    query_key = mm(joined, win[:, :256])
    queries = (query_key[:, :128] * 0.25).astype(BF16)
    keys = query_key[:, 128:].astype(BF16)
    values = mm(slot_rows, win[:, 256:]).astype(BF16)
    heads = heads_ref[...]
    block = heads[1024:]
    spread = jnp.concatenate(
        [
            queries * jnp.concatenate([heads[128 * h : 128 * h + 16]] * 9, axis=0)
            for h in range(HEAD_COUNT)
        ],
        axis=0,
    )
    yield
    scores = mm(spread, keys[:128], NT)
    tail = mm(queries, jnp.concatenate([keys[128:]] * 8, axis=0) * block, NT)
    yield

    def same(row):
        return jnp.where((bucket == row) & (row >= 0), 0.0, MASKED)

    main_bias = same(bucket_row[0:1, :])
    tail = tail + same(bucket_row[1:2, :])
    segment = iota((WINDOW_SLOTS, 128), 1) >> 4
    tail_top = jnp.zeros((WINDOW_SLOTS, 128), F32)
    pieces = []
    for h in range(HEAD_COUNT):
        main = scores[WINDOW_SLOTS * h : WINDOW_SLOTS * (h + 1)] + main_bias
        own_tail = segment == h
        top = jnp.max(jnp.maximum(main, jnp.where(own_tail, tail, LOWEST)), axis=1, keepdims=True)
        tail_top = jnp.where(own_tail, top, tail_top)
        pieces.append(jnp.exp(main - top).astype(BF16))
    pieces.append(jnp.exp(tail - tail_top).astype(BF16))
    expo = jnp.concatenate(pieces, axis=1)
    low(jnp.concatenate([joined, slot_rows, queries, keys, values, expo], axis=1))
    yield
    summed = mm(expo, jnp.concatenate([expand_heads(values, heads), heads], axis=1))
    yield
    share = jnp.where(bucket >= 0, 1.0, 0.0) / summed[:, 128:]
    attended = summed[:, :128] * share
    full(jnp.concatenate([attended, share], axis=1))
    return mm(attended.astype(BF16), project_out(weights_ref)).astype(BF16)


def attend_back_stages(
    run, dbranch, heads_ref, unfold_ref, weights_ref, low_ref, full_ref, scratch
):
    attended_ref, dbranch_ref, dqkv_ref = scratch
    here = run_rows(run)
    dattended = mm(dbranch, project_out(weights_ref), NT).astype(BF16).astype(F32)
    yield
    heads = heads_ref[...]
    block = heads[1024:]
    out = full_ref[here, 0:128]
    attended_ref[here, :] = out.astype(BF16)
    dout = (dattended * full_ref[here, 128:256]).astype(BF16)
    weighed = dout.astype(F32) * out
    weighed_high = weighed.astype(BF16)
    weighed_low = (weighed - weighed_high.astype(F32)).astype(BF16)
    centre = mm(weighed_high, block) + mm(weighed_low, block)
    queries = low_ref[here, 256:384]
    keys_wide = expand_heads(low_ref[here, 384:512], heads)
    dprob = mm(dout, expand_heads(low_ref[here, 512:640], heads), NT)
    yield
    expo = low_ref[here, 640:]
    pieces = [
        (
            (dprob[:, 128 * h : 128 * h + 128] - centre[:, 16 * h : 16 * h + 1])
            * expo[:, 128 * h : 128 * h + 128].astype(F32)
        ).astype(BF16)
        for h in range(HEAD_COUNT)
    ]
    pieces.append(((dprob[:, 1024:] - centre) * expo[:, 1024:].astype(F32)).astype(BF16))
    dscore = jnp.concatenate(pieces, axis=1)
    yield
    dqueries = (mm(dscore, keys_wide) * 0.25).astype(BF16)

    def gathered(left, right):
        wide = mm(left, right, TN)
        main = jnp.concatenate(
            [wide[16 * h : 16 * h + 16, 128 * h : 128 * h + 128] for h in range(HEAD_COUNT)],
            axis=0,
        )
        return jnp.concatenate([main, wide[:, 1024:] * block.astype(F32)], axis=1).astype(BF16)

    folded = jnp.concatenate([gathered(queries, dscore), gathered(dout, expo)], axis=0)
    yield
    dkeys_values = mm(unfold_ref[...], folded, NT).astype(BF16)
    dqkv = jnp.concatenate([dqueries, dkeys_values], axis=1)
    dqkv_ref[here, :] = dqkv
    yield
    return mm(dqkv, project_in(weights_ref), NT).astype(BF16)


def projection_grads(low_ref, scratch, dwin_ref, dwout_ref):
    attended_ref, dbranch_ref, dqkv_ref = scratch
    dwout_ref[...] = mm(attended_ref[...], dbranch_ref[...], TN)
    dqkv = dqkv_ref[...]
    dwin_ref[:, :256] = mm(low_ref[:, 0:128], dqkv[:, :256], TN)
    dwin_ref[:, 256:] = mm(low_ref[:, 128:256], dqkv[:, 256:], TN)


def owner_kernel(
    last,
    recv_ref,
    bucket_ref,
    bucket_row_ref,
    heads_ref,
    weights_ref,
    rows_ref,
    *rest,
):
    if last:
        pos_ref, *rest = rest
    (
        recv_col_far,
        send_ref,
        low_far,
        full_far,
        leave_ref,
        low_ref,
        full_ref,
        recv_col_ref,
        sems,
        recv_sem,
    ) = rest
    recv_copy = pltpu.make_async_copy(recv_col_far, recv_col_ref, recv_sem.at[0])
    recv_copy.start()

    def one_run(run):
        here = run_rows(run)

        def low(rows):
            low_ref[here, :] = rows

        def full(rows):
            full_ref[here, 0:256] = rows

        if last:
            landed = pick_rows(recv_ref[here, :], rows_ref[...])
        else:
            landed = mm(one_hot_rows(recv_ref[0], run * WINDOW_SLOTS, WINDOW_SLOTS), rows_ref[...])
        state = landed[:, :128]
        pos = pos_ref[here, :].astype(F32) if last else landed[:, 128:]
        yield
        branch = yield from attend_stages(
            run,
            state.astype(BF16),
            (state + pos).astype(BF16),
            bucket_ref[here, :].astype(F32),
            bucket_row_ref[run],
            heads_ref,
            weights_ref,
            low,
            full,
        )
        if not last:
            leave_ref[here, :] = branch
            return
        yield
        resid = state + branch.astype(F32)
        full_ref[here, 256:384] = resid
        expand, contract, vecs = feed_weights(weights_ref)
        second = (yield from feed_forward(resid, expand, contract, vecs))[-1]
        yield
        unit, _ = centred_rows(second)
        leave_ref[here, :] = (unit * vecs[5:6, :] + vecs[6:7, :]).astype(BF16)

    low_copies = [kept_copy(0, g, STORE_BOUNDS, low_far, low_ref, sems, True) for g in range(len(STORE_BOUNDS) - 1)]
    full_copies = [kept_copy(1, g, STORE_BOUNDS, full_far, full_ref, sems, True) for g in range(len(STORE_BOUNDS) - 1)]
    ahead = [(STORE_BOUNDS[g + 1] + 3, copy.start) for g, copy in enumerate(low_copies)]
    ahead += [(STORE_BOUNDS[g + 1] + 6, copy.start) for g, copy in enumerate(full_copies)]
    interleave(NSUB, one_run, ahead)
    recv_copy.wait()
    land_rows(recv_col_ref, leave_ref[...], send_ref)
    for copy in low_copies + full_copies:
        copy.wait()


def owner_back_kernel(
    last,
    late,
    slot_col_ref,
    heads_ref,
    unfold_ref,
    weights_ref,
    grads_ref,
    *rest,
):
    if not last:
        dexpand_ref, *rest = rest
    recv_col_far, low_far, full_far, send_ref, *rest = rest
    if last:
        dwin_ref, dwout_ref, dexpand_ref, dcontract_ref, dvecs_ref, *rest = rest
        active_ref, douter_ref, first_ref, dinner_ref, *rest = rest
        ffn_refs = (active_ref, douter_ref, first_ref, dinner_ref)
    else:
        dwin_ref, dwout_ref, flat_ref, *rest = rest
    (
        attended_ref,
        dbranch_ref,
        dqkv_ref,
        drows_ref,
        low_ref,
        full_ref,
        recv_col_ref,
        sems,
        recv_sem,
    ) = rest
    scratch = (attended_ref, dbranch_ref, dqkv_ref)
    ahead = []
    bounds = LOAD_BOUNDS[1 if last else 0]
    for g, first in enumerate(bounds[:-1]):
        for k, far, near in ((1, full_far, full_ref), (0, low_far, low_ref)):
            copy = kept_copy(k, g, bounds, far, near, sems, False)
            copy.start()
            ahead.append((first if last else first + 1, copy.wait))
    recv_copy = pltpu.make_async_copy(recv_col_far, recv_col_ref, recv_sem.at[0])
    recv_copy.start()
    dvecs = []

    def one_run(run):
        here = run_rows(run)

        grad = dbranch_ref[here, :]
        if last:
            grad = grad.astype(F32)
            dresid = yield from feed_back(
                here, full_ref[here, 256:384], grad, weights_ref, ffn_refs, dvecs
            )
            dbranch = dresid.astype(BF16)
            dbranch_ref[here, :] = dbranch
        else:
            dbranch = grad

        drows = yield from attend_back_stages(
            run, dbranch, heads_ref, unfold_ref, weights_ref, low_ref, full_ref, scratch
        )
        if last:
            drows = (dresid + drows.astype(F32)).astype(BF16)
        drows_ref[here, :] = drows

    for run in range(NSUB):
        here = run_rows(run)
        dbranch_ref[here, :] = pick_rows(slot_col_ref[here, :], grads_ref[...]).astype(BF16)
    interleave(NSUB, one_run, ahead)
    recv_copy.wait()
    drows = drows_ref[...]
    if last:
        dvecs_ref[...] = sum(dvecs)
        dcontract_ref[...] = mm(active_ref[...], douter_ref[...], TN)
        dexpand_ref[...] = mm(first_ref[...], dinner_ref[...], TN)
        projection_grads(low_ref, scratch, dwin_ref, dwout_ref)
        land_rows(recv_col_ref, drows, send_ref)
        return
    projection_grads(low_ref, scratch, dwin_ref, dwout_ref)
    devices, rows, _ = send_ref.shape
    capacity = recv_col_ref.shape[0] // devices
    for c in range(recv_col_ref.shape[0] // 128):
        sent = pick_rows(recv_col_ref[c * 128 : c * 128 + 128, :], drows).astype(BF16)
        for part in range(128 // capacity):
            send_ref[c * 128 // capacity + part, 0:capacity, :] = sent[
                part * capacity : part * capacity + capacity
            ]
    share, quarter_rows = late
    store_projections(flat_ref, 0, dwin_ref, dwout_ref)
    for j in range(2):
        flat_ref[pl.ds(512 + j, 8, stride=2), :] = dexpand_ref[0:8, 128 * j : 128 * j + 128]
    flat_ref[pl.ds(528, flat_ref.shape[0] - 528), :] = jnp.zeros(
        (flat_ref.shape[0] - 528, 128), F32
    )
    owners = devices // 4
    for device in range(devices):
        quarter, owner = divmod(device, owners)
        block = share_block(
            flat_ref, owner * share, share, quarter * quarter_rows, rows - capacity, quarter_rows
        )
        send_ref[device, capacity:rows, :] = block.astype(BF16)


def share_block(flat_ref, start, share, first_row, rows, used_rows):
    row, shift = divmod(start, 128)
    row = row + first_row
    lane = iota((rows, 128), 1)
    line = iota((rows, 128), 0)
    block = flat_ref[pl.ds(row, rows), :]
    if shift:
        after = flat_ref[pl.ds(row + 1, rows), :]
        block = pltpu.roll(jnp.where(lane >= shift, block, after), 128 - shift, 1)
    inside = (line < used_rows) & ((line + first_row) * 128 + lane < share)
    return jnp.where(inside, block, 0.0)


def store_projections(flat_ref, base, dwin_ref, dwout_ref):
    for j in range(3):
        flat_ref[pl.ds(base + j, 128, stride=3), :] = dwin_ref[:, 128 * j : 128 * j + 128]
    flat_ref[pl.ds(base + 384, 128), :] = dwout_ref[...]


def centred_rows(rows):
    centre = rows - jnp.mean(rows, axis=-1, keepdims=True)
    spread = jnp.mean(centre * centre, axis=-1, keepdims=True)
    inverse = lax.rsqrt(spread + 1e-05)
    return centre * inverse, inverse


def norm_back(grad, gain, unit, inverse):
    dunit = grad * gain
    return (
        dunit
        - jnp.mean(dunit, axis=-1, keepdims=True)
        - unit * jnp.mean(dunit * unit, axis=-1, keepdims=True)
    ) * inverse


def feed_forward(resid, expand, contract, vecs):
    unit, inverse = centred_rows(resid)
    first = unit * vecs[3:4, :] + vecs[4:5, :]
    first_low = first.astype(BF16)
    bias = jnp.concatenate([vecs[0:1, :], vecs[1:2, :]], axis=1)
    inner = mm(first_low, expand) + bias
    yield
    below = 0.5 + 0.5 * lax.erf(inner * math.sqrt(0.5))
    active = (inner * below).astype(BF16)
    second = first + (mm(active, contract) + vecs[2:3, :])
    return unit, inverse, first_low, inner, below, active, second


def feed_back(here, resid, grad, weights_ref, ffn_refs, dvecs):
    active_ref, douter_ref, first_ref, dinner_ref = ffn_refs
    expand, contract, vecs = feed_weights(weights_ref)
    unit_first, inverse_first, first_low, inner, below, active, second = yield from feed_forward(
        resid, expand, contract, vecs
    )
    active_ref[here, :] = active
    first_ref[here, :] = first_low
    yield
    unit, inverse = centred_rows(second)
    dsecond = norm_back(grad, vecs[5:6, :], unit, inverse)
    douter = dsecond.astype(BF16)
    douter_ref[here, :] = douter
    dactive = mm(douter, contract, NT)
    slope = below + inner * (jnp.exp(-0.5 * inner * inner) * (1.0 / math.sqrt(2.0 * math.pi)))
    yield
    dinner = (dactive * slope).astype(BF16)
    dinner_ref[here, :] = dinner
    dfirst = mm(dinner, expand, NT) + dsecond
    yield

    def down(rows):
        return jnp.sum(rows, axis=0, keepdims=True)

    dbias = down(dinner.astype(F32))
    dvecs.append(
        jnp.concatenate(
            [
                dbias[:, :128],
                dbias[:, 128:],
                down(douter.astype(F32)),
                down(dfirst * unit_first),
                down(dfirst),
                down(grad * unit),
                down(grad),
                jnp.zeros((1, 128), F32),
            ],
            axis=0,
        )
    )
    return norm_back(dfirst, vecs[3:4, :], unit_first, inverse_first)


ROWS = 128


def part_rows(part):
    return pl.ds(part * ROWS, ROWS)


def home_forward_kernel(
    route_col_ref,
    place_col_ref,
    branch_ref,
    state_ref,
    weights_ref,
    send_ref,
    resid_ref,
    result_ref,
):
    def some_rows(part):
        here = part_rows(part)
        expand, contract, vecs = feed_weights(weights_ref)
        resid = state_ref[here, :].astype(F32) + pick_rows(route_col_ref[here, :], branch_ref[...])
        yield
        resid_ref[here, :] = resid
        second = (yield from feed_forward(resid, expand, contract, vecs))[-1]
        yield
        unit, _ = centred_rows(second)
        result_ref[here, :] = (unit * vecs[5:6, :] + vecs[6:7, :]).astype(BF16)

    interleave(result_ref.shape[0] // ROWS, some_rows)
    place_rows(place_col_ref, result_ref[...], send_ref)


def home_backward_kernel(
    route_col_ref,
    arrived_ref,
    resid_ref,
    weights_ref,
    place_col_far,
    dresid_ref,
    send_ref,
    dexpand_ref,
    dcontract_ref,
    dvecs_ref,
    active_ref,
    douter_ref,
    first_ref,
    dinner_ref,
    low_ref,
    place_col_ref,
    sem,
):
    place_copy = pltpu.make_async_copy(place_col_far, place_col_ref, sem.at[0])
    place_copy.start()
    ffn_refs = (active_ref, douter_ref, first_ref, dinner_ref)
    dvecs = []

    def some_rows(part):
        here = part_rows(part)
        grad = pick_rows(route_col_ref[here, :], arrived_ref[...])
        yield
        dresid = yield from feed_back(
            here, resid_ref[here, :], grad, weights_ref, ffn_refs, dvecs
        )
        dresid_ref[here, :] = dresid
        low_ref[here, :] = dresid.astype(BF16)

    interleave(dresid_ref.shape[0] // ROWS, some_rows)
    dvecs_ref[...] = sum(dvecs)
    place_copy.wait()
    place_rows(place_col_ref, low_ref[...], send_ref)
    dcontract_ref[...] = mm(active_ref[...], douter_ref[...], TN)
    dexpand_ref[...] = mm(first_ref[...], dinner_ref[...], TN)


def take_kernel(route_col_ref, arrived_ref, out_ref):
    for part in range(out_ref.shape[0] // ROWS):
        here = part_rows(part)
        out_ref[here, :] = pick_rows(route_col_ref[here, :], arrived_ref[...]).astype(BF16)


def finish_kernel(route_col_ref, arrived_ref, dresid_ref, out_ref, rows_ref):
    devices, rows, _ = arrived_ref.shape
    capacity = rows_ref.shape[0] // devices
    for device in range(devices):
        rows_ref[device * capacity : (device + 1) * capacity, :] = arrived_ref[
            device, 0:capacity, :
        ]
    for part in range(out_ref.shape[0] // ROWS):
        here = part_rows(part)
        out_ref[here, :] = dresid_ref[here, :] + pick_rows(route_col_ref[here, :], rows_ref[...])


def late_kernel(quarter_rows, me_ref, early_ref, arrived_ref, *refs):
    outs, parts_ref = refs[:4], refs[4]
    devices, rows, _ = arrived_ref.shape
    late_rows = outs[0].shape[0]
    capacity = rows - late_rows
    late = arrived_ref[0, capacity:rows, :].astype(F32)
    for device in range(1, devices):
        late = late + arrived_ref[device, capacity:rows, :].astype(F32)
    early = early_ref[...]
    square = jnp.sum(early * early) + jnp.sum(late * late)
    line = iota((late_rows, 128), 0)
    parts_ref[0] = jnp.where(line < quarter_rows, late, square)
    for part in range(3):
        piece = early_ref[pl.ds(part * quarter_rows, quarter_rows), :]
        parts_ref[part + 1, 0:quarter_rows, :] = piece
        parts_ref[part + 1, quarter_rows:late_rows, :] = jnp.full(
            (late_rows - quarter_rows, 128), square, F32
        )
    quarter = me_ref[0] // (devices // 4)
    for k, out_ref in enumerate(outs):
        out_ref[...] = parts_ref[quarter ^ k]


def unpack_kernel(share, me_ref, shards_ref, *rest):
    flat_ref = rest[-1]
    outs = rest[:-1]
    devices, block_rows, _ = shards_ref.shape
    lane = iota((block_rows, 128), 1)
    me = me_ref[0]
    for device in range(devices):
        row, shift = divmod(device * share, 128)
        block = shards_ref[me ^ device].astype(F32)
        if shift:
            block = pltpu.roll(block, shift, 1)
            before = jnp.concatenate([flat_ref[pl.ds(row, 1), :], block[:-1]], axis=0)
            block = jnp.where(lane >= shift, block, before)
        flat_ref[pl.ds(row, block_rows), :] = block
    for layer, out_ref in enumerate(outs):
        base = layer * LAYER_ROWS
        for j in range(3):
            out_ref[128 * j : 128 * j + 128, :] = flat_ref[pl.ds(base + j, 128, stride=3), :].astype(
                BF16
            )
        out_ref[384:512, :] = flat_ref[pl.ds(base + 384, 128), :].astype(BF16)
        for j in range(2):
            out_ref[512 + 128 * j : 640 + 128 * j, :] = flat_ref[
                pl.ds(base + 512 + j, 128, stride=2), :
            ].astype(BF16)
        out_ref[768:1024, :] = flat_ref[pl.ds(base + 768, 256), :].astype(BF16)
        vecs = flat_ref[pl.ds(base + 1024, 16), :]
        out_ref[1024:1040, :] = jnp.where(iota((16, 128), 0) < 7, vecs, 0.0).astype(BF16)


def pack_kernel(
    share,
    quarter_rows,
    dwin_ref,
    dwout_ref,
    dexpand_ref,
    dcontract_ref,
    dvecs_ref,
    dexpand_zero_ref,
    dcontract_zero_ref,
    dvecs_zero_ref,
    out_ref,
    flat_ref,
    block_ref,
):
    devices, early_rows, _ = out_ref.shape
    flat_ref[0:512, :] = jnp.zeros((512, 128), F32)
    store_projections(flat_ref, LAYER_ROWS, dwin_ref, dwout_ref)
    for base, expand, contract, vecs in (
        (0, dexpand_zero_ref, dcontract_zero_ref, dvecs_zero_ref),
        (LAYER_ROWS, dexpand_ref, dcontract_ref, dvecs_ref),
    ):
        for j in range(2):
            flat_ref[pl.ds(base + 512 + j, 128, stride=2), :] = expand[:, 128 * j : 128 * j + 128]
        flat_ref[pl.ds(base + 768, 256), :] = contract[...]
        flat_ref[pl.ds(base + 1024, 7), :] = vecs[0:7, :]
    end = LAYERS * LAYER_ROWS
    flat_ref[pl.ds(end, flat_ref.shape[0] - end), :] = jnp.zeros(
        (flat_ref.shape[0] - end, 128), F32
    )
    owners = devices // 4
    block_ref[...] = jnp.zeros_like(block_ref)
    for device in range(devices):
        quarter, owner = divmod(device, owners)
        for part in range(3):
            start = ((part + 1) * owners + owner) * share
            first_row = quarter * quarter_rows
            block_ref[pl.ds(part * quarter_rows, quarter_rows), :] = share_block(
                flat_ref, start, share, first_row, quarter_rows, quarter_rows
            )
        out_ref[device] = block_ref[...].astype(BF16)


def call(
    name,
    micros,
    body,
    outs,
    *args,
    fresh=(),
    scratch=(),
    vmem=24,
    smem=0,
    far_in=0,
    far_out=0,
    sems=(),
):
    near = pl.BlockSpec(memory_space=pltpu.VMEM)
    far = pl.BlockSpec(memory_space=pltpu.HBM)
    specs = [pl.BlockSpec(memory_space=pltpu.SMEM)] * smem
    specs += [near] * (len(args) - smem - far_in) + [far] * far_in
    args = [
        x if i < smem or i in fresh else pltpu.with_memory_space_constraint(x, pltpu.HBM)
        for i, x in enumerate(args)
    ]
    return pl.pallas_call(
        body,
        out_shape=tuple(
            shape_of(o[0], o[1]) if len(o) == 2 else pltpu.HBM(o[0], o[1]) for o in outs
        ),
        in_specs=specs,
        out_specs=tuple([near] * (len(outs) - far_out) + [far] * far_out),
        scratch_shapes=[pltpu.VMEM(s[0], s[1]) for s in scratch]
        + [pltpu.SemaphoreType.DMA(s) for s in sems],
        compiler_params=pltpu.CompilerParams(vmem_limit_bytes=vmem << 20),
        cost_estimate=pl.CostEstimate(
            flops=int(micros * 1e9), bytes_accessed=1 << 16, transcendentals=0
        ),
        name=name,
    )(*args)


def exchange(buffer):
    return lax.all_to_all(buffer, AXES, split_axis=0, concat_axis=0, tiled=True)


def swapped(value, pair, devices, k):
    step = (pair[-1] if k & 1 else 0) ^ (pair[0] if k & 2 else 0)
    return lax.ppermute(value, AXES, [(i, i ^ step) for i in range(devices)])


def paired(parts):
    while len(parts) > 1:
        parts = [parts[i] + parts[i + 1] for i in range(0, len(parts), 2)]
    return parts[0]


def after(value, *others):
    return lax.optimization_barrier((value, *others))[0]


def shards(
    tokens,
    positions,
    cotangent,
    route_send,
    recv_slot,
    slot_bucket,
    master,
    first_moment,
    second_moment,
):
    devices = lax.axis_size("grp") * lax.axis_size("win")
    me = lax.axis_index(AXES)
    home = tokens.shape[0]
    arrivals = recv_slot.shape[2]
    share = master.shape[0]
    share_rows = -(-share // 128)
    block_rows = -(-share_rows // 8) * 8
    quarter_rows = -(-share_rows // 4)
    late_rows = -(-(quarter_rows + 1) // 8) * 8
    early_rows = -(-3 * quarter_rows // 8) * 8
    capacity = arrivals // devices
    width = PILLAR_WIDTH
    flat_rows = -(-(((devices - 1) * share) // 128 + block_rows + 8) // 8) * 8
    late_flat_rows = -(-max(536, ((devices // 4) * share) // 128 + late_rows + 16) // 8) * 8

    heads, unfold, *tables = call(
        "tables",
        4,
        tables_kernel,
        (((EXPANDED, 128), BF16, True), ((WINDOW_SLOTS, 256), BF16, True))
        + (
            ((home, 128), jnp.int16, True),
            ((arrivals, 128), jnp.int16, True),
            ((DEVICE_SLOTS + 64, 128), BF16, True),
            ((NSUB, 2, 128), F32, True),
        )
        * LAYERS,
        route_send,
        recv_slot,
        slot_bucket,
    )
    route_col, recv_col, bucket, bucket_row = (tables[k::4] for k in range(4))
    (send,) = call(
        "start",
        3,
        start_kernel,
        (((arrivals, 2 * width), BF16),),
        route_send,
        tokens,
        positions,
    )
    pos_send, cotangent_send = call(
        "start_next",
        3,
        start_next_kernel,
        (((arrivals, width), BF16, True), ((arrivals, width), BF16, True)),
        route_send,
        positions,
        cotangent,
    )

    copies = jnp.pad(master.astype(BF16), (0, block_rows * 128 - share)).reshape(1, block_rows, 128)
    bits = [devices >> (i + 1) for i in range(devices.bit_length() - 1)]
    for i in range(0, len(bits), 2):
        pair = bits[i : i + 2]
        others = [swapped(copies, pair, devices, k) for k in range(1, 2 ** len(pair))]
        copies = jnp.stack([copies, *others], axis=1).reshape(-1, block_rows, 128)
        if copies.shape[0] == 4:
            arrived = exchange(after(send, copies))
    params = call(
        "unpack",
        2,
        functools.partial(unpack_kernel, share),
        (((1040, width), BF16, True),) * LAYERS,
        me.reshape(1),
        copies,
        scratch=(((flat_rows, 128), F32),),
        smem=1,
    )
    kept_zero = (
        ((DEVICE_SLOTS, 640 + EXPANDED), BF16, True),
        ((DEVICE_SLOTS, 2 * width), F32, True),
    )
    kept_one = (kept_zero[0], ((DEVICE_SLOTS, 3 * width), F32, True))
    recv_col_shape = ((arrivals, 128), jnp.int16)
    slots_low = ((DEVICE_SLOTS, width), BF16)
    slots_wide = ((DEVICE_SLOTS, FF), BF16)
    back_scratch = (slots_low, slots_low, ((DEVICE_SLOTS, 3 * width), BF16))
    arrival_shape = ((arrivals, width), BF16)

    pos_arrived = exchange(after(pos_send, arrived))
    def owner(layer, rows, *pos):
        kept = (kept_zero, kept_one)[layer]
        return call(
            ("first_owner", "last_owner")[layer],
            (13, 18)[layer],
            functools.partial(owner_kernel, layer == 1),
            (arrival_shape, *kept),
            slot_col[1] if layer else recv_slot,
            bucket[layer],
            bucket_row[layer],
            heads,
            params[layer],
            rows,
            *pos,
            recv_col[layer],
            fresh=(5,),
            scratch=(slots_low, *kept, recv_col_shape),
            far_in=1,
            far_out=2,
            sems=((2, len(STORE_BOUNDS) - 1), (1,)),
            vmem=40,
        )

    send, *stored_zero = owner(0, arrived)
    inverse = call(
        "inverse",
        6,
        inverse_kernel,
        (
            ((DEVICE_SLOTS + 64, 128), jnp.int16, True),
            ((arrivals, 128), jnp.int16, True),
        )
        * LAYERS,
        after(route_send, stored_zero[1]),
        recv_slot,
    )
    slot_col, place_col = inverse[0::2], inverse[1::2]
    branch = exchange(after(send, pos_arrived))
    (pos_slots,) = call(
        "slots", 4, slots_kernel, ((*slots_low, True),), slot_col[1], pos_arrived
    )
    send, resid_zero = call(
        "home",
        8,
        home_forward_kernel,
        (arrival_shape, ((home, width), F32, True)),
        route_col[0],
        place_col[1],
        branch,
        tokens,
        params[0],
        fresh=(2,),
        scratch=(((home, width), BF16),),
    )
    arrived = exchange(send)
    cotangent_arrived = exchange(after(cotangent_send, arrived))
    send, *stored_one = owner(1, arrived, pos_slots)
    mixed_arrived = exchange(after(send, cotangent_arrived))
    send, *grads_one = call(
        "last_owner_back",
        22,
        functools.partial(owner_back_kernel, True, None),
        (
            arrival_shape,
            ((width, 3 * width), F32, True),
            ((width, width), F32, True),
            ((width, FF), F32, True),
            ((FF, width), F32, True),
            ((8, width), F32, True),
        ),
        slot_col[1],
        heads,
        unfold,
        params[1],
        cotangent_arrived,
        recv_col[1],
        *stored_one,
        scratch=(
            slots_wide,
            slots_low,
            slots_low,
            slots_wide,
            *back_scratch,
            slots_low,
            *kept_one,
            recv_col_shape,
        ),
        far_in=3,
        sems=((2, len(LOAD_BOUNDS[1]) - 1), (1,)),
        vmem=40,
    )
    arrived = exchange(after(send, mixed_arrived))
    (mixed,) = call(
        "take", 2, take_kernel, (((home, width), BF16),), route_col[1], mixed_arrived
    )
    dresid, send, *ffn_zero = call(
        "home_back",
        10,
        home_backward_kernel,
        (
            ((home, width), F32, True),
            arrival_shape,
            ((width, FF), F32, True),
            ((FF, width), F32, True),
            ((8, width), F32, True),
        ),
        route_col[1],
        arrived,
        resid_zero,
        params[0],
        place_col[0],
        fresh=(1,),
        far_in=1,
        sems=((1,),),
        scratch=(
            ((home, FF), BF16),
            ((home, width), BF16),
            ((home, width), BF16),
            ((home, FF), BF16),
            ((home, width), BF16),
            recv_col_shape,
        ),
    )
    arrived = exchange(send)
    (packed,) = call(
        "pack",
        1,
        functools.partial(pack_kernel, share, quarter_rows),
        (((devices, early_rows, 128), BF16, True),),
        *grads_one,
        *ffn_zero,
        scratch=(((flat_rows, 128), F32), ((early_rows, 128), F32)),
    )
    early = exchange(after(packed, arrived))
    (send,) = call(
        "first_owner_back",
        16,
        functools.partial(owner_back_kernel, False, (share, quarter_rows)),
        (((devices, capacity + late_rows, width), BF16),),
        slot_col[0],
        heads,
        unfold,
        params[0],
        arrived,
        ffn_zero[0],
        recv_col[0],
        *stored_zero,
        fresh=(4,),
        scratch=(
            ((width, 3 * width), F32),
            ((width, width), F32),
            ((late_flat_rows, 128), F32),
            *back_scratch,
            slots_low,
            *kept_zero,
            recv_col_shape,
        ),
        far_in=3,
        sems=((2, len(LOAD_BOUNDS[0]) - 1), (1,)),
        vmem=40,
    )
    arrived = exchange(after(send, early))
    early = jnp.sum(early.astype(F32), axis=0)
    quarters = call(
        "late",
        1,
        functools.partial(late_kernel, quarter_rows),
        (((late_rows, 128), F32, True),) * 4,
        me.reshape(1),
        after(early, mixed),
        arrived,
        fresh=(2,),
        scratch=(((4, late_rows, 128), F32),),
        smem=1,
    )
    (tokens_grad,) = call(
        "finish",
        3,
        finish_kernel,
        (((home, width), F32),),
        route_col[0],
        arrived,
        dresid,
        fresh=(1,),
        scratch=(((arrivals, width), BF16),),
    )
    quarters = [quarters[0]] + [
        swapped(quarters[k], bits[:2], devices, k) for k in range(1, 4)
    ]
    square = after(paired([q[quarter_rows:] for q in quarters]), tokens_grad)
    for i in range(2, len(bits), 2):
        pair = bits[i : i + 2]
        square = paired(
            [square] + [swapped(square, pair, devices, k) for k in range(1, 2 ** len(pair))]
        )
    total = jnp.sqrt(square[0, 0])
    quarters = jnp.stack([q[:quarter_rows] for q in quarters])
    quarter = me // (devices // 4)
    for bit in (1, 2):
        other = quarters.reshape(4 // (2 * bit), 2, bit, quarter_rows, 128)[:, ::-1]
        quarters = jnp.where(quarter & bit, other.reshape(quarters.shape), quarters)
    shard = quarters.reshape(-1)[:share]
    clip_limit = 0.25 * math.sqrt(NPARAM)
    factor = jnp.minimum(1.0, clip_limit / (total + 1e-06))
    clipped = shard * factor
    new_first = beta_one * first_moment + (1.0 - beta_one) * clipped
    new_second = beta_two * second_moment + (1.0 - beta_two) * clipped * clipped
    first_hat = new_first / (1.0 - beta_one**adam_step)
    second_hat = new_second / (1.0 - beta_two**adam_step)
    new_master = master - rate * (first_hat / (jnp.sqrt(second_hat) + adam_eps) + decay * master)
    return (
        mixed,
        tokens_grad,
        total.reshape(1),
        clipped,
        new_master,
        new_first,
        new_second,
        new_master.astype(BF16),
    )


def solution(mesh):
    in_specs = (
        P(("grp", "win"), None),
        P(None, ("grp", "win"), None),
        P(("grp", "win"), None),
        P(None, ("grp", "win")),
        P(None, ("grp", "win"), None),
        P(None, ("grp", "win")),
        P(("grp", "win")),
        P(("grp", "win")),
        P(("grp", "win")),
    )
    out_specs = (
        P(("grp", "win"), None),
        P(("grp", "win"), None),
        P(),
        P(("grp", "win")),
        P(("grp", "win")),
        P(("grp", "win")),
        P(("grp", "win")),
        P(("grp", "win")),
    )
    return jax.shard_map(shards, mesh=mesh, in_specs=in_specs, out_specs=out_specs, check_vma=False)
```

```python
import functools
import math

import jax
import jax.numpy as jnp
from jax import lax
from jax.experimental import pallas as pl
from jax.experimental.pallas import tpu as pltpu
from jax.sharding import PartitionSpec as P

PILLAR_WIDTH = 128
FF = 256
HEAD_COUNT = 8
HDIM = 16
WINDOW_SLOTS = 144
LAYERS = 2
DEVICE_SLOTS = 1728
NSUB = 12
NPARAM = 263936
LAYER_ROWS = 1031
EXPANDED = HEAD_COUNT * WINDOW_SLOTS
MASKED = -1e30
LOWEST = -3e38

beta_one = 0.5
beta_two = 0.5
adam_step = 4
rate = 0.1
decay = 0.01
adam_eps = 1e-08

BF16 = jnp.bfloat16
F32 = jnp.float32
AXES = ("grp", "win")

NN = (((1,), (0,)), ((), ()))
NT = (((1,), (1,)), ((), ()))
TN = (((0,), (0,)), ((), ()))


def mm(left, right, dims=NN):
    return lax.dot_general(left, right, dims, preferred_element_type=F32)


def iota(shape, dim):
    return lax.broadcasted_iota(jnp.int32, shape, dim)


def shape_of(shape, dtype):
    return jax.ShapeDtypeStruct(shape, dtype)


def one_hot_rows(row_ids, first, count):
    return jnp.where(iota((count, row_ids.shape[1]), 0) + first == row_ids, 1.0, 0.0).astype(BF16)


def one_hot_columns(column_ids, width):
    lane = iota(column_ids.shape, 1)
    pieces = [
        jnp.where(column_ids == lane + 128 * k, 1.0, 0.0).astype(BF16)
        for k in range(-(-width // 128))
    ]
    return jnp.concatenate(pieces, axis=1)[:, :width]


def expand_heads(block, heads):
    main = block[:128]
    tail = block[128:]
    return jnp.concatenate([main] * HEAD_COUNT + [tail] * HEAD_COUNT, axis=0) * heads


def pick_rows(column_ids, source):
    half = source.shape[0] // 2
    column_ids = column_ids.astype(jnp.int32)
    upper = column_ids >= half
    local = jnp.where(upper, column_ids - half, column_ids)
    both = mm(one_hot_columns(local, half), jnp.concatenate([source[:half], source[half:]], axis=1))
    return jnp.where(upper, both[:, 128:], both[:, :128])


def inverse_kernel(route_ref, recv_ref, *outs):
    for layer in range(LAYERS):
        for ids, out_ref in (
            (recv_ref[layer], outs[2 * layer]),
            (route_ref[layer : layer + 1, :], outs[2 * layer + 1]),
        ):
            place = iota((ids.shape[1], 128), 0) + 1
            parts = jnp.concatenate(
                [(place >> 6).astype(F32).astype(BF16), (place & 63).astype(F32).astype(BF16)], axis=1
            )
            for c in range(out_ref.shape[0] // 128):
                found = mm(one_hot_rows(ids, c * 128, 128), parts)
                found = found[:, :128] * 64.0 + found[:, 128:] - 1.0
                out_ref[c * 128 : (c + 1) * 128, :] = found.astype(jnp.int32).astype(jnp.int16)


def place_rows(place_col_ref, low_rows, send, chunk=256):
    for c in range(send.shape[0] // chunk):
        part = slice(c * chunk, (c + 1) * chunk)
        send[part, :] = pick_rows(place_col_ref[part, :], low_rows).astype(BF16)


def scatter_rows(route_row, low_rows, send, chunk=256):
    for c in range(send.shape[0] // chunk):
        hot = one_hot_rows(route_row, c * chunk, chunk)
        send[c * chunk : (c + 1) * chunk, :] = mm(hot, low_rows).astype(BF16)


def land_rows(recv_col, slot_values, send, chunk=128):
    for c in range(send.shape[0] // chunk):
        part = slice(c * chunk, (c + 1) * chunk)
        send[part, :] = pick_rows(recv_col[part, :], slot_values).astype(BF16)


def on_lanes(row, out_type):
    here = iota((128, 128), 0) == iota((128, 128), 1)
    spread = jnp.where(here, jnp.broadcast_to(row, (128, 128)), 0)
    ones = jnp.ones((128, 128), BF16)
    if out_type == BF16:
        return mm(spread.astype(F32).astype(BF16), ones).astype(BF16)
    high = mm((spread >> 6).astype(F32).astype(BF16), ones)
    low = mm((spread & 63).astype(F32).astype(BF16), ones)
    return (high * 64.0 + low).astype(jnp.int32).astype(out_type)


def tables_kernel(route_ref, recv_ref, bucket_ref, heads_ref, unfold_ref, *outs):
    slot = iota((EXPANDED, 128), 0)
    head = jnp.where(slot < 1024, slot >> 7, (slot - 1024) >> 4)
    heads_ref[...] = jnp.where(head == iota((EXPANDED, 128), 1) >> 4, 1.0, 0.0).astype(BF16)
    wide = iota((WINDOW_SLOTS, 256), 1)
    wide = jnp.where(wide < 128, wide, 128 + (wide & 15))
    unfold_ref[...] = jnp.where(iota((WINDOW_SLOTS, 256), 0) == wide, 1.0, 0.0).astype(BF16)
    for layer in range(LAYERS):
        route_col_ref, recv_col_ref, bucket_col_ref, bucket_row_ref = outs[4 * layer : 4 * layer + 4]
        bucket = bucket_ref[layer : layer + 1, :]
        for ids, out_ref in (
            (route_ref[layer : layer + 1, :], route_col_ref),
            (recv_ref[layer], recv_col_ref),
            (jnp.concatenate([bucket, bucket[:, :64]], axis=1), bucket_col_ref),
        ):
            for c in range(out_ref.shape[0] // 128):
                part = slice(c * 128, (c + 1) * 128)
                out_ref[part, :] = on_lanes(ids[:, part], out_ref.dtype)
        bucket = bucket.astype(F32)
        for run in range(NSUB):
            base = run * WINDOW_SLOTS
            tail = bucket[:, base + 128 : base + 144]
            bucket_row_ref[run] = jnp.concatenate(
                [bucket[:, base : base + 128], jnp.concatenate([tail] * 8, axis=1)], axis=0
            )


def start_kernel(route_ref, tokens_ref, pos_ref, out_ref):
    both = jnp.concatenate([tokens_ref[...], pos_ref[0]], axis=1)
    scatter_rows(route_ref[0:1, :], both, out_ref)


def start_next_kernel(route_ref, pos_ref, cotangent_ref, pos_out_ref, cotangent_out_ref):
    both = jnp.concatenate([pos_ref[1], cotangent_ref[...]], axis=1)
    for c in range(pos_out_ref.shape[0] // 256):
        part = slice(c * 256, (c + 1) * 256)
        sent = mm(one_hot_rows(route_ref[1:2, :], c * 256, 256), both).astype(BF16)
        pos_out_ref[part, :] = sent[:, :128]
        cotangent_out_ref[part, :] = sent[:, 128:]


def slots_kernel(slot_col_ref, rows_ref, out_ref):
    for run in range(NSUB):
        part = slice(run * WINDOW_SLOTS, (run + 1) * WINDOW_SLOTS)
        out_ref[part, :] = pick_rows(slot_col_ref[part, :], rows_ref[...]).astype(BF16)


def project_in(weights_ref):
    return jnp.concatenate([weights_ref[128 * j : 128 * j + 128, :] for j in range(3)], axis=1)


def project_out(weights_ref):
    return weights_ref[384:512, :]


def feed_weights(weights_ref):
    expand = jnp.concatenate([weights_ref[512:640, :], weights_ref[640:768, :]], axis=1)
    return expand, weights_ref[768:1024, :], weights_ref[1024:1040, :].astype(F32)


def interleave(count, make, ahead=()):
    waiting = [make(i) for i in range(count)]
    running = []
    turn = 0
    while waiting or running:
        for when, act in ahead:
            if when == turn:
                act()
        if waiting:
            running.insert(0, waiting.pop(0))
        running = [part for part in running if next(part, running) is not running]
        turn += 1
    for when, act in ahead:
        if when >= turn:
            act()


def run_rows(run):
    return pl.ds(run * WINDOW_SLOTS, WINDOW_SLOTS)


STORE_BOUNDS = tuple(range(NSUB + 1))
LOAD_BOUNDS = ((0, 4, 12), (0, 3, 7, 12))


def kept_copy(k, group, bounds, far, near, sems, out):
    first, last = bounds[group : group + 2]
    here = pl.ds(first * WINDOW_SLOTS, (last - first) * WINDOW_SLOTS)
    far, near = far.at[here, :], near.at[here, :]
    ends = (near, far) if out else (far, near)
    return pltpu.make_async_copy(*ends, sems.at[k, group])


def attend_stages(run, slot_rows, joined, bucket, bucket_row, heads_ref, weights_ref, low, full):
    win = project_in(weights_ref)
    query_key = mm(joined, win[:, :256])
    queries = (query_key[:, :128] * 0.25).astype(BF16)
    keys = query_key[:, 128:].astype(BF16)
    values = mm(slot_rows, win[:, 256:]).astype(BF16)
    heads = heads_ref[...]
    block = heads[1024:]
    spread = jnp.concatenate(
        [
            queries * jnp.concatenate([heads[128 * h : 128 * h + 16]] * 9, axis=0)
            for h in range(HEAD_COUNT)
        ],
        axis=0,
    )
    yield
    scores = mm(spread, keys[:128], NT)
    tail = mm(queries, jnp.concatenate([keys[128:]] * 8, axis=0) * block, NT)
    yield

    def same(row):
        return jnp.where((bucket == row) & (row >= 0), 0.0, MASKED)

    main_bias = same(bucket_row[0:1, :])
    tail = tail + same(bucket_row[1:2, :])
    segment = iota((WINDOW_SLOTS, 128), 1) >> 4
    tail_top = jnp.zeros((WINDOW_SLOTS, 128), F32)
    pieces = []
    for h in range(HEAD_COUNT):
        main = scores[WINDOW_SLOTS * h : WINDOW_SLOTS * (h + 1)] + main_bias
        own_tail = segment == h
        top = jnp.max(jnp.maximum(main, jnp.where(own_tail, tail, LOWEST)), axis=1, keepdims=True)
        tail_top = jnp.where(own_tail, top, tail_top)
        pieces.append(jnp.exp(main - top).astype(BF16))
    pieces.append(jnp.exp(tail - tail_top).astype(BF16))
    expo = jnp.concatenate(pieces, axis=1)
    low(jnp.concatenate([joined, slot_rows, queries, keys, values, expo], axis=1))
    yield
    summed = mm(expo, jnp.concatenate([expand_heads(values, heads), heads], axis=1))
    yield
    share = jnp.where(bucket >= 0, 1.0, 0.0) / summed[:, 128:]
    attended = summed[:, :128] * share
    full(jnp.concatenate([attended, share], axis=1))
    return mm(attended.astype(BF16), project_out(weights_ref)).astype(BF16)


def attend_back_stages(
    run, dbranch, heads_ref, unfold_ref, weights_ref, low_ref, full_ref, scratch
):
    attended_ref, dbranch_ref, dqkv_ref = scratch
    here = run_rows(run)
    dattended = mm(dbranch, project_out(weights_ref), NT).astype(BF16).astype(F32)
    yield
    heads = heads_ref[...]
    block = heads[1024:]
    out = full_ref[here, 0:128]
    attended_ref[here, :] = out.astype(BF16)
    dout = (dattended * full_ref[here, 128:256]).astype(BF16)
    weighed = dout.astype(F32) * out
    weighed_high = weighed.astype(BF16)
    weighed_low = (weighed - weighed_high.astype(F32)).astype(BF16)
    centre = mm(weighed_high, block) + mm(weighed_low, block)
    queries = low_ref[here, 256:384]
    keys_wide = expand_heads(low_ref[here, 384:512], heads)
    dprob = mm(dout, expand_heads(low_ref[here, 512:640], heads), NT)
    yield
    expo = low_ref[here, 640:]
    pieces = [
        (
            (dprob[:, 128 * h : 128 * h + 128] - centre[:, 16 * h : 16 * h + 1])
            * expo[:, 128 * h : 128 * h + 128].astype(F32)
        ).astype(BF16)
        for h in range(HEAD_COUNT)
    ]
    pieces.append(((dprob[:, 1024:] - centre) * expo[:, 1024:].astype(F32)).astype(BF16))
    dscore = jnp.concatenate(pieces, axis=1)
    yield
    dqueries = (mm(dscore, keys_wide) * 0.25).astype(BF16)
    yield

    def gathered(left, right):
        wide = mm(left, right, TN)
        main = jnp.concatenate(
            [wide[16 * h : 16 * h + 16, 128 * h : 128 * h + 128] for h in range(HEAD_COUNT)],
            axis=0,
        )
        return jnp.concatenate([main, wide[:, 1024:] * block.astype(F32)], axis=1).astype(BF16)

    folded = jnp.concatenate([gathered(queries, dscore), gathered(dout, expo)], axis=0)
    yield
    dkeys_values = mm(unfold_ref[...], folded, NT).astype(BF16)
    dqkv = jnp.concatenate([dqueries, dkeys_values], axis=1)
    dqkv_ref[here, :] = dqkv
    yield
    return mm(dqkv, project_in(weights_ref), NT).astype(BF16)


def projection_grads(low_ref, scratch, dwin_ref, dwout_ref):
    attended_ref, dbranch_ref, dqkv_ref = scratch
    dwout_ref[...] = mm(attended_ref[...], dbranch_ref[...], TN)
    dqkv = dqkv_ref[...]
    dwin_ref[:, :256] = mm(low_ref[:, 0:128], dqkv[:, :256], TN)
    dwin_ref[:, 256:] = mm(low_ref[:, 128:256], dqkv[:, 256:], TN)


def owner_kernel(
    last,
    recv_ref,
    bucket_ref,
    bucket_row_ref,
    heads_ref,
    weights_ref,
    rows_ref,
    *rest,
):
    if last:
        pos_ref, *rest = rest
    (
        recv_col_far,
        send_ref,
        low_far,
        full_far,
        leave_ref,
        low_ref,
        full_ref,
        recv_col_ref,
        sems,
        recv_sem,
    ) = rest
    recv_copy = pltpu.make_async_copy(recv_col_far, recv_col_ref, recv_sem.at[0])
    recv_copy.start()

    def one_run(run):
        here = run_rows(run)

        def low(rows):
            low_ref[here, :] = rows

        def full(rows):
            full_ref[here, 0:256] = rows

        if last:
            landed = pick_rows(recv_ref[here, :], rows_ref[...])
        else:
            landed = mm(one_hot_rows(recv_ref[0], run * WINDOW_SLOTS, WINDOW_SLOTS), rows_ref[...])
        state = landed[:, :128]
        pos = pos_ref[here, :].astype(F32) if last else landed[:, 128:]
        yield
        branch = yield from attend_stages(
            run,
            state.astype(BF16),
            (state + pos).astype(BF16),
            bucket_ref[here, :].astype(F32),
            bucket_row_ref[run],
            heads_ref,
            weights_ref,
            low,
            full,
        )
        if not last:
            leave_ref[here, :] = branch
            return
        yield
        resid = state + branch.astype(F32)
        full_ref[here, 256:384] = resid
        expand, contract, vecs = feed_weights(weights_ref)
        second = (yield from feed_forward(resid, expand, contract, vecs))[-1]
        yield
        unit, _ = centred_rows(second)
        leave_ref[here, :] = (unit * vecs[5:6, :] + vecs[6:7, :]).astype(BF16)

    low_copies = [kept_copy(0, g, STORE_BOUNDS, low_far, low_ref, sems, True) for g in range(len(STORE_BOUNDS) - 1)]
    full_copies = [kept_copy(1, g, STORE_BOUNDS, full_far, full_ref, sems, True) for g in range(len(STORE_BOUNDS) - 1)]
    ahead = [(STORE_BOUNDS[g + 1] + 3, copy.start) for g, copy in enumerate(low_copies)]
    ahead += [(STORE_BOUNDS[g + 1] + 6, copy.start) for g, copy in enumerate(full_copies)]
    interleave(NSUB, one_run, ahead)
    recv_copy.wait()
    land_rows(recv_col_ref, leave_ref[...], send_ref)
    for copy in low_copies + full_copies:
        copy.wait()


def owner_back_kernel(
    last,
    late,
    slot_col_ref,
    heads_ref,
    unfold_ref,
    weights_ref,
    grads_ref,
    *rest,
):
    if not last:
        dexpand_ref, *rest = rest
    recv_col_far, low_far, full_far, send_ref, *rest = rest
    if last:
        dwin_ref, dwout_ref, dexpand_ref, dcontract_ref, dvecs_ref, *rest = rest
        active_ref, douter_ref, first_ref, dinner_ref, *rest = rest
        ffn_refs = (active_ref, douter_ref, first_ref, dinner_ref)
    else:
        dwin_ref, dwout_ref, flat_ref, *rest = rest
    (
        attended_ref,
        dbranch_ref,
        dqkv_ref,
        drows_ref,
        low_ref,
        full_ref,
        recv_col_ref,
        sems,
        recv_sem,
    ) = rest
    scratch = (attended_ref, dbranch_ref, dqkv_ref)
    ahead = []
    bounds = LOAD_BOUNDS[1 if last else 0]
    for g, first in enumerate(bounds[:-1]):
        for k, far, near in ((1, full_far, full_ref), (0, low_far, low_ref)):
            copy = kept_copy(k, g, bounds, far, near, sems, False)
            copy.start()
            ahead.append((first if last else first + 1, copy.wait))
    recv_copy = pltpu.make_async_copy(recv_col_far, recv_col_ref, recv_sem.at[0])
    recv_copy.start()
    dvecs = []

    def one_run(run):
        here = run_rows(run)

        grad = dbranch_ref[here, :]
        if last:
            grad = grad.astype(F32)
            dresid = yield from feed_back(
                here, full_ref[here, 256:384], grad, weights_ref, ffn_refs, dvecs
            )
            dbranch = dresid.astype(BF16)
            dbranch_ref[here, :] = dbranch
        else:
            dbranch = grad

        drows = yield from attend_back_stages(
            run, dbranch, heads_ref, unfold_ref, weights_ref, low_ref, full_ref, scratch
        )
        if last:
            drows = (dresid + drows.astype(F32)).astype(BF16)
        drows_ref[here, :] = drows

    for run in range(NSUB):
        here = run_rows(run)
        dbranch_ref[here, :] = pick_rows(slot_col_ref[here, :], grads_ref[...]).astype(BF16)
    interleave(NSUB, one_run, ahead)
    recv_copy.wait()
    drows = drows_ref[...]
    if last:
        dvecs_ref[...] = sum(dvecs)
        dcontract_ref[...] = mm(active_ref[...], douter_ref[...], TN)
        dexpand_ref[...] = mm(first_ref[...], dinner_ref[...], TN)
        projection_grads(low_ref, scratch, dwin_ref, dwout_ref)
        land_rows(recv_col_ref, drows, send_ref)
        return
    projection_grads(low_ref, scratch, dwin_ref, dwout_ref)
    devices, rows, _ = send_ref.shape
    capacity = recv_col_ref.shape[0] // devices
    for c in range(recv_col_ref.shape[0] // 128):
        sent = pick_rows(recv_col_ref[c * 128 : c * 128 + 128, :], drows).astype(BF16)
        for part in range(128 // capacity):
            send_ref[c * 128 // capacity + part, 0:capacity, :] = sent[
                part * capacity : part * capacity + capacity
            ]
    share, quarter_rows = late
    store_projections(flat_ref, 0, dwin_ref, dwout_ref)
    for j in range(2):
        flat_ref[pl.ds(512 + j, 8, stride=2), :] = dexpand_ref[0:8, 128 * j : 128 * j + 128]
    flat_ref[pl.ds(528, flat_ref.shape[0] - 528), :] = jnp.zeros(
        (flat_ref.shape[0] - 528, 128), F32
    )
    owners = devices // 4
    for device in range(devices):
        quarter, owner = divmod(device, owners)
        block = share_block(
            flat_ref, owner * share, share, quarter * quarter_rows, rows - capacity, quarter_rows
        )
        send_ref[device, capacity:rows, :] = block.astype(BF16)


def share_block(flat_ref, start, share, first_row, rows, used_rows):
    row, shift = divmod(start, 128)
    row = row + first_row
    lane = iota((rows, 128), 1)
    line = iota((rows, 128), 0)
    block = flat_ref[pl.ds(row, rows), :]
    if shift:
        after = flat_ref[pl.ds(row + 1, rows), :]
        block = pltpu.roll(jnp.where(lane >= shift, block, after), 128 - shift, 1)
    inside = (line < used_rows) & ((line + first_row) * 128 + lane < share)
    return jnp.where(inside, block, 0.0)


def store_projections(flat_ref, base, dwin_ref, dwout_ref):
    for j in range(3):
        flat_ref[pl.ds(base + j, 128, stride=3), :] = dwin_ref[:, 128 * j : 128 * j + 128]
    flat_ref[pl.ds(base + 384, 128), :] = dwout_ref[...]


def centred_rows(rows):
    centre = rows - jnp.mean(rows, axis=-1, keepdims=True)
    spread = jnp.mean(centre * centre, axis=-1, keepdims=True)
    inverse = lax.rsqrt(spread + 1e-05)
    return centre * inverse, inverse


def norm_back(grad, gain, unit, inverse):
    dunit = grad * gain
    return (
        dunit
        - jnp.mean(dunit, axis=-1, keepdims=True)
        - unit * jnp.mean(dunit * unit, axis=-1, keepdims=True)
    ) * inverse


def feed_forward(resid, expand, contract, vecs):
    unit, inverse = centred_rows(resid)
    first = unit * vecs[3:4, :] + vecs[4:5, :]
    first_low = first.astype(BF16)
    bias = jnp.concatenate([vecs[0:1, :], vecs[1:2, :]], axis=1)
    inner = mm(first_low, expand) + bias
    yield
    below = 0.5 + 0.5 * lax.erf(inner * math.sqrt(0.5))
    active = (inner * below).astype(BF16)
    second = first + (mm(active, contract) + vecs[2:3, :])
    return unit, inverse, first_low, inner, below, active, second


def feed_back(here, resid, grad, weights_ref, ffn_refs, dvecs):
    active_ref, douter_ref, first_ref, dinner_ref = ffn_refs
    expand, contract, vecs = feed_weights(weights_ref)
    unit_first, inverse_first, first_low, inner, below, active, second = yield from feed_forward(
        resid, expand, contract, vecs
    )
    active_ref[here, :] = active
    first_ref[here, :] = first_low
    yield
    unit, inverse = centred_rows(second)
    dsecond = norm_back(grad, vecs[5:6, :], unit, inverse)
    douter = dsecond.astype(BF16)
    douter_ref[here, :] = douter
    dactive = mm(douter, contract, NT)
    slope = below + inner * (jnp.exp(-0.5 * inner * inner) * (1.0 / math.sqrt(2.0 * math.pi)))
    yield
    dinner = (dactive * slope).astype(BF16)
    dinner_ref[here, :] = dinner
    dfirst = mm(dinner, expand, NT) + dsecond
    yield

    def down(rows):
        return jnp.sum(rows, axis=0, keepdims=True)

    dbias = down(dinner.astype(F32))
    dvecs.append(
        jnp.concatenate(
            [
                dbias[:, :128],
                dbias[:, 128:],
                down(douter.astype(F32)),
                down(dfirst * unit_first),
                down(dfirst),
                down(grad * unit),
                down(grad),
                jnp.zeros((1, 128), F32),
            ],
            axis=0,
        )
    )
    return norm_back(dfirst, vecs[3:4, :], unit_first, inverse_first)


ROWS = 128


def part_rows(part):
    return pl.ds(part * ROWS, ROWS)


def home_forward_kernel(
    route_col_ref,
    place_col_ref,
    branch_ref,
    state_ref,
    weights_ref,
    send_ref,
    resid_ref,
    result_ref,
):
    def some_rows(part):
        here = part_rows(part)
        expand, contract, vecs = feed_weights(weights_ref)
        resid = state_ref[here, :].astype(F32) + pick_rows(route_col_ref[here, :], branch_ref[...])
        yield
        resid_ref[here, :] = resid
        second = (yield from feed_forward(resid, expand, contract, vecs))[-1]
        yield
        unit, _ = centred_rows(second)
        result_ref[here, :] = (unit * vecs[5:6, :] + vecs[6:7, :]).astype(BF16)

    interleave(result_ref.shape[0] // ROWS, some_rows)
    place_rows(place_col_ref, result_ref[...], send_ref)


def home_backward_kernel(
    route_col_ref,
    arrived_ref,
    resid_ref,
    weights_ref,
    place_col_far,
    dresid_ref,
    send_ref,
    dexpand_ref,
    dcontract_ref,
    dvecs_ref,
    active_ref,
    douter_ref,
    first_ref,
    dinner_ref,
    low_ref,
    place_col_ref,
    sem,
):
    place_copy = pltpu.make_async_copy(place_col_far, place_col_ref, sem.at[0])
    place_copy.start()
    ffn_refs = (active_ref, douter_ref, first_ref, dinner_ref)
    dvecs = []

    def some_rows(part):
        here = part_rows(part)
        grad = pick_rows(route_col_ref[here, :], arrived_ref[...])
        yield
        dresid = yield from feed_back(
            here, resid_ref[here, :], grad, weights_ref, ffn_refs, dvecs
        )
        dresid_ref[here, :] = dresid
        low_ref[here, :] = dresid.astype(BF16)

    interleave(dresid_ref.shape[0] // ROWS, some_rows)
    dvecs_ref[...] = sum(dvecs)
    place_copy.wait()
    place_rows(place_col_ref, low_ref[...], send_ref)
    dcontract_ref[...] = mm(active_ref[...], douter_ref[...], TN)
    dexpand_ref[...] = mm(first_ref[...], dinner_ref[...], TN)


def take_kernel(route_col_ref, arrived_ref, out_ref):
    for part in range(out_ref.shape[0] // ROWS):
        here = part_rows(part)
        out_ref[here, :] = pick_rows(route_col_ref[here, :], arrived_ref[...]).astype(BF16)


def finish_kernel(route_col_ref, arrived_ref, dresid_ref, out_ref, rows_ref):
    devices, rows, _ = arrived_ref.shape
    capacity = rows_ref.shape[0] // devices
    for device in range(devices):
        rows_ref[device * capacity : (device + 1) * capacity, :] = arrived_ref[
            device, 0:capacity, :
        ]
    for part in range(out_ref.shape[0] // ROWS):
        here = part_rows(part)
        out_ref[here, :] = dresid_ref[here, :] + pick_rows(route_col_ref[here, :], rows_ref[...])


def late_kernel(quarter_rows, me_ref, early_ref, arrived_ref, *refs):
    outs, parts_ref = refs[:4], refs[4]
    devices, rows, _ = arrived_ref.shape
    late_rows = outs[0].shape[0]
    capacity = rows - late_rows
    late = arrived_ref[0, capacity:rows, :].astype(F32)
    for device in range(1, devices):
        late = late + arrived_ref[device, capacity:rows, :].astype(F32)
    early = early_ref[...]
    square = jnp.sum(early * early) + jnp.sum(late * late)
    line = iota((late_rows, 128), 0)
    parts_ref[0] = jnp.where(line < quarter_rows, late, square)
    for part in range(3):
        piece = early_ref[pl.ds(part * quarter_rows, quarter_rows), :]
        parts_ref[part + 1, 0:quarter_rows, :] = piece
        parts_ref[part + 1, quarter_rows:late_rows, :] = jnp.full(
            (late_rows - quarter_rows, 128), square, F32
        )
    quarter = me_ref[0] // (devices // 4)
    for k, out_ref in enumerate(outs):
        out_ref[...] = parts_ref[quarter ^ k]


def unpack_kernel(share, me_ref, shards_ref, *rest):
    flat_ref = rest[-1]
    outs = rest[:-1]
    devices, block_rows, _ = shards_ref.shape
    lane = iota((block_rows, 128), 1)
    me = me_ref[0]
    for device in range(devices):
        row, shift = divmod(device * share, 128)
        block = shards_ref[me ^ device].astype(F32)
        if shift:
            block = pltpu.roll(block, shift, 1)
            before = jnp.concatenate([flat_ref[pl.ds(row, 1), :], block[:-1]], axis=0)
            block = jnp.where(lane >= shift, block, before)
        flat_ref[pl.ds(row, block_rows), :] = block
    for layer, out_ref in enumerate(outs):
        base = layer * LAYER_ROWS
        for j in range(3):
            out_ref[128 * j : 128 * j + 128, :] = flat_ref[pl.ds(base + j, 128, stride=3), :].astype(
                BF16
            )
        out_ref[384:512, :] = flat_ref[pl.ds(base + 384, 128), :].astype(BF16)
        for j in range(2):
            out_ref[512 + 128 * j : 640 + 128 * j, :] = flat_ref[
                pl.ds(base + 512 + j, 128, stride=2), :
            ].astype(BF16)
        out_ref[768:1024, :] = flat_ref[pl.ds(base + 768, 256), :].astype(BF16)
        vecs = flat_ref[pl.ds(base + 1024, 16), :]
        out_ref[1024:1040, :] = jnp.where(iota((16, 128), 0) < 7, vecs, 0.0).astype(BF16)


def pack_kernel(
    share,
    quarter_rows,
    dwin_ref,
    dwout_ref,
    dexpand_ref,
    dcontract_ref,
    dvecs_ref,
    dexpand_zero_ref,
    dcontract_zero_ref,
    dvecs_zero_ref,
    out_ref,
    flat_ref,
    block_ref,
):
    devices, early_rows, _ = out_ref.shape
    flat_ref[0:512, :] = jnp.zeros((512, 128), F32)
    store_projections(flat_ref, LAYER_ROWS, dwin_ref, dwout_ref)
    for base, expand, contract, vecs in (
        (0, dexpand_zero_ref, dcontract_zero_ref, dvecs_zero_ref),
        (LAYER_ROWS, dexpand_ref, dcontract_ref, dvecs_ref),
    ):
        for j in range(2):
            flat_ref[pl.ds(base + 512 + j, 128, stride=2), :] = expand[:, 128 * j : 128 * j + 128]
        flat_ref[pl.ds(base + 768, 256), :] = contract[...]
        flat_ref[pl.ds(base + 1024, 7), :] = vecs[0:7, :]
    end = LAYERS * LAYER_ROWS
    flat_ref[pl.ds(end, flat_ref.shape[0] - end), :] = jnp.zeros(
        (flat_ref.shape[0] - end, 128), F32
    )
    owners = devices // 4
    block_ref[...] = jnp.zeros_like(block_ref)
    for device in range(devices):
        quarter, owner = divmod(device, owners)
        for part in range(3):
            start = ((part + 1) * owners + owner) * share
            first_row = quarter * quarter_rows
            block_ref[pl.ds(part * quarter_rows, quarter_rows), :] = share_block(
                flat_ref, start, share, first_row, quarter_rows, quarter_rows
            )
        out_ref[device] = block_ref[...].astype(BF16)


def call(
    name,
    micros,
    body,
    outs,
    *args,
    fresh=(),
    scratch=(),
    vmem=24,
    smem=0,
    far_in=0,
    far_out=0,
    sems=(),
):
    near = pl.BlockSpec(memory_space=pltpu.VMEM)
    far = pl.BlockSpec(memory_space=pltpu.HBM)
    specs = [pl.BlockSpec(memory_space=pltpu.SMEM)] * smem
    specs += [near] * (len(args) - smem - far_in) + [far] * far_in
    args = [
        x if i < smem or i in fresh else pltpu.with_memory_space_constraint(x, pltpu.HBM)
        for i, x in enumerate(args)
    ]
    return pl.pallas_call(
        body,
        out_shape=tuple(
            shape_of(o[0], o[1]) if len(o) == 2 else pltpu.HBM(o[0], o[1]) for o in outs
        ),
        in_specs=specs,
        out_specs=tuple([near] * (len(outs) - far_out) + [far] * far_out),
        scratch_shapes=[pltpu.VMEM(s[0], s[1]) for s in scratch]
        + [pltpu.SemaphoreType.DMA(s) for s in sems],
        compiler_params=pltpu.CompilerParams(vmem_limit_bytes=vmem << 20),
        cost_estimate=pl.CostEstimate(
            flops=int(micros * 1e9), bytes_accessed=1 << 16, transcendentals=0
        ),
        name=name,
    )(*args)


def exchange(buffer):
    return lax.all_to_all(buffer, AXES, split_axis=0, concat_axis=0, tiled=True)


def swapped(value, pair, devices, k):
    step = (pair[-1] if k & 1 else 0) ^ (pair[0] if k & 2 else 0)
    return lax.ppermute(value, AXES, [(i, i ^ step) for i in range(devices)])


def paired(parts):
    while len(parts) > 1:
        parts = [parts[i] + parts[i + 1] for i in range(0, len(parts), 2)]
    return parts[0]


def after(value, *others):
    return lax.optimization_barrier((value, *others))[0]


def shards(
    tokens,
    positions,
    cotangent,
    route_send,
    recv_slot,
    slot_bucket,
    master,
    first_moment,
    second_moment,
):
    devices = lax.axis_size("grp") * lax.axis_size("win")
    me = lax.axis_index(AXES)
    home = tokens.shape[0]
    arrivals = recv_slot.shape[2]
    share = master.shape[0]
    share_rows = -(-share // 128)
    block_rows = -(-share_rows // 8) * 8
    quarter_rows = -(-share_rows // 4)
    late_rows = -(-(quarter_rows + 1) // 8) * 8
    early_rows = -(-3 * quarter_rows // 8) * 8
    capacity = arrivals // devices
    width = PILLAR_WIDTH
    flat_rows = -(-(((devices - 1) * share) // 128 + block_rows + 8) // 8) * 8
    late_flat_rows = -(-max(536, ((devices // 4) * share) // 128 + late_rows + 16) // 8) * 8

    heads, unfold, *tables = call(
        "tables",
        4,
        tables_kernel,
        (((EXPANDED, 128), BF16, True), ((WINDOW_SLOTS, 256), BF16, True))
        + (
            ((home, 128), jnp.int16, True),
            ((arrivals, 128), jnp.int16, True),
            ((DEVICE_SLOTS + 64, 128), BF16, True),
            ((NSUB, 2, 128), F32, True),
        )
        * LAYERS,
        route_send,
        recv_slot,
        slot_bucket,
    )
    route_col, recv_col, bucket, bucket_row = (tables[k::4] for k in range(4))
    (send,) = call(
        "start",
        3,
        start_kernel,
        (((arrivals, 2 * width), BF16),),
        route_send,
        tokens,
        positions,
    )
    pos_send, cotangent_send = call(
        "start_next",
        3,
        start_next_kernel,
        (((arrivals, width), BF16, True), ((arrivals, width), BF16, True)),
        route_send,
        positions,
        cotangent,
    )

    copies = jnp.pad(master.astype(BF16), (0, block_rows * 128 - share)).reshape(1, block_rows, 128)
    bits = [devices >> (i + 1) for i in range(devices.bit_length() - 1)]
    for i in range(0, len(bits), 2):
        pair = bits[i : i + 2]
        others = [swapped(copies, pair, devices, k) for k in range(1, 2 ** len(pair))]
        copies = jnp.stack([copies, *others], axis=1).reshape(-1, block_rows, 128)
        if copies.shape[0] == 4:
            arrived = exchange(after(send, copies))
    params = call(
        "unpack",
        2,
        functools.partial(unpack_kernel, share),
        (((1040, width), BF16, True),) * LAYERS,
        me.reshape(1),
        copies,
        scratch=(((flat_rows, 128), F32),),
        smem=1,
    )
    kept_zero = (
        ((DEVICE_SLOTS, 640 + EXPANDED), BF16, True),
        ((DEVICE_SLOTS, 2 * width), F32, True),
    )
    kept_one = (kept_zero[0], ((DEVICE_SLOTS, 3 * width), F32, True))
    recv_col_shape = ((arrivals, 128), jnp.int16)
    slots_low = ((DEVICE_SLOTS, width), BF16)
    slots_wide = ((DEVICE_SLOTS, FF), BF16)
    back_scratch = (slots_low, slots_low, ((DEVICE_SLOTS, 3 * width), BF16))
    arrival_shape = ((arrivals, width), BF16)

    pos_arrived = exchange(after(pos_send, arrived))
    def owner(layer, rows, *pos):
        kept = (kept_zero, kept_one)[layer]
        return call(
            ("first_owner", "last_owner")[layer],
            (13, 18)[layer],
            functools.partial(owner_kernel, layer == 1),
            (arrival_shape, *kept),
            slot_col[1] if layer else recv_slot,
            bucket[layer],
            bucket_row[layer],
            heads,
            params[layer],
            rows,
            *pos,
            recv_col[layer],
            fresh=(5,),
            scratch=(slots_low, *kept, recv_col_shape),
            far_in=1,
            far_out=2,
            sems=((2, len(STORE_BOUNDS) - 1), (1,)),
            vmem=40,
        )

    send, *stored_zero = owner(0, arrived)
    inverse = call(
        "inverse",
        6,
        inverse_kernel,
        (
            ((DEVICE_SLOTS + 64, 128), jnp.int16, True),
            ((arrivals, 128), jnp.int16, True),
        )
        * LAYERS,
        after(route_send, stored_zero[1]),
        recv_slot,
    )
    slot_col, place_col = inverse[0::2], inverse[1::2]
    branch = exchange(after(send, pos_arrived))
    (pos_slots,) = call(
        "slots", 4, slots_kernel, ((*slots_low, True),), slot_col[1], pos_arrived
    )
    send, resid_zero = call(
        "home",
        8,
        home_forward_kernel,
        (arrival_shape, ((home, width), F32, True)),
        route_col[0],
        place_col[1],
        branch,
        tokens,
        params[0],
        fresh=(2,),
        scratch=(((home, width), BF16),),
    )
    arrived = exchange(send)
    cotangent_arrived = exchange(after(cotangent_send, arrived))
    send, *stored_one = owner(1, arrived, pos_slots)
    mixed_arrived = exchange(after(send, cotangent_arrived))
    send, *grads_one = call(
        "last_owner_back",
        22,
        functools.partial(owner_back_kernel, True, None),
        (
            arrival_shape,
            ((width, 3 * width), F32, True),
            ((width, width), F32, True),
            ((width, FF), F32, True),
            ((FF, width), F32, True),
            ((8, width), F32, True),
        ),
        slot_col[1],
        heads,
        unfold,
        params[1],
        cotangent_arrived,
        recv_col[1],
        *stored_one,
        scratch=(
            slots_wide,
            slots_low,
            slots_low,
            slots_wide,
            *back_scratch,
            slots_low,
            *kept_one,
            recv_col_shape,
        ),
        far_in=3,
        sems=((2, len(LOAD_BOUNDS[1]) - 1), (1,)),
        vmem=40,
    )
    arrived = exchange(after(send, mixed_arrived))
    (mixed,) = call(
        "take", 2, take_kernel, (((home, width), BF16),), route_col[1], mixed_arrived
    )
    dresid, send, *ffn_zero = call(
        "home_back",
        10,
        home_backward_kernel,
        (
            ((home, width), F32, True),
            arrival_shape,
            ((width, FF), F32, True),
            ((FF, width), F32, True),
            ((8, width), F32, True),
        ),
        route_col[1],
        arrived,
        resid_zero,
        params[0],
        place_col[0],
        fresh=(1,),
        far_in=1,
        sems=((1,),),
        scratch=(
            ((home, FF), BF16),
            ((home, width), BF16),
            ((home, width), BF16),
            ((home, FF), BF16),
            ((home, width), BF16),
            recv_col_shape,
        ),
    )
    arrived = exchange(send)
    (packed,) = call(
        "pack",
        1,
        functools.partial(pack_kernel, share, quarter_rows),
        (((devices, early_rows, 128), BF16, True),),
        *grads_one,
        *ffn_zero,
        scratch=(((flat_rows, 128), F32), ((early_rows, 128), F32)),
    )
    early = exchange(after(packed, arrived))
    (send,) = call(
        "first_owner_back",
        16,
        functools.partial(owner_back_kernel, False, (share, quarter_rows)),
        (((devices, capacity + late_rows, width), BF16),),
        slot_col[0],
        heads,
        unfold,
        params[0],
        arrived,
        ffn_zero[0],
        recv_col[0],
        *stored_zero,
        fresh=(4,),
        scratch=(
            ((width, 3 * width), F32),
            ((width, width), F32),
            ((late_flat_rows, 128), F32),
            *back_scratch,
            slots_low,
            *kept_zero,
            recv_col_shape,
        ),
        far_in=3,
        sems=((2, len(LOAD_BOUNDS[0]) - 1), (1,)),
        vmem=40,
    )
    arrived = exchange(after(send, early))
    early = jnp.sum(early.astype(F32), axis=0)
    quarters = call(
        "late",
        1,
        functools.partial(late_kernel, quarter_rows),
        (((late_rows, 128), F32, True),) * 4,
        me.reshape(1),
        after(early, mixed),
        arrived,
        fresh=(2,),
        scratch=(((4, late_rows, 128), F32),),
        smem=1,
    )
    (tokens_grad,) = call(
        "finish",
        3,
        finish_kernel,
        (((home, width), F32),),
        route_col[0],
        arrived,
        dresid,
        fresh=(1,),
        scratch=(((arrivals, width), BF16),),
    )
    quarters = [quarters[0]] + [
        swapped(quarters[k], bits[:2], devices, k) for k in range(1, 4)
    ]
    square = after(paired([q[quarter_rows:] for q in quarters]), tokens_grad)
    for i in range(2, len(bits), 2):
        pair = bits[i : i + 2]
        square = paired(
            [square] + [swapped(square, pair, devices, k) for k in range(1, 2 ** len(pair))]
        )
    total = jnp.sqrt(square[0, 0])
    quarters = jnp.stack([q[:quarter_rows] for q in quarters])
    quarter = me // (devices // 4)
    for bit in (1, 2):
        other = quarters.reshape(4 // (2 * bit), 2, bit, quarter_rows, 128)[:, ::-1]
        quarters = jnp.where(quarter & bit, other.reshape(quarters.shape), quarters)
    shard = quarters.reshape(-1)[:share]
    clip_limit = 0.25 * math.sqrt(NPARAM)
    factor = jnp.minimum(1.0, clip_limit / (total + 1e-06))
    clipped = shard * factor
    new_first = beta_one * first_moment + (1.0 - beta_one) * clipped
    new_second = beta_two * second_moment + (1.0 - beta_two) * clipped * clipped
    first_hat = new_first / (1.0 - beta_one**adam_step)
    second_hat = new_second / (1.0 - beta_two**adam_step)
    new_master = master - rate * (first_hat / (jnp.sqrt(second_hat) + adam_eps) + decay * master)
    return (
        mixed,
        tokens_grad,
        total.reshape(1),
        clipped,
        new_master,
        new_first,
        new_second,
        new_master.astype(BF16),
    )


def solution(mesh):
    in_specs = (
        P(("grp", "win"), None),
        P(None, ("grp", "win"), None),
        P(("grp", "win"), None),
        P(None, ("grp", "win")),
        P(None, ("grp", "win"), None),
        P(None, ("grp", "win")),
        P(("grp", "win")),
        P(("grp", "win")),
        P(("grp", "win")),
    )
    out_specs = (
        P(("grp", "win"), None),
        P(("grp", "win"), None),
        P(),
        P(("grp", "win")),
        P(("grp", "win")),
        P(("grp", "win")),
        P(("grp", "win")),
        P(("grp", "win")),
    )
    return jax.shard_map(shards, mesh=mesh, in_specs=in_specs, out_specs=out_specs, check_vma=False)
```
